32 devices in a mesh: replica: 8 (over z, x), shard: 4 (over y, core).
Axes of the slice: x: 2, y: 2, z: 4, core: 2. Of those that a mesh axis runs over, the one named last changes fastest.
Arguments:
- tokens: bfloat16 [32768, 768], P(('replica', 'shard')), may hold values from -6 to 6
- segment_ids: int32 [32, 1024], P(('replica', 'shard')), may hold values from 0 to 4, as said below
- positions: int32 [32, 1024], P(('replica', 'shard')), may hold values from 0 to 799, as said below
- first_gain: bfloat16 [768], P('shard'), may hold values from 0.5 to 1.5
- first_shift: bfloat16 [768], P('shard'), may hold values from -1.25 to 1.25
- query_weight: bfloat16 [768, 768], P('shard'), may hold values from -0.21875 to 0.21875
- query_bias: bfloat16 [768], P('shard'), may hold values from -1.25 to 1.25
- shared_weight: bfloat16 [768, 128], P('shard'), may hold values from -0.21875 to 0.21875
- shared_bias: bfloat16 [128], P('shard'), may hold values from -1.25 to 1.25
- output_weight: bfloat16 [768, 768], P('shard'), may hold values from -1.5 to 1.5
- output_bias: bfloat16 [768], P('shard'), may hold values from -1.25 to 1.25
- second_gain: bfloat16 [768], P('shard'), may hold values from 0.5 to 1.5
- second_shift: bfloat16 [768], P('shard'), may hold values from -1.25 to 1.25
- up_weight: bfloat16 [768, 3072], P('shard'), may hold values from -0.21875 to 0.21875
- up_bias: bfloat16 [3072], P('shard'), may hold values from -1.25 to 1.25
- down_weight: bfloat16 [3072, 768], P('shard'), may hold values from -0.109375 to 0.109375
- down_bias: bfloat16 [768], P('shard'), may hold values from -1.25 to 1.25
- result_grad: bfloat16 [32768, 768], P(('replica', 'shard')), may hold values from -6 to 6
- shared_grad: bfloat16 [32768, 128], P(('replica', 'shard')), may hold values from -6 to 6
Outputs:
- block_output: bfloat16 [32768, 768], P(('replica', 'shard'))
- shared_cache: bfloat16 [32768, 128], P(('replica', 'shard'))
- tokens_grad: bfloat16 [32768, 768], P(('replica', 'shard'))
- grad_first_gain: float32 [768], P('shard')
- grad_first_shift: float32 [768], P('shard')
- grad_query_weight: float32 [768, 768], P('shard')
- grad_query_bias: float32 [768], P('shard')
- grad_shared_weight: float32 [768, 128], P('shard')
- grad_shared_bias: float32 [128], P('shard')
- grad_output_weight: float32 [768, 768], P('shard')
- grad_output_bias: float32 [768], P('shard')
- grad_second_gain: float32 [768], P('shard')
- grad_second_shift: float32 [768], P('shard')
- grad_up_weight: float32 [768, 3072], P('shard')
- grad_up_bias: float32 [3072], P('shard')
- grad_down_weight: float32 [3072, 768], P('shard')
- grad_down_bias: float32 [768], P('shard')
The draws below stay inside these ranges and needn't reach their ends.
Inputs may be any that keep to these rules, and one draw needn't show every extreme that they name: `segment_ids`: ids start at 0 and rise by one at each new document of a sequence; the first document of every sequence has 800 tokens and every other document except the last has 60 to 800; in the first sequence every document after the first except the last has exactly 60. `positions`: the place of a token counted from its document's first token.
All inputs are finite; a program needn't handle non-finite values.
Results may differ from the reference program's by a relative error of at most 0.011.
Values may be sent and summed in bfloat16 or wider, within the bound.
No kernel may reach another device: no remote copies, remote signals or barrier semaphores. Data moves between devices by JAX's collectives and lax.ppermute only.
A program may use at most 256 MiB of HBM per device.

```python
import jax
import jax.numpy as jnp
from jax import lax

D = 768
HEADS = 12
FF = 3072
HEAD_DIM = 64
ROT = 16
SEQ_LEN = 1024
DOC_MIN = 60
DOC_MAX = 800
SEQS = 32
TOKENS = 32768


def document_layout(key):
    base_key = jax.random.fold_in(key, 11)
    doc_slots = SEQ_LEN // DOC_MIN + 1
    doc_sizes = jax.random.randint(base_key, (SEQS, doc_slots), DOC_MIN, DOC_MAX + 1)
    slot_index = jnp.arange(doc_slots)[None, :]
    seq_index = jnp.arange(SEQS)[:, None]
    doc_sizes = jnp.where(seq_index == 0, DOC_MIN, doc_sizes)
    doc_sizes = jnp.where(slot_index == 0, DOC_MAX, doc_sizes).astype(jnp.int32)
    doc_ends = jnp.cumsum(doc_sizes, axis=1)
    token_index = jnp.arange(SEQ_LEN, dtype=jnp.int32)
    passed = doc_ends[:, None, :] <= token_index[None, :, None]
    seg_ids = jnp.sum(passed.astype(jnp.int32), axis=2).astype(jnp.int32)
    starts = jnp.sum(jnp.where(passed, doc_sizes[:, None, :], 0), axis=2).astype(jnp.int32)
    token_pos = (token_index[None, :] - starts).astype(jnp.int32)
    return (seg_ids, token_pos)


def draw_segment_ids(key, part):
    return document_layout(key)[0]


def draw_positions(key, part):
    return document_layout(key)[1]


def block_levels(rng, dims, split, smallest, top_value):
    level = 1.0
    for axis_at, parts in split:
        draws = jax.random.uniform(jax.random.fold_in(jax.random.fold_in(rng, 6), axis_at), (parts,), jnp.float32, smallest / len(split), top_value / len(split))
        level = level * jnp.repeat(jnp.exp(draws), dims[axis_at] // parts).reshape((-1,) + (1,) * (len(dims) - 1 - axis_at))
    return level


def normal_values(key, dims, width, bound, pieces=(), kind=jnp.bfloat16):
    values = width * jax.random.normal(key, dims, jnp.float32)
    if pieces:
        values = values * block_levels(key, dims, pieces, -0.22, 0.18)
    return jnp.clip(values, -bound, bound).astype(kind)


def setup_inputs(seed: int = 0) -> dict:
    arg_keys = jax.random.split(jax.random.key(seed), 20)
    return {
        "tokens": normal_values(arg_keys[0], (TOKENS, D), 1.0, 6.0, ((0, 32),)),
        "segment_ids": draw_segment_ids(jax.random.fold_in(arg_keys[19], 71), 0),
        "positions": draw_positions(jax.random.fold_in(arg_keys[19], 71), 0),
        "first_gain": jnp.clip(1.0 + 0.1 * jax.random.normal(arg_keys[3], (D,), jnp.float32), 0.5, 1.5).astype(jnp.bfloat16),
        "first_shift": normal_values(arg_keys[4], (D,), 0.2, 1.25, ((0, 4),)),
        "query_weight": normal_values(arg_keys[5], (D, D), D ** -0.5, 0.21875, ((0, 4),)),
        "query_bias": normal_values(arg_keys[6], (D,), 0.2, 1.25, ((0, 4),)),
        "shared_weight": normal_values(arg_keys[7], (D, 2 * HEAD_DIM), D ** -0.5, 0.21875, ((0, 4),)),
        "shared_bias": normal_values(arg_keys[8], (2 * HEAD_DIM,), 0.2, 1.25, ((0, 4),)),
        "output_weight": normal_values(arg_keys[9], (D, D), (D // 48) ** -0.5, 1.5, ((0, 4),)),
        "output_bias": normal_values(arg_keys[10], (D,), 0.2, 1.25, ((0, 4),)),
        "second_gain": jnp.clip(1.0 + 0.1 * jax.random.normal(arg_keys[11], (D,), jnp.float32), 0.5, 1.5).astype(jnp.bfloat16),
        "second_shift": normal_values(arg_keys[12], (D,), 0.2, 1.25, ((0, 4),)),
        "up_weight": normal_values(arg_keys[13], (D, FF), D ** -0.5, 0.21875, ((0, 4),)),
        "up_bias": normal_values(arg_keys[14], (FF,), 0.2, 1.25, ((0, 4),)),
        "down_weight": normal_values(arg_keys[15], (FF, D), FF ** -0.5, 0.109375, ((0, 4),)),
        "down_bias": normal_values(arg_keys[16], (D,), 0.2, 1.25, ((0, 4),)),
        "result_grad": normal_values(arg_keys[17], (TOKENS, D), 1.0, 6.0, ((0, 32),)),
        "shared_grad": normal_values(arg_keys[18], (TOKENS, 2 * HEAD_DIM), 1.0, 6.0, ((0, 32),)),
    }


@jax.custom_vjp
def low(v):
    return lax.optimization_barrier(v.astype(jnp.bfloat16)).astype(jnp.float32)

@jax.custom_vjp
def low_back(v):
    return v

def low_keep(v):
    return (low(v), None)

def low_pass(kept, grad):
    return (grad,)

def back_keep(v):
    return (v, None)

def back_low(kept, grad):
    return (low(grad),)
low.defvjp(low_keep, low_pass)
low_back.defvjp(back_keep, back_low)
epsilon = 1e-05
highest = lax.Precision.HIGHEST

def matmul_hi(left, right):
    return jnp.dot(left, right, precision=highest, preferred_element_type=jnp.float32)

def layer_norm(values, gain_vec, shift_vec):
    centre = values - lax.optimization_barrier(jnp.mean(values, axis=-1, keepdims=True))
    spread = lax.optimization_barrier(jnp.mean(centre * centre, axis=-1, keepdims=True))
    return centre * lax.rsqrt(spread + epsilon) * gain_vec + shift_vec

def rotary_tables(token_pos, rot_dims):
    half_dims = rot_dims // 2
    inv_freq = 10000.0 ** (-2.0 * jnp.arange(half_dims, dtype=jnp.float32) / rot_dims)
    angles = token_pos.astype(jnp.float32)[:, None] * inv_freq[None, :]
    return (jnp.cos(angles), jnp.sin(angles))

def rotate(values, rot_cos, rot_sin, rot_dims):
    half_dims = rot_dims // 2
    first_half = values[..., :half_dims]
    second_half = values[..., half_dims:rot_dims]
    cos_rows = rot_cos[:, None, :]
    sin_rows = rot_sin[:, None, :]
    return jnp.concatenate([first_half * cos_rows - second_half * sin_rows, second_half * cos_rows + first_half * sin_rows, values[..., rot_dims:]], axis=-1)

def layer_forward(param_list, inputs, seg_ids, token_pos):
    gain_a, shift_a, weight_q, bias_q, weight_s, bias_s, weight_o, bias_o, gain_m, shift_m, weight_up, bias_up, weight_down, bias_down = param_list
    length = inputs.shape[0]
    norm_a = low(layer_norm(inputs, gain_a, shift_a))
    rot_cos, rot_sin = rotary_tables(token_pos, ROT)
    query_lin = low_back(matmul_hi(norm_a, weight_q)) + bias_q
    queries = low(rotate(query_lin.reshape(length, HEADS, HEAD_DIM), rot_cos, rot_sin, ROT))
    shared_lin = low_back(matmul_hi(norm_a, weight_s)) + bias_s
    key_rot = rotate(shared_lin[:, None, :HEAD_DIM], rot_cos, rot_sin, ROT)[:, 0]
    shared = low(jnp.concatenate([key_rot, shared_lin[:, HEAD_DIM:]], axis=1))
    key_rows = shared[:, :HEAD_DIM]
    value_rows = shared[:, HEAD_DIM:]
    score_scale = HEAD_DIM ** (-0.5)
    raw_scores = jnp.einsum('qhd,kd->hqk', queries, key_rows, precision=highest) * score_scale
    key_index = jnp.arange(length)
    allowed = (seg_ids[:, None] == seg_ids[None, :]) & (key_index[None, :] <= key_index[:, None])
    logits = jnp.where(allowed[None], low_back(raw_scores), -1e+30)
    row_max = lax.optimization_barrier(jnp.max(logits, axis=-1, keepdims=True))
    exp_terms = jnp.exp(logits - row_max)
    probs = low(exp_terms / lax.optimization_barrier(jnp.sum(exp_terms, axis=-1, keepdims=True)))
    attended = jnp.einsum('hqk,kd->qhd', probs, value_rows, precision=highest).reshape(length, HEADS * HEAD_DIM)
    attended = low(low_back(attended))
    branch_a = matmul_hi(attended, weight_o) + bias_o
    norm_m = low(layer_norm(inputs, gain_m, shift_m))
    up_lin = low_back(matmul_hi(norm_m, weight_up)) + bias_up
    hidden = low(jax.nn.gelu(up_lin, approximate=False))
    branch_m = matmul_hi(hidden, weight_down) + bias_down
    return (inputs + branch_a + branch_m, shared)

def reference(tokens, segment_ids, positions, first_gain, first_shift, query_weight, query_bias, shared_weight, shared_bias, output_weight, output_bias, second_gain, second_shift, up_weight, up_bias, down_weight, down_bias, result_grad, shared_grad):
    param_list = tuple((value_in.astype(jnp.float32) for value_in in (first_gain, first_shift, query_weight, query_bias, shared_weight, shared_bias, output_weight, output_bias, second_gain, second_shift, up_weight, up_bias, down_weight, down_bias)))
    inputs = tokens.astype(jnp.float32).reshape(SEQS, SEQ_LEN, D)
    out_grads = result_grad.astype(jnp.float32).reshape(SEQS, SEQ_LEN, D)
    cache_grads = shared_grad.astype(jnp.float32).reshape(SEQS, SEQ_LEN, 2 * HEAD_DIM)
    zero_grads = tuple((jnp.zeros(value_in.shape, jnp.float32) for value_in in param_list))

    def scan_step(totals, seq_item):
        seq_in, seg_ids, token_pos, seq_grad, seq_cache_grad = seq_item
        outputs, pull_back = jax.vjp(lambda params_in, values_in: layer_forward(params_in, values_in, seg_ids, token_pos), param_list, seq_in)
        param_grads, input_grad = pull_back((seq_grad, seq_cache_grad))
        totals = tuple((acc + new for acc, new in zip(totals, param_grads)))
        return (totals, (outputs[0].astype(jnp.bfloat16), outputs[1].astype(jnp.bfloat16), input_grad.astype(jnp.bfloat16)))
    totals, stacked = lax.scan(scan_step, zero_grads, (inputs, segment_ids, positions, out_grads, cache_grads))
    return (stacked[0].reshape(TOKENS, D), stacked[1].reshape(TOKENS, 2 * HEAD_DIM), stacked[2].reshape(TOKENS, D), totals[0], totals[1], totals[2], totals[3], totals[4], totals[5], totals[6], totals[7], totals[8], totals[9], totals[10], totals[11], totals[12], totals[13])
```

```python
import functools

import jax
import jax.numpy as jnp
from jax import lax
from jax.experimental import pallas as pl
from jax.experimental.pallas import tpu as pltpu
from jax.sharding import PartitionSpec as P

HEAD_DIM = 64
ROT = 16
FIRST_DOC = 800
EPS = 1e-05
F32 = jnp.float32
BF16 = jnp.bfloat16
WAVES = 3


def dnn(a, b):
    return lax.dot_general(a, b, (((1,), (0,)), ((), ())), preferred_element_type=F32)


def dnt(a, b):
    return lax.dot_general(a, b, (((1,), (1,)), ((), ())), preferred_element_type=F32)


def dtn(a, b):
    return lax.dot_general(a, b, (((0,), (0,)), ((), ())), preferred_element_type=F32)


def sum8(v):
    return jnp.sum(v.reshape(-1, 8, v.shape[1]), axis=0)


def normalize(x):
    centre = x - jnp.mean(x, axis=-1, keepdims=True)
    var = jnp.mean(centre * centre, axis=-1, keepdims=True)
    rstd = lax.rsqrt(var + EPS)
    return centre * rstd, rstd


ANY = pl.BlockSpec(memory_space=pl.ANY)
SMEM = pl.BlockSpec(memory_space=pltpu.SMEM)
VM = pl.BlockSpec(memory_space=pltpu.VMEM)


def shape(dims, kind):
    return jax.ShapeDtypeStruct(dims, kind)


def pack_up(sc, up_weight, waves):
    rows, ff = up_weight.shape
    chunk = ff // 4
    wid = chunk // WAVES

    def kern(sc_ref, w_ref, *outs):
        s = sc_ref[0]
        for n, w in enumerate(waves):
            for k in range(4):
                t = jnp.bitwise_xor(s, k)
                a = pl.multiple_of(t * chunk + w * wid, 256)
                b = pl.multiple_of(jnp.bitwise_xor(t, 2) * chunk + w * wid, 256)
                out = outs[n * 4 + k]
                out[:, :wid] = w_ref[:, pl.ds(a, wid)]
                out[:, wid:] = w_ref[:, pl.ds(b, wid)]

    res = pl.pallas_call(
        kern,
        in_specs=[SMEM, VM],
        out_specs=[VM] * (4 * len(waves)),
        out_shape=[shape((rows, 2 * wid), BF16)] * (4 * len(waves)),
        cost_estimate=pl.CostEstimate(flops=0, bytes_accessed=6 * rows * ff, transcendentals=0),
        name="pack_up",
    )(sc, up_weight)
    return [res[n * 4 : n * 4 + 4] for n in range(len(waves))]


def pack_attn(sc, query_weight, shared_weight):
    rows, cols = query_weight.shape
    half = cols // 2
    sw = shared_weight.shape[1]

    def kern(sc_ref, q_ref, s_ref, o0, o1):
        c = jnp.bitwise_and(sc_ref[0], 1)
        for k, out in enumerate((o0, o1)):
            a = pl.multiple_of(jnp.bitwise_xor(c, k) * half, 128)
            out[:, :half] = q_ref[:, pl.ds(a, half)]
            out[:, half:] = s_ref[...]

    return pl.pallas_call(
        kern,
        in_specs=[SMEM, VM, VM],
        out_specs=[VM, VM],
        out_shape=[shape((rows, half + sw), BF16)] * 2,
        cost_estimate=pl.CostEstimate(flops=0, bytes_accessed=6 * rows * cols, transcendentals=0),
        name="pack_attn",
    )(sc, query_weight, shared_weight)


def norm_pair(which, tok, dy, vec, prev):
    n_tok, width = tok.shape
    blk = n_tok // 2
    base = 2 * which

    def kern(tok_ref, dy_ref, vec_ref, *refs):
        nm, nmt, na, nat, dyc, dyt, ob = refs[len(prev) :]
        xhat, _ = normalize(tok_ref[...].astype(F32))
        a = (xhat * vec_ref[0:1, :] + vec_ref[1:2, :]).astype(BF16)
        m = (xhat * vec_ref[2:3, :] + vec_ref[3:4, :]).astype(BF16)
        g = dy_ref[...]
        na[...] = a
        nm[...] = m
        dyc[...] = g
        nat[...] = a.T
        nmt[...] = m.T
        dyt[...] = g.T

        @pl.when(pl.program_id(0) == 0)
        def _():
            ob[...] = jnp.zeros_like(ob)

        ob[...] += sum8(g.astype(F32))

    row = pl.BlockSpec((blk, width), lambda i: (i + base, 0))
    col = pl.BlockSpec((width, blk), lambda i: (0, i + base))
    src = pl.BlockSpec((blk, width), lambda i: (i, 0))
    whole = pl.BlockSpec((8, width), lambda i: (0, 0))
    res = pl.pallas_call(
        kern,
        grid=(2,),
        in_specs=[src, src, whole] + [ANY] * len(prev),
        out_specs=[row, col, row, col, row, col, whole],
        out_shape=[shape((2 * n_tok, width), BF16), shape((width, 2 * n_tok), BF16)] * 3
        + [shape((8, width), F32)],
        input_output_aliases={3 + i: i for i in range(len(prev))},
        cost_estimate=pl.CostEstimate(
            flops=20 * n_tok * width, bytes_accessed=16 * n_tok * width, transcendentals=0
        ),
        name="norm_pair",
    )(tok, dy, vec, *prev)
    return res[:6], res[6]


def mlp_wave(wave, sc, nm, nmt, dy, dyt, up_pieces, down_own, down_recv, bias, acc):
    n_tok, width = nm.shape
    blk = n_tok // 4
    rows, wid2 = up_pieces[0].shape
    wid = wid2 // 2
    half = width // 2
    first = acc is None

    def kern(sc_ref, nm_r, nmt_r, dy_r, dyt_r, p0, p1, p2, p3, d0, d1, b_r, *refs):
        if first:
            br_i = gn_i = None
        else:
            br_i, gn_i = refs[:2]
            refs = refs[2:]
        br, gn, keep, send, ub, w_s, wd_s, acc_u, acc_d = refs
        i = pl.program_id(0)
        s = sc_ref[0]
        y = jnp.right_shift(s, 1)

        @pl.when(i == 0)
        def _():
            acc_u[...] = jnp.zeros_like(acc_u)
            acc_d[...] = jnp.zeros_like(acc_d)
            ub[...] = jnp.zeros_like(ub)
            for k, piece in enumerate((p0, p1, p2, p3)):
                at = pl.multiple_of(jnp.bitwise_xor(s, k) * rows, 16)
                w_s[pl.ds(at, rows), :] = piece[...]
            wd_s[:wid, :] = d0[...]
            wd_s[wid:, :] = d1[...]

        up = dnn(nm_r[...], w_s[...]) + b_r[0:1, :]
        cdf = 0.5 * (1.0 + lax.erf(up * 0.7071067811865476))
        hid = (up * cdf).astype(BF16)
        slope = cdf + up * (jnp.exp(-0.5 * up * up) * 0.3989422804014327)
        gu = dnt(dy_r[...], wd_s[...]) * slope
        gl = gu.astype(BF16)
        if first:
            br[...] = dnn(hid, wd_s[...])
            gn[...] = dnt(gl, w_s[...])
        else:
            br[...] = br_i[...] + dnn(hid, wd_s[...])
            gn[...] = gn_i[...] + dnt(gl, w_s[...])
        acc_u[...] += dnn(nmt_r[...], gl)
        acc_d[...] += dnn(dyt_r[...], hid)
        ub[...] += sum8(gu)

        @pl.when(i == pl.num_programs(0) - 1)
        def _():
            mine = pl.multiple_of(y * half, 16)
            other = pl.multiple_of((1 - y) * half, 16)
            keep[:half, :] = acc_u[pl.ds(mine, half), :].astype(BF16)
            send[:half, :wid] = acc_u[pl.ds(other, half), wid:].astype(BF16)
            send[:half, wid:] = acc_u[pl.ds(other, half), :wid].astype(BF16)
            keep[half:, :wid] = acc_d[:half, :wid].astype(BF16)
            keep[half:, wid:] = acc_d[half:, :wid].astype(BF16)
            send[half:, :wid] = acc_d[:half, wid:].astype(BF16)
            send[half:, wid:] = acc_d[half:, wid:].astype(BF16)

    row = pl.BlockSpec((blk, width), lambda i: (i, 0))
    col = pl.BlockSpec((width, blk), lambda i: (0, i))

    def fixed(dims, at=(0, 0)):
        return pl.BlockSpec(dims, lambda i: at)

    extra = [] if first else list(acc)
    return pl.pallas_call(
        kern,
        grid=(4,),
        in_specs=[SMEM, row, col, row, col]
        + [fixed((rows, wid2))] * 4
        + [fixed((wid, width), (wave, 0)), fixed((wid, width)), fixed((8, wid2))]
        + [row] * len(extra),
        out_specs=[row, row, fixed((width, wid2)), fixed((width, wid2)), fixed((8, wid2))],
        out_shape=[shape((n_tok, width), F32)] * 2
        + [shape((width, wid2), BF16)] * 2
        + [shape((8, wid2), F32)],
        scratch_shapes=[
            pltpu.VMEM((width, wid2), BF16),
            pltpu.VMEM((wid2, width), BF16),
            pltpu.VMEM((width, wid2), F32),
            pltpu.VMEM((width, wid2), F32),
        ],
        input_output_aliases={} if first else {12: 0, 13: 1},
        cost_estimate=pl.CostEstimate(
            flops=12 * n_tok * width * wid2,
            bytes_accessed=16 * n_tok * width,
            transcendentals=2 * n_tok * wid2,
        ),
        name="mlp_wave",
    )(sc, nm, nmt, dy, dyt, *up_pieces, down_own, down_recv, bias, *extra)


def attention(which, sc, arrs, acc, own):
    (na, nat, dy, dyt, tok, br, gn, qs_pieces, o_pieces, vec, qs_bias, tables, seg_row, seg_col, cgrad) = arrs
    length, width = tok.shape
    rows, wq = qs_pieces[0].shape
    wh = wq - 2 * HEAD_DIM
    o_rows = o_pieces[0].shape[0]
    pairs = wh // 128
    chunk = 256
    n_chunk = length // chunk
    first = acc is None
    tail = length - FIRST_DOC
    half = width // 2
    blocks = []
    at = 0
    while at + chunk <= FIRST_DOC - FIRST_DOC % chunk - chunk:
        blocks.append((at, chunk, 0, at + chunk, False))
        at += chunk
    blocks.append((at, FIRST_DOC - at, 0, FIRST_DOC, False))
    blocks.append((FIRST_DOC, tail, FIRST_DOC, tail, True))

    def kern(sc_ref, na_r, dy_r, q0, q1, q2, q3, o0, o1, vec_r, qb_r, tc_r, ta_r, tb_r, sr_r, scol_r, cg_r,
             nat_h, dyt_h, tok_h, br_h, gn_h, *refs):
        if first:
            aqs_h = ao_h = asm_h = None
        else:
            aqs_h, ao_h, asm_h = refs[:3]
            refs = refs[3:]
        outp, hp, cache = refs[:3]
        refs = refs[3:]
        if first:
            gqs_o, go_o, sm_o = refs[:3]
            refs = refs[3:]
        else:
            keep_o, send_o, o_first, o_second, sm_o = refs[:5]
            refs = refs[5:]
        (wqs, wo, q_s, do_s, o_s, gqs_s, dq_s, kz, zk, vz, zv, ek, ok, ev, ov,
         nat_v, dyt_v, tok_v, br_v, gn_v, aqs_v, ao_v, sems) = refs
        s = sc_ref[0]
        y = jnp.right_shift(s, 1)

        copies = [
            pltpu.make_async_copy(br_h.at[pl.ds(which * length, length), :], br_v, sems.at[0]),
            pltpu.make_async_copy(gn_h.at[pl.ds(which * length, length), :], gn_v, sems.at[1]),
            pltpu.make_async_copy(tok_h, tok_v, sems.at[2]),
            pltpu.make_async_copy(nat_h.at[:, pl.ds(which * length, length)], nat_v, sems.at[3]),
            pltpu.make_async_copy(dyt_h.at[:, pl.ds(which * length, length)], dyt_v, sems.at[4]),
        ]
        if not first:
            copies.append(pltpu.make_async_copy(aqs_h, aqs_v, sems.at[5]))
            copies.append(pltpu.make_async_copy(ao_h, ao_v, sems.at[6]))
        for c in copies:
            c.start()

        for k, piece in enumerate((q0, q1, q2, q3)):
            at = pl.multiple_of(jnp.bitwise_xor(s, k) * rows, 16)
            wqs[pl.ds(at, rows), :] = piece[...]
        wo[pl.ds(pl.multiple_of(y * o_rows, 16), o_rows), :] = o0[...]
        wo[pl.ds(pl.multiple_of((1 - y) * o_rows, 16), o_rows), :] = o1[...]
        ek[...] = jnp.zeros_like(ek)
        ok[...] = jnp.zeros_like(ok)
        ev[...] = jnp.zeros_like(ev)
        ov[...] = jnp.zeros_like(ov)

        lane = lax.broadcasted_iota(jnp.int32, (1, 128), 1)
        low = lane < HEAD_DIM

        def turn(v, c, a, b, sign):
            return v * c + sign * (pltpu.roll(v, 120, 1) * a + pltpu.roll(v, 8, 1) * b)

        def tabs(at, keys):
            c = tc_r[pl.ds(at, chunk), :]
            a = ta_r[pl.ds(at, chunk), :]
            b = tb_r[pl.ds(at, chunk), :]
            if keys:
                c = jnp.where(low, c, 1.0)
                a = jnp.where(low, a, 0.0)
                b = jnp.where(low, b, 0.0)
            return c, a, b

        @pl.loop(0, n_chunk)
        def _(n):
            at = pl.multiple_of(n * chunk, chunk)
            sl = pl.ds(at, chunk)
            lin = dnn(na_r[sl, :], wqs[...]) + qb_r[0:1, :]
            tq = tabs(at, False)
            for p in range(pairs):
                v = turn(lin[:, p * 128 : (p + 1) * 128], *tq, 1.0)
                q_s[sl, p * 128 : (p + 1) * 128] = v.astype(BF16) * BF16(0.125)
            v = turn(lin[:, wh:], *tabs(at, True), 1.0)
            kv = v.astype(BF16)
            cache[sl, :] = kv
            vr = pltpu.roll(v, 64, 1)
            zero = jnp.zeros_like(v)
            kz[sl, :] = jnp.where(low, v, zero).astype(BF16)
            zv[sl, :] = jnp.where(low, zero, v).astype(BF16)
            zk[sl, :] = jnp.where(low, zero, vr).astype(BF16)
            vz[sl, :] = jnp.where(low, vr, zero).astype(BF16)
            do_s[sl, :] = dnt(dy_r[sl, :], wo[...]).astype(BF16)

        @pl.loop(0, pairs)
        def _(p):
            cols = pl.ds(pl.multiple_of(p * 128, 128), 128)
            for r0, rn, k0, kn, segs in blocks:
                q2 = q_s[r0 : r0 + rn, cols]
                do2 = do_s[r0 : r0 + rn, cols]
                qi = lax.broadcasted_iota(jnp.int32, (rn, kn), 0) + r0
                ki = lax.broadcasted_iota(jnp.int32, (rn, kn), 1) + k0
                allowed = ki <= qi
                if segs:
                    allowed = allowed & (scol_r[...] == sr_r[0:1, :])
                o2 = dq2 = None
                for ks, vs, ak, av in ((kz, vz, ek, ev), (zk, zv, ok, ov)):
                    kk = ks[k0 : k0 + kn, :]
                    vv = vs[k0 : k0 + kn, :]
                    logit = jnp.where(allowed, dnt(q2, kk), -1e30)
                    top = jnp.max(logit, axis=-1, keepdims=True)
                    ex = jnp.exp(logit - top)
                    prob = ex * (1.0 / jnp.sum(ex, axis=-1, keepdims=True))
                    pb = prob.astype(BF16)
                    dp = dnt(do2, vv)
                    mean = jnp.sum(prob * dp, axis=-1, keepdims=True)
                    ds = (prob * (dp - mean)).astype(BF16)
                    o_t = dnn(pb, vv)
                    dq_t = dnn(ds, kk)
                    o2 = o_t if o2 is None else o2 + o_t
                    dq2 = dq_t if dq2 is None else dq2 + dq_t
                    ak[k0 : k0 + kn, :] += dtn(ds, q2)
                    av[k0 : k0 + kn, :] += dtn(pb, do2)
                o_s[r0 : r0 + rn, cols] = o2.astype(BF16)
                dq_s[r0 : r0 + rn, cols] = dq2

        for c in copies[:3]:
            c.wait()

        zrow = jnp.zeros((8, width), F32)
        if first:
            sm_o[...] = jnp.zeros_like(sm_o)
        else:
            sm_o[...] = asm_h[...]

        @pl.loop(0, n_chunk)
        def _(n):
            at = pl.multiple_of(n * chunk, chunk)
            sl = pl.ds(at, chunk)
            tq = tabs(at, False)
            for p in range(pairs):
                cc = slice(p * 128, (p + 1) * 128)
                v = turn(dq_s[sl, cc] * 0.125, *tq, -1.0)
                sm_o[32:40, cc] += sum8(v)
                gqs_s[sl, cc] = v.astype(BF16)
            gk = ek[sl, :] + pltpu.roll(ok[sl, :], 64, 1)
            gv = pltpu.roll(ev[sl, :], 64, 1) + ov[sl, :]
            v = jnp.where(low, gk, gv)
            if own:
                v = v + cg_r[sl, :].astype(F32)
            v = turn(v, *tabs(at, True), -1.0)
            sm_o[32:40, wh:wq] += sum8(v)
            gqs_s[sl, wh:] = v.astype(BF16)
            outp[sl, :] = (br_v[sl, :] + dnn(o_s[sl, :], wo[...])).astype(BF16)
            ea = dnt(gqs_s[sl, :], wqs[...])
            em = gn_v[sl, :]
            xhat, _r = normalize(tok_v[sl, :].astype(F32))
            hp[sl, :] = (ea * vec_r[0:1, :] + em * vec_r[2:3, :]).astype(BF16)
            sm_o[0:8, :] += sum8(ea * xhat)
            sm_o[8:16, :] += sum8(ea)
            sm_o[16:24, :] += sum8(em * xhat)
            sm_o[24:32, :] += sum8(em)

        for c in copies[3:]:
            c.wait()

        if first:
            gqs_o[...] = dnn(nat_v[...], gqs_s[...])
            go_o[...] = dnn(dyt_v[...], o_s[...])
        else:
            aqs_v[...] += dnn(nat_v[...], gqs_s[...])
            mine = pl.multiple_of(y * half, 16)
            other = pl.multiple_of((1 - y) * half, 16)
            keep_o[...] = aqs_v[pl.ds(mine, half), :].astype(BF16)
            send_o[...] = aqs_v[pl.ds(other, half), :].astype(BF16)
            ao_v[...] += dnn(dyt_v[...], o_s[...])
            got = ao_v[...].T
            low_half = got[:o_rows, :].astype(BF16)
            high_half = got[o_rows:, :].astype(BF16)
            o_first[...] = jnp.where(y == 0, low_half, high_half)
            o_second[...] = jnp.where(y == 0, high_half, low_half)

    def fixed(dims, at=(0, 0)):
        return pl.BlockSpec(dims, lambda i: at, pipeline_mode=pl.Buffered(1))

    extra = [] if first else list(acc)
    ospec = [fixed((length, width)), fixed((length, width)), fixed((length, 128))]
    oshape = [shape((length, width), BF16)] * 2 + [shape((length, 128), BF16)]
    if first:
        ospec += [fixed((width, wq)), fixed((width, wh)), fixed((40, width))]
        oshape += [shape((width, wq), F32), shape((width, wh), F32), shape((40, width), F32)]
    else:
        ospec += [fixed((half, wq))] * 2 + [fixed((o_rows, width))] * 2 + [fixed((40, width))]
        oshape += [shape((half, wq), BF16)] * 2 + [shape((o_rows, width), BF16)] * 2 + [shape((40, width), F32)]
    tab = fixed((length, 128))
    return pl.pallas_call(
        kern,
        grid=(1,),
        in_specs=[SMEM, fixed((length, width), (which, 0)), fixed((length, width), (which, 0))]
        + [fixed((rows, wq))] * 4
        + [fixed((o_rows, width))] * 2
        + [fixed((8, width)), fixed((8, wq)), tab, tab, tab, fixed((1, tail)), fixed((tail, 1)), tab]
        + [ANY] * 5
        + ([] if first else [ANY, ANY, fixed((40, width))]),
        out_specs=ospec,
        out_shape=oshape,
        scratch_shapes=[
            pltpu.VMEM((width, wq), BF16),
            pltpu.VMEM((wh, width), BF16),
            pltpu.VMEM((length, wh), BF16),
            pltpu.VMEM((length, wh), BF16),
            pltpu.VMEM((length, wh), BF16),
            pltpu.VMEM((length, wq), BF16),
            pltpu.VMEM((length, wh), F32),
        ]
        + [pltpu.VMEM((length, 128), BF16)] * 4
        + [pltpu.VMEM((length, 128), F32)] * 4
        + [
            pltpu.VMEM((width, length), BF16),
            pltpu.VMEM((width, length), BF16),
            pltpu.VMEM((length, width), BF16),
            pltpu.VMEM((length, width), F32),
            pltpu.VMEM((length, width), F32),
            pltpu.VMEM((8, 128) if first else (width, wq), F32),
            pltpu.VMEM((8, 128) if first else (width, wh), F32),
            pltpu.SemaphoreType.DMA((7,)),
        ],
        cost_estimate=pl.CostEstimate(
            flops=2 * length * width * (3 * wq + 3 * wh) + 12 * length * length * wh,
            bytes_accessed=30 * length * width,
            transcendentals=length * length * wh // 128,
        ),
        name="attention",
    )(sc, na, dy, *qs_pieces, *o_pieces, vec, qs_bias, *tables, seg_row, seg_col, cgrad,
      nat, dyt, tok, br, gn, *extra)


def finish(tok, dy, out_own, out_in, h_own, h_in, vec):
    n_tok, width = tok.shape
    blk = n_tok // 4

    def kern(tok_r, dy_r, oo, oi, ho, hi, vec_r, out, tg):
        x = tok_r[...].astype(F32)
        xhat, rstd = normalize(x)
        out[...] = (x + oo[...].astype(F32) + oi[...].astype(F32) + vec_r[4:5, :] + vec_r[5:6, :]).astype(BF16)
        h = ho[...].astype(F32) + hi[...].astype(F32)
        mean = jnp.mean(h, axis=-1, keepdims=True)
        cov = jnp.mean(h * xhat, axis=-1, keepdims=True)
        tg[...] = (dy_r[...].astype(F32) + rstd * (h - mean - xhat * cov)).astype(BF16)

    row = pl.BlockSpec((blk, width), lambda i: (i, 0))
    return pl.pallas_call(
        kern,
        grid=(4,),
        in_specs=[row] * 6 + [pl.BlockSpec((8, width), lambda i: (0, 0))],
        out_specs=[row, row],
        out_shape=[shape((n_tok, width), BF16)] * 2,
        cost_estimate=pl.CostEstimate(
            flops=20 * n_tok * width, bytes_accessed=16 * n_tok * width, transcendentals=0
        ),
        name="finish",
    )(tok, dy, out_own, out_in, h_own, h_in, vec)


def mlp_grads(sc, offs, waves, width, ff):
    n_p = len(waves[0])
    _, prow, wid2 = waves[0][0].shape
    wid = wid2 // 2
    chunk = ff // 4
    shard_rows = width // 4

    def kern(sc_ref, off_ref, *refs):
        up, down, tmp = refs[-3:]
        s = sc_ref[0]
        for w in range(WAVES):
            for n in range(n_p):
                ref = refs[w * n_p + n]
                at = pl.multiple_of(off_ref[n], 8)
                for k in range(4):
                    t = jnp.bitwise_xor(s, k)
                    lanes = pl.multiple_of(t * chunk + w * wid, 256)
                    h = (k >> 1) * wid
                    up[pl.ds(at, prow), pl.ds(lanes, wid)] = ref[k & 1, :, h : h + wid].astype(F32)
                for j in range(4):
                    h = (j >> 1) * wid
                    tmp[pl.ds(j * shard_rows + at, prow), :] = ref[2 + (j & 1), :, h : h + wid].astype(F32)
            down[w * wid : (w + 1) * wid, :] = tmp[...].T

    flat = [p for wv in waves for p in wv]
    return pl.pallas_call(
        kern,
        in_specs=[SMEM, SMEM] + [VM] * len(flat),
        out_specs=[VM, VM],
        out_shape=[shape((shard_rows, ff), F32), shape((chunk, width), F32)],
        scratch_shapes=[pltpu.VMEM((width, wid), F32)],
        cost_estimate=pl.CostEstimate(flops=0, bytes_accessed=12 * shard_rows * ff, transcendentals=0),
        name="mlp_grads",
    )(sc, offs, *flat)


def attn_grads(sc, offs, qs, og, width):
    n_p = len(qs)
    _, prow, wq = qs[0].shape
    shard_rows = width // 4
    wh = width // 2

    def kern(sc_ref, off_ref, *refs):
        gq, gs, go = refs[-3:]
        c = jnp.bitwise_and(sc_ref[0], 1)
        for n in range(n_p):
            at = pl.multiple_of(off_ref[n], 8)
            ref = refs[n]
            for k in range(2):
                lanes = pl.multiple_of(jnp.bitwise_xor(c, k) * wh, 128)
                gq[pl.ds(at, prow), pl.ds(lanes, wh)] = ref[k, :, :wh].astype(F32)
            gs[pl.ds(at, prow), :] = ref[0, :, wh:].astype(F32)
            go[pl.ds(at, prow), :] = refs[n_p + n][0].astype(F32)

    return pl.pallas_call(
        kern,
        in_specs=[SMEM, SMEM] + [VM] * (2 * n_p),
        out_specs=[VM] * 3,
        out_shape=[shape((shard_rows, width), F32), shape((shard_rows, wq - wh), F32), shape((shard_rows, width), F32)],
        name="attn_grads",
    )(sc, offs, *qs, *og)


class Replicas:
    def __init__(self, count):
        self.count = count
        self.stages = []
        left, stride = count, 1
        size = 2
        while left > 1:
            size = min(size, left)
            self.stages.append((size, stride))
            stride *= size
            left //= size
            size = 4
        self.rank = lax.axis_index("replica")

    def digit(self, stage):
        size, stride = stage
        return (self.rank // stride) % size

    def move(self, value, stage, j):
        size, stride = stage
        pairs = []
        for r in range(self.count):
            q = (r // stride) % size
            pairs.append((r, r + ((q ^ j) - q) * stride))
        return lax.ppermute(value, "replica", pairs)

    def scatter(self, parts):
        for stage in self.stages:
            size = stage[0]
            q = self.digit(stage)
            rows = parts[0].shape[1] // size

            def piece(k):
                at = (q ^ k) * rows
                cuts = [lax.dynamic_slice_in_dim(p, at, rows, axis=1).astype(F32) for p in parts]
                return sum(cuts[1:], cuts[0]).astype(BF16)

            outs = [piece(k) for k in range(size)]
            parts = [outs[0]] + [self.move(outs[k], stage, k) for k in range(1, size)]
        return sum([p.astype(F32) for p in parts[1:]], parts[0].astype(F32))

    def gather(self, piece, total_rows):
        out = [(piece, jnp.int32(0))]
        rows = piece.shape[1]
        spans = []
        span = total_rows
        for stage in self.stages:
            span //= stage[0]
            spans.append(span)
        base = jnp.int32(0)
        found = [(piece, ())]
        for stage in reversed(self.stages):
            new = []
            for arr, rel in found:
                for j in range(stage[0]):
                    new.append((arr if j == 0 else self.move(arr, stage, j), (j,) + rel))
            found = new
        arrays, offs = [], []
        for arr, rel in found:
            off = jnp.int32(0)
            for stage, sp, j in zip(self.stages, spans, rel):
                off = off + (self.digit(stage) ^ j) * sp
            arrays.append(arr)
            offs.append(off)
        offs = jnp.stack(offs).astype(jnp.int32)
        if rows % 8:
            whole = jnp.zeros((piece.shape[0], total_rows, piece.shape[2]), piece.dtype)
            for n, arr in enumerate(arrays):
                whole = lax.dynamic_update_slice_in_dim(whole, arr, offs[n], axis=1)
            return [whole], jnp.zeros((1,), jnp.int32)
        return arrays, offs

    def total(self, value):
        for stage in self.stages:
            parts = [value] + [self.move(value, stage, j) for j in range(1, stage[0])]
            q = self.digit(stage)
            rank = [q ^ j for j in range(stage[0])]
            acc = None
            for m in range(stage[0]):
                term = parts[0]
                for j in range(1, stage[0]):
                    term = jnp.where(rank[j] == m, parts[j], term)
                acc = term if acc is None else acc + term
            value = acc
        return value


def to_shard(value, k):
    return lax.ppermute(value, "shard", [(s, s ^ k) for s in range(4)])


def swap_core_first(value, flip):
    pairs = []
    for s in range(4):
        y, c = s >> 1, s & 1
        pairs.append((s, ((c ^ flip) << 1) | y))
    return lax.ppermute(value, "shard", pairs)


def swap_core_back(value, flip):
    pairs = []
    for s in range(4):
        y, c = s >> 1, s & 1
        pairs.append((((c ^ flip) << 1) | y, s))
    return lax.ppermute(value, "shard", pairs)


def after(value, *others):
    return lax.optimization_barrier((value,) + others)[0]


def rotary(pos):
    lane = jnp.arange(128) % HEAD_DIM
    half = ROT // 2
    inv = 10000.0 ** (-2.0 * (lane % half).astype(F32) / ROT)
    ang = pos.astype(F32)[:, None] * inv[None, :]
    cos, sin = jnp.cos(ang), jnp.sin(ang)
    turned = lane < ROT
    tc = jnp.where(turned, cos, 1.0)
    ta = jnp.where(lane < half, -sin, 0.0)
    tb = jnp.where(turned & (lane >= half), sin, 0.0)
    return tc, ta, tb


def shards(
    tokens, segment_ids, positions, first_gain, first_shift, query_weight, query_bias, shared_weight,
    shared_bias, output_weight, output_bias, second_gain, second_shift, up_weight, up_bias, down_weight,
    down_bias, result_grad, shared_grad, *, replicas,
):
    width = tokens.shape[1]
    ff = up_weight.shape[1]
    part = width // 4
    chunk = ff // 4
    wid = chunk // WAVES
    rep = Replicas(replicas)
    s = lax.axis_index("shard")
    c = s & 1
    sc = jnp.stack([s]).astype(jnp.int32)

    small = jnp.concatenate(
        [first_gain, first_shift, second_gain, second_shift, output_bias, down_bias, query_bias, up_bias, shared_bias]
    )
    small = jnp.pad(small, (0, -small.shape[0] % 128)).reshape(1, -1)
    near = [small] + [to_shard(small, k) for k in (1, 2, 3)]
    tok_in = to_shard(tokens, 1)
    dy_in = to_shard(result_grad, 1)
    ints = jnp.concatenate([segment_ids, positions], axis=0)
    ints_in = to_shard(ints, 1)

    (up0,) = pack_up(sc, up_weight, (0,))
    up_in = [up0[0]] + [to_shard(up0[k], k) for k in (1, 2, 3)]
    down_in = [to_shard(down_weight[:wid], 2)]
    up12 = pack_up(sc, up_weight, (1, 2))
    qs_out = pack_attn(sc, query_weight, shared_weight)

    lo = jnp.where(c == 0, near[0], near[1]), jnp.where(c == 0, near[1], near[0])
    hi = jnp.where(c == 0, near[2], near[3]), jnp.where(c == 0, near[3], near[2])
    y0 = s < 2
    order = jnp.concatenate(
        [jnp.where(y0, lo[0], hi[0]), jnp.where(y0, lo[1], hi[1]), jnp.where(y0, hi[0], lo[0]), jnp.where(y0, hi[1], lo[1])]
    ).astype(F32)
    vec = order[:, : 7 * part].reshape(4, 7, part).transpose(1, 0, 2).reshape(7, width)
    vec = jnp.pad(vec, ((0, 1), (0, 0)))
    sb = order[:, 7 * part + chunk : 7 * part + chunk + 2 * HEAD_DIM // 4].reshape(1, 2 * HEAD_DIM)
    wh = width // 2
    qb = lax.dynamic_slice(vec, (6, c * wh), (1, wh))
    qs_bias = jnp.broadcast_to(jnp.concatenate([qb, sb], axis=1), (8, wh + 2 * HEAD_DIM))
    ub_own = near[0][0, 7 * part : 7 * part + chunk].astype(F32)
    ub_in = near[2][0, 7 * part : 7 * part + chunk].astype(F32)

    prev, ob = norm_pair(0, tokens, result_grad, vec, [])
    prev, _ = norm_pair(1, tok_in, dy_in, vec, prev)
    nm, nmt, na, nat, dy, dyt = prev

    tabs = [rotary(positions[0]), rotary(ints_in[1])]
    segs = [segment_ids[0], ints_in[0]]

    acc = None
    waves, ub_g = [], []
    ups = [up_in]
    o_in = qs_in = None
    for w in range(WAVES):
        gate = ups[w][1:] + [down_in[w]]
        if w + 1 < WAVES:
            mine = up12[w]
            src = [after(mine[k], *gate) for k in (1, 2, 3)]
            ups.append([mine[0]] + [to_shard(v, k) for k, v in zip((1, 2, 3), src)])
            down_in.append(to_shard(after(down_weight[(w + 1) * wid : (w + 2) * wid], *gate), 2))
        else:
            q_src = [after(qs_out[k & 1], *gate) for k in (1, 2, 3)]
            qs_in = [qs_out[0]] + [to_shard(v, k) for k, v in zip((1, 2, 3), q_src)]
            o_src = after(output_weight, *gate)
            o_in = [swap_core_first(o_src, 0), swap_core_first(o_src, 1)]
        bias = jnp.concatenate([ub_own[w * wid : (w + 1) * wid], ub_in[w * wid : (w + 1) * wid]])
        bias = jnp.broadcast_to(bias[None], (8, 2 * wid))
        br, gn, keep, send, ub = mlp_wave(
            w, sc, nm, nmt, dy, dyt, ups[w], down_weight, down_in[w], bias, acc
        )
        acc = (br, gn)
        ub_g.append(jnp.sum(ub, axis=0))
        recv = to_shard(send, 2)
        waves.append((keep.reshape(4, part, 2 * wid), recv.reshape(4, part, 2 * wid)))
    br, gn = acc

    pieces = []
    for keep, recv in waves:
        total = rep.scatter([keep, recv]).astype(BF16)
        mine = jnp.where(c == 0, total[0], total[1])
        theirs = jnp.where(c == 0, total[1], total[0])
        pieces.append(jnp.concatenate([mine[None], to_shard(theirs, 1)[None], total[2:]], axis=0))

    def attend(which, acc, tok, cg, own):
        seg = segs[which][FIRST_DOC:]
        return attention(
            which, sc,
            (na, nat, dy, dyt, tok, br, gn, qs_in, o_in, vec, qs_bias, tabs[which], seg[None, :], seg[:, None], cg),
            acc, own,
        )

    out_p, h_p, _, gqs, go, sm = attend(1, None, tok_in, shared_grad, False)
    out_in = to_shard(out_p, 1)
    h_in = to_shard(h_p, 1)
    out_o, h_o, cache, keep, send, o_first, o_second, sm = attend(0, (gqs, go, sm), tokens, shared_grad, True)

    got = []
    offs = None
    for p in pieces:
        arrs, offs = rep.gather(p, part)
        got.append(arrs)
    grad_up, grad_down = mlp_grads(sc, offs, got, width, ff)

    recv = to_shard(send, 2)
    o_terms = [swap_core_back(o_first, 0)[None], swap_core_back(o_second, 1)[None]]
    wq = keep.shape[1]
    qs_sum = rep.scatter([keep.reshape(2, part, wq), recv.reshape(2, part, wq)])
    o_sum = rep.scatter(o_terms).astype(BF16)
    mine = jnp.where(c == 0, qs_sum[0], qs_sum[1])
    theirs = jnp.where(c == 0, qs_sum[1], qs_sum[0]).astype(BF16)
    back = to_shard(theirs, 1)
    shared = mine[:, wh:].astype(BF16).astype(F32) + back[:, wh:].astype(F32)
    front = jnp.concatenate([mine[:, :wh], shared], axis=1).astype(BF16)
    qs_piece = jnp.stack([front, back])
    qs_all, offs = rep.gather(qs_piece, part)
    o_all, _ = rep.gather(o_sum, part)
    grad_q, grad_s, grad_o = attn_grads(sc, offs, qs_all, o_all, width)

    block_output, tokens_grad = finish(tokens, result_grad, out_o, out_in, h_o, h_in, vec)

    lines = jnp.sum(sm.reshape(5, 8, width), axis=1)
    qb_g = jnp.where(c == 0, jnp.pad(lines[4:5, :wh], ((0, 0), (0, wh))), jnp.pad(lines[4:5, :wh], ((0, 0), (wh, 0))))
    sb_g = lines[4, wh : wh + 2 * HEAD_DIM].reshape(4, -1)
    ob_g = jnp.sum(ob, axis=0, keepdims=True)
    seven = jnp.concatenate([lines[:4], ob_g, qb_g], axis=0)
    six = seven.reshape(6, 4, part).transpose(1, 0, 2).reshape(4, 6 * part)
    ub_a = jnp.concatenate([u[:wid] for u in ub_g])
    ub_b = jnp.concatenate([u[wid:] for u in ub_g])
    who = jnp.arange(4)[:, None]
    ub_t = jnp.where(who == s, ub_a[None], 0.0) + jnp.where(who == (s ^ 2), ub_b[None], 0.0)
    table = jnp.concatenate([six, ub_t, sb_g], axis=1)
    table = jnp.pad(table, ((0, 0), (0, -table.shape[1] % 128)))
    terms = [lax.dynamic_slice_in_dim(table, s ^ k, 1, axis=0) for k in range(4)]
    mine = terms[0] + sum(to_shard(terms[k], k) for k in (1, 2, 3))
    tot = rep.total(mine)[0]
    cut = lambda n: tot[n * part : (n + 1) * part]
    ub_out = tot[6 * part : 6 * part + chunk]
    sb_out = tot[6 * part + chunk : 6 * part + chunk + 2 * HEAD_DIM // 4]
    return (
        block_output, cache, tokens_grad,
        cut(0), cut(1), grad_q, cut(5), grad_s, sb_out, grad_o, cut(4),
        cut(2), cut(3), grad_up, ub_out, grad_down, cut(4),
    )


def solution(mesh):
    both = P(("replica", "shard"), None)
    one, two = P("shard"), P("shard", None)
    body = functools.partial(shards, replicas=mesh.shape["replica"])
    return jax.shard_map(
        body,
        mesh=mesh,
        in_specs=(both, both, both, one, one, two, one, two, one, two, one, one, one, two, one, two, one, both, both),
        out_specs=(both, both, both, one, one, two, one, two, one, two, one, one, one, two, one, two, one),
        check_vma=False,
    )
```

```python
import jax
import jax.numpy as jnp
from jax import lax
from jax.experimental import pallas as pl
from jax.experimental.pallas import tpu as pltpu
from jax.sharding import PartitionSpec as P


HEAD_DIM = 64
ROT = 16
FIRST_DOC = 800
EPS = 1e-05
F32 = jnp.float32
BF16 = jnp.bfloat16
WAVES = 3


def dnn(a, b):
    return lax.dot_general(a, b, (((1,), (0,)), ((), ())), preferred_element_type=F32)


def dnt(a, b):
    return lax.dot_general(a, b, (((1,), (1,)), ((), ())), preferred_element_type=F32)


def dtn(a, b):
    return lax.dot_general(a, b, (((0,), (0,)), ((), ())), preferred_element_type=F32)


def sum8(v):
    return jnp.sum(v.reshape(-1, 8, v.shape[1]), axis=0)


def normalize(x):
    centre = x - jnp.mean(x, axis=-1, keepdims=True)
    var = jnp.mean(centre * centre, axis=-1, keepdims=True)
    rstd = lax.rsqrt(var + EPS)
    return centre * rstd, rstd


ANY = pl.BlockSpec(memory_space=pl.ANY)
SMEM = pl.BlockSpec(memory_space=pltpu.SMEM)
VM = pl.BlockSpec(memory_space=pltpu.VMEM)


def shape(dims, kind):
    return jax.ShapeDtypeStruct(dims, kind)


def head_columns(w, c):
    width = w.shape[1]
    part = width // 4
    lane = lax.broadcasted_iota(jnp.int32, (1, width), 1)
    r = pltpu.roll(w, (width - c * part) % width, 1)
    return jnp.where(lane < part, r, pltpu.roll(r, width - part, 1))[:, : 2 * part]


def head_spread(x, c, width):
    part = width // 4
    lane = lax.broadcasted_iota(jnp.int32, (1, width), 1)
    v = jnp.concatenate([x, jnp.zeros_like(x)], axis=1)
    zero = jnp.zeros_like(v)
    u = jnp.where(lane < part, v, zero)
    u = u + pltpu.roll(jnp.where((lane >= part) & (lane < 2 * part), v, zero), part, 1)
    return pltpu.roll(u, c * part, 1)


def up_piece(w_ref, s, k, w, chunk):
    wid = chunk // WAVES
    t = jnp.bitwise_xor(s, k)
    a = pl.multiple_of(t * chunk + w * wid, 256)
    b = pl.multiple_of(jnp.bitwise_xor(t, 2) * chunk + w * wid, 256)
    return jnp.concatenate([w_ref[:, pl.ds(a, wid)], w_ref[:, pl.ds(b, wid)]], axis=1)


def fold(out, at, rows, v, lanes):
    h = rows // 2
    out[at : at + rows, :] = v[:, :lanes]
    out[at + rows : at + rows + h, : lanes // 2] = v[:h, lanes:]
    out[at + rows : at + rows + h, lanes // 2 :] = v[h:, lanes:]


def unfold(ref, at, rows, lanes):
    h = rows // 2
    top = ref[at : at + rows, :]
    low = ref[at + rows : at + rows + h, :]
    return jnp.concatenate(
        [top, jnp.concatenate([low[:, : lanes // 2], low[:, lanes // 2 :]], axis=0)], axis=1
    )


def pack_small(sc, seven, shared_bias, up_bias):
    part = seven[0].shape[0]
    width = up_bias.shape[0]
    few = shared_bias.shape[0]

    def kern(sc_ref, *refs):
        out, tmp = refs[-2:]
        s = sc_ref[0]
        tmp[...] = jnp.zeros_like(tmp)
        for i in range(7):
            tmp[i : i + 1, :part] = refs[i][...].astype(F32).reshape(1, part)
        tmp[:7, :] = pltpu.roll(tmp[0:8, :], s * part, 1)[:7]
        tmp[7:8, :few] = refs[7][...].astype(F32).reshape(1, few)
        tmp[7:8, :] = pltpu.roll(tmp[0:8, :], s * few, 1)[7:8]
        tmp[pl.ds(8 + s, 1), :] = refs[8][...].astype(F32).reshape(1, width)
        out[...] = tmp[...].astype(BF16)

    return pl.pallas_call(
        kern,
        in_specs=[SMEM] + [VM] * 9,
        out_specs=VM,
        out_shape=shape((16, width), BF16),
        scratch_shapes=[pltpu.VMEM((16, width), F32)],
        name="pack_small",
    )(sc, *seven, shared_bias, up_bias)


def pack_first(sc, up_weight, down_weight):
    rows, ff = up_weight.shape
    chunk, width = down_weight.shape
    wid = chunk // WAVES

    def kern(sc_ref, w_ref, d_ref, own, k1, k3, m2):
        s = sc_ref[0]
        own[...] = up_piece(w_ref, s, 0, 0, chunk)
        k1[...] = up_piece(w_ref, s, 1, 0, chunk)
        k3[...] = up_piece(w_ref, s, 3, 0, chunk)
        m2[:rows, :] = up_piece(w_ref, s, 2, 0, chunk)
        fold(m2, rows, wid, d_ref[...], 2 * wid)

    return pl.pallas_call(
        kern,
        grid=(1,),
        in_specs=[SMEM, pl.BlockSpec((rows, ff), lambda i: (0, 0)), pl.BlockSpec((wid, width), lambda i: (0, 0))],
        out_specs=[pl.BlockSpec((rows, 2 * wid), lambda i: (0, 0))] * 3
        + [pl.BlockSpec((rows + wid * 3 // 2, 2 * wid), lambda i: (0, 0))],
        out_shape=[shape((rows, 2 * wid), BF16)] * 3 + [shape((rows + wid * 3 // 2, 2 * wid), BF16)],
        name="pack_first",
    )(sc, up_weight, down_weight)


def pack_core(sc, up_weight, query_weight, shared_weight):
    rows, ff = up_weight.shape
    width = query_weight.shape[1]
    chunk = ff // 4
    wid = chunk // WAVES
    n = 2 * (WAVES - 1)
    half = width // 2

    def kern(sc_ref, w_ref, q_ref, s_ref, out):
        s = sc_ref[0]
        c = jnp.bitwise_and(s, 1)
        for w in range(1, WAVES):
            for i, k in enumerate((1, 3)):
                at = (2 * (w - 1) + i) * rows
                out[at : at + rows, :] = up_piece(w_ref, s, k, w, chunk)
        out[n * rows :, :half] = head_columns(q_ref[...].astype(F32), 1 - c).astype(BF16)
        out[n * rows :, half:] = s_ref[...]

    return pl.pallas_call(
        kern,
        in_specs=[SMEM, VM, VM, VM],
        out_specs=VM,
        out_shape=shape(((n + 1) * rows, 2 * wid), BF16),
        name="pack_core",
    )(sc, up_weight, query_weight, shared_weight)


def pack_rest(sc, up_weight, down_weight, query_weight, shared_weight, output_weight, got):
    rows, _ = up_weight.shape
    chunk, width = down_weight.shape
    wid = chunk // WAVES
    lanes = 2 * wid
    n = 2 * (WAVES - 1)
    half = width // 2

    def kern(sc_ref, w_ref, d_ref, q_ref, s_ref, o_ref, g_ref, own1, own2, ownq, y1, y2, ya):
        s = sc_ref[0]
        c = jnp.bitwise_and(s, 1)
        for w, own, out in ((1, own1, y1), (2, own2, y2)):
            own[...] = up_piece(w_ref, s, 0, w, chunk)
            out[:rows, :] = up_piece(w_ref, s, 2, w, chunk)
            at = (2 * (w - 1) + 1) * rows
            out[rows : 2 * rows, :] = g_ref[at : at + rows, :]
            fold(out, 2 * rows, wid, d_ref[w * wid : (w + 1) * wid, :], lanes)
        mine = head_columns(q_ref[...].astype(F32), c).astype(BF16)
        for out in (ownq, ya):
            out[:rows, :half] = mine
            out[:rows, half:] = s_ref[...]
        ya[rows : 2 * rows, :] = g_ref[n * rows :, :]
        fold(ya, 2 * rows, rows, o_ref[...], lanes)

    msg = 2 * rows + wid * 3 // 2
    msg_a = 2 * rows + rows * 3 // 2
    return pl.pallas_call(
        kern,
        in_specs=[SMEM] + [VM] * 6,
        out_specs=[VM] * 6,
        out_shape=[shape((rows, lanes), BF16)] * 3
        + [shape((msg, lanes), BF16)] * 2
        + [shape((msg_a, lanes), BF16)],
        name="pack_rest",
    )(sc, up_weight, down_weight, query_weight, shared_weight, output_weight, got)


def norm_pair(which, tok, dy, near, prev):
    n_tok, width = tok.shape
    n_near = len(near)
    blk = n_tok // 2
    base = 2 * which

    def kern(tok_ref, dy_ref, *refs):
        nm, nmt, na, nat, dyc, dyt, ob, vec_ref = refs[n_near + len(prev) :]
        vec_ref[...] = sum([r[...].astype(F32) for r in refs[1:n_near]], refs[0][...].astype(F32))
        xhat, _ = normalize(tok_ref[...].astype(F32))
        a = (xhat * vec_ref[0:1, :] + vec_ref[1:2, :]).astype(BF16)
        m = (xhat * vec_ref[2:3, :] + vec_ref[3:4, :]).astype(BF16)
        g = dy_ref[...]
        na[...] = a
        nm[...] = m
        dyc[...] = g
        nat[...] = a.T
        nmt[...] = m.T
        dyt[...] = g.T

        @pl.when(pl.program_id(0) == 0)
        def _():
            ob[...] = jnp.zeros_like(ob)

        ob[...] += sum8(g.astype(F32))

    row = pl.BlockSpec((blk, width), lambda i: (i + base, 0))
    col = pl.BlockSpec((width, blk), lambda i: (0, i + base))
    src = pl.BlockSpec((blk, width), lambda i: (i, 0))
    whole = pl.BlockSpec((8, width), lambda i: (0, 0))
    small = pl.BlockSpec((16, width), lambda i: (0, 0))
    res = pl.pallas_call(
        kern,
        grid=(2,),
        in_specs=[src, src] + [small] * n_near + [ANY] * len(prev),
        out_specs=[row, col, row, col, row, col, whole, small],
        out_shape=[shape((2 * n_tok, width), BF16), shape((width, 2 * n_tok), BF16)] * 3
        + [shape((8, width), F32), shape((16, width), F32)],
        input_output_aliases={2 + n_near + i: i for i in range(len(prev))},
        cost_estimate=pl.CostEstimate(
            flops=20 * n_tok * width, bytes_accessed=16 * n_tok * width, transcendentals=0
        ),
        name="norm_pair",
    )(tok, dy, *near, *prev)
    return res[:6], res[6], res[7]


def col_sums(v):
    part = v[:, :128]
    for i in range(128, v.shape[1], 128):
        part = part + v[:, i : i + 128]
    return sum8(part.T)


def mlp_wave(wave, sc, nm, nmt, dy, dyt, pieces, down_at, down_own, vec, split):
    n_tok, width = nm.shape
    blk = n_tok // 4
    rows = width // 4
    chunk = down_own.shape[0]
    wid = chunk // WAVES
    wid2 = 2 * wid
    half = width // 2
    srcs = []
    for arr, _ in list(pieces) + [down_at]:
        if not any(arr is t for t in srcs):
            srcs.append(arr)
    where = [next(i for i, t in enumerate(srcs) if t is arr) for arr, _ in list(pieces) + [down_at]]
    n_src = len(srcs)

    def kern(sc_ref, nm_r, nmt_r, dy_r, dyt_r, d0, vec_r, *refs):
        got, refs = refs[:n_src], refs[n_src:]
        hid_o, gl_o, w_s, wd_s, ub, rs = refs[:6]
        b_s, acc_u, acc_d = refs[-3:]
        grads = refs[6:-3]
        i = pl.program_id(0)
        s = sc_ref[0]
        y = jnp.right_shift(s, 1)

        @pl.when(i == 0)
        def _():
            acc_u[...] = jnp.zeros_like(acc_u)
            acc_d[...] = jnp.zeros_like(acc_d)
            ub[...] = jnp.zeros_like(ub)
            for k in range(4):
                at = pl.multiple_of(jnp.bitwise_xor(s, k) * rows, 16)
                r0 = pieces[k][1]
                w_s[pl.ds(at, rows), :] = got[where[k]][r0 : r0 + rows, :]
            wd_s[:wid, :] = d0[...]
            wd_s[wid:, :] = unfold(got[where[4]], down_at[1], wid, wid2)
            for h, t in enumerate((s, jnp.bitwise_xor(s, 2))):
                line = vec_r[pl.ds(8 + t, 1), :]
                b_s[:, h * wid : (h + 1) * wid] = jnp.broadcast_to(line[:, wave * wid : (wave + 1) * wid], (8, wid))

        up = dnn(nm_r[...], w_s[...]) + b_s[0:1, :]
        cdf = 0.5 * (1.0 + lax.erf(up * 0.7071067811865476))
        hid = (up * cdf).astype(BF16)
        slope = cdf + up * (jnp.exp(-0.5 * up * up) * 0.3989422804014327)
        gu = dnt(dy_r[...], wd_s[...]) * slope
        gl = gu.astype(BF16)
        hid_o[...] = hid
        gl_o[...] = gl
        acc_u[...] += dnn(nmt_r[...], gl)
        acc_d[...] += dnn(dyt_r[...], hid)
        ub[...] += sum8(gu)

        @pl.when(i == pl.num_programs(0) - 1)
        def _():
            mine = pl.multiple_of(y * half, 16)
            other = pl.multiple_of((1 - y) * half, 16)
            if split:
                keep_u, send_u, keep_d, send_d = grads
                d = 0
            else:
                keep_u = keep_d = grads[0]
                send_u = send_d = grads[1]
                d = half
            keep_u[:half, :] = acc_u[pl.ds(mine, half), :].astype(BF16)
            send_u[:half, :wid] = acc_u[pl.ds(other, half), wid:].astype(BF16)
            send_u[:half, wid:] = acc_u[pl.ds(other, half), :wid].astype(BF16)
            keep_d[d:, :wid] = acc_d[:half, :wid].astype(BF16)
            keep_d[d:, wid:] = acc_d[half:, :wid].astype(BF16)
            send_d[d:, :wid] = acc_d[:half, wid:].astype(BF16)
            send_d[d:, wid:] = acc_d[half:, wid:].astype(BF16)
            w = w_s[...].astype(F32)
            rs[0:8, :] = col_sums(w * acc_u[...])
            rs[8:16, :] = col_sums(w * jnp.sum(ub[...], axis=0, keepdims=True))

    row = pl.BlockSpec((blk, width), lambda i: (i, 0))
    col = pl.BlockSpec((width, blk), lambda i: (0, i))
    mid = pl.BlockSpec((blk, wid2), lambda i: (i, 0))

    def fixed(dims, at=(0, 0)):
        return pl.BlockSpec(dims, lambda i: at)

    grads = [(half, wid2)] * 4 if split else [(width, wid2)] * 2
    return pl.pallas_call(
        kern,
        grid=(4,),
        in_specs=[SMEM, row, col, row, col]
        + [fixed((wid, width), (wave, 0)), fixed((16, width))]
        + [fixed(t.shape) for t in srcs],
        out_specs=[mid, mid, fixed((width, wid2)), fixed((wid2, width)), fixed((8, wid2)), fixed((16, width))]
        + [fixed(g) for g in grads],
        out_shape=[shape((n_tok, wid2), BF16)] * 2
        + [shape((width, wid2), BF16), shape((wid2, width), BF16), shape((8, wid2), F32), shape((16, width), F32)]
        + [shape(g, BF16) for g in grads],
        scratch_shapes=[
            pltpu.VMEM((8, wid2), F32),
            pltpu.VMEM((width, wid2), F32),
            pltpu.VMEM((width, wid2), F32),
        ],
        cost_estimate=pl.CostEstimate(
            flops=8 * n_tok * width * wid2,
            bytes_accessed=10 * n_tok * width,
            transcendentals=2 * n_tok * wid2,
        ),
        name="mlp_wave",
    )(sc, nm, nmt, dy, dyt, down_own, vec, *srcs)


def attention(sc, na, dy, weights, vec, waves_of, seg_rows, cgrad):
    width = na.shape[1]
    length = cgrad.shape[0]
    rows, wq = weights[0].shape
    o_rows = weights[3].shape[0]
    core_rows = weights[1].shape[0]
    wh = wq - 2 * HEAD_DIM
    pairs = wh // 128
    chunk = 256
    n_chunk = length // chunk
    tail = length - FIRST_DOC
    blocks = []
    at = 0
    while at + chunk <= FIRST_DOC - FIRST_DOC % chunk - chunk:
        blocks.append((at, chunk, 0, at + chunk, False))
        at += chunk
    blocks.append((at, FIRST_DOC - at, 0, FIRST_DOC, False))
    blocks.append((FIRST_DOC, tail, FIRST_DOC, tail, True))

    def kern(sc_ref, na_r, dy_r, vec_r, cs_r, sr_r, cg_r, *refs):
        q0, cg_in, mg_in, o0 = refs[:4]
        o_s, gqs_s, cache, sums, wqs, wo = refs[4:10]
        q_s, do_s, dq_s, kz, zk, vz, zv, ek, ok, ev, ov, tc_r, ta_r, tb_r, sg_s = refs[10:]
        s = sc_ref[0]
        c = jnp.bitwise_and(s, 1)
        y = jnp.right_shift(s, 1)
        step = pl.program_id(0)

        @pl.when(step == 0)
        def _():
            for k in range(4):
                at = pl.multiple_of(jnp.bitwise_xor(s, k) * rows, 16)
                piece = (q0, cg_in, mg_in, mg_in)[k]
                r0 = (0, 0, 0, rows)[k]
                wqs[pl.ds(at, rows), :] = piece[r0 : r0 + rows, :]
            wo[pl.ds(pl.multiple_of(y * o_rows, 16), o_rows), :] = o0[...]
            wo[pl.ds(pl.multiple_of((1 - y) * o_rows, 16), o_rows), :] = unfold(mg_in, 2 * rows, o_rows, wq)
            sums[...] = jnp.zeros_like(sums)

        ek[...] = jnp.zeros_like(ek)
        ok[...] = jnp.zeros_like(ok)
        ev[...] = jnp.zeros_like(ev)
        ov[...] = jnp.zeros_like(ov)
        lane = lax.broadcasted_iota(jnp.int32, (1, 128), 1)
        low = lane < HEAD_DIM
        qb_line = jnp.broadcast_to(head_columns(vec_r[0:8, :], c)[6:7, :], (8, wh))
        sb_line = jnp.broadcast_to(vec_r[7:8, : 2 * HEAD_DIM], (8, 2 * HEAD_DIM))
        qb_all = jnp.concatenate([qb_line, sb_line], axis=1)[0:1, :]

        def spread(v, lo, hi):
            i = lax.broadcasted_iota(jnp.int32, (8, 128), 0)
            ln = lax.broadcasted_iota(jnp.int32, (8, 128), 1)
            ln = jnp.bitwise_and(ln, HEAD_DIM - 1)
            hit = (jnp.bitwise_and(ln, ROT // 2 - 1) == i) & (ln >= lo) & (ln < hi)
            return lax.dot_general(v, hit.astype(F32), (((0,), (0,)), ((), ())),
                                   precision=lax.Precision.HIGHEST, preferred_element_type=F32)

        still = jnp.bitwise_and(lax.broadcasted_iota(jnp.int32, (1, 128), 1), HEAD_DIM - 1) >= ROT
        cs = cs_r[0]
        tc_r[...] = spread(cs[0:8, :], 0, ROT) + jnp.where(still, 1.0, 0.0)
        ta_r[...] = spread(-cs[8:16, :], 0, ROT // 2)
        tb_r[...] = spread(cs[8:16, :], ROT // 2, ROT)
        last = jnp.broadcast_to(sr_r[0].astype(F32), (8, length))
        sg_s[...] = pltpu.roll(last, length - FIRST_DOC, 1)[:, : sg_s.shape[1]]
        seg_cols = sg_s[...].T[:tail, 0:1]

        def turn(v, c, a, b, sign):
            return v * c + sign * (pltpu.roll(v, 120, 1) * a + pltpu.roll(v, 8, 1) * b)

        def tabs(at, keys):
            c = tc_r[pl.ds(at, chunk), :]
            a = ta_r[pl.ds(at, chunk), :]
            b = tb_r[pl.ds(at, chunk), :]
            if keys:
                c = jnp.where(low, c, 1.0)
                a = jnp.where(low, a, 0.0)
                b = jnp.where(low, b, 0.0)
            return c, a, b

        @pl.loop(0, n_chunk)
        def _(n):
            at = pl.multiple_of(n * chunk, chunk)
            sl = pl.ds(at, chunk)
            lin = dnn(na_r[sl, :], wqs[...]) + qb_all
            tq = tabs(at, False)
            for p in range(pairs):
                v = turn(lin[:, p * 128 : (p + 1) * 128], *tq, 1.0)
                q_s[sl, p * 128 : (p + 1) * 128] = v.astype(BF16) * BF16(0.125)
            v = turn(lin[:, wh:], *tabs(at, True), 1.0)
            kv = v.astype(BF16)
            cache[sl, :] = kv
            vr = pltpu.roll(v, 64, 1)
            zero = jnp.zeros_like(v)
            kz[sl, :] = jnp.where(low, v, zero).astype(BF16)
            zv[sl, :] = jnp.where(low, zero, v).astype(BF16)
            zk[sl, :] = jnp.where(low, zero, vr).astype(BF16)
            vz[sl, :] = jnp.where(low, vr, zero).astype(BF16)
            do_s[sl, :] = dnt(dy_r[sl, :], wo[...]).astype(BF16)

        @pl.loop(0, pairs)
        def _(p):
            cols = pl.ds(pl.multiple_of(p * 128, 128), 128)
            for r0, rn, k0, kn, segs in blocks:
                q2 = q_s[r0 : r0 + rn, cols]
                do2 = do_s[r0 : r0 + rn, cols]
                dof = do2.astype(F32)
                keys = [ks[k0 : k0 + kn, :] for ks in (kz, zk)]
                vals = [vs[k0 : k0 + kn, :] for vs in (vz, zv)]
                free = 0 if segs else r0 // 128 * 128
                qi = lax.broadcasted_iota(jnp.int32, (rn, kn - free), 0) + r0
                ki = lax.broadcasted_iota(jnp.int32, (rn, kn - free), 1) + k0 + free
                allowed = ki <= qi
                if segs:
                    allowed = allowed & (seg_cols == sg_s[0:1, :tail])
                exps, invs = [], []
                for kk in keys:
                    logit = dnt(q2, kk)
                    edge = jnp.where(allowed, logit[:, free:], -1e30)
                    logit = jnp.concatenate([logit[:, :free], edge], axis=1) if free else edge
                    ex = jnp.exp(logit - jnp.max(logit, axis=-1, keepdims=True))
                    exps.append(ex)
                    invs.append(1.0 / jnp.sum(ex, axis=-1, keepdims=True))
                scale = jnp.where(low, invs[0], invs[1])
                dos = (dof * scale).astype(BF16)
                exb = [ex.astype(BF16) for ex in exps]
                o2 = (dnn(exb[0], vals[0]) + dnn(exb[1], vals[1])) * scale
                o_s[r0 : r0 + rn, cols] = o2.astype(BF16)
                dsb = []
                for e in range(2):
                    dp = dnt(dos, vals[e])
                    mean = jnp.sum(exps[e] * dp, axis=-1, keepdims=True) * invs[e]
                    dsb.append((exps[e] * (dp - mean)).astype(BF16))
                dq_s[r0 : r0 + rn, cols] = dnn(dsb[0], keys[0]) + dnn(dsb[1], keys[1])
                for e, (ak, av) in enumerate(((ek, ev), (ok, ov))):
                    ak[k0 : k0 + kn, :] += dtn(dsb[e], q2)
                    av[k0 : k0 + kn, :] += dtn(exb[e], dos)

        @pl.loop(0, n_chunk)
        def _(n):
            at = pl.multiple_of(n * chunk, chunk)
            sl = pl.ds(at, chunk)
            tq = tabs(at, False)
            for p in range(pairs):
                cc = slice(p * 128, (p + 1) * 128)
                v = turn(dq_s[sl, cc] * 0.125, *tq, -1.0)
                sums[:, cc] += sum8(v)
                gqs_s[sl, cc] = v.astype(BF16)
            gk = ek[sl, :] + pltpu.roll(ok[sl, :], 64, 1)
            gv = pltpu.roll(ev[sl, :], 64, 1) + ov[sl, :]
            v = jnp.where(low, gk, gv)
            v = v + jnp.where(step == 1, cg_r[sl, :].astype(F32), 0.0)
            v = turn(v, *tabs(at, True), -1.0)
            sums[:, wh:] += sum8(v)
            gqs_s[sl, wh:] = v.astype(BF16)

    def fixed(dims, at=(0, 0)):
        return pl.BlockSpec(dims, lambda i: at, pipeline_mode=pl.Buffered(1))

    def seq(lanes):
        return pl.BlockSpec((length, lanes), lambda i: (1 - i, 0))

    seg_w = (tail + 127) // 128 * 128
    total = na.shape[0]
    return pl.pallas_call(
        kern,
        grid=(2,),
        in_specs=[SMEM, seq(width), seq(width), fixed((16, width))]
        + [pl.BlockSpec((1, 16, length), lambda i: (1 - i, 0, 0)), pl.BlockSpec((1, 1, length), lambda i: (1 - i, 0, 0))]
        + [fixed((length, 128))]
        + [fixed((rows, wq)), fixed((rows, wq), (core_rows // rows - 1, 0)), fixed(weights[2].shape), fixed((o_rows, width))],
        out_specs=[seq(wh), seq(wq), fixed((length, 128)), fixed((8, wq)), fixed((width, wq)), fixed((wh, width))],
        out_shape=[
            shape((total, wh), BF16), shape((total, wq), BF16), shape((length, 128), BF16), shape((8, wq), F32),
            shape((width, wq), BF16), shape((wh, width), BF16),
        ],
        scratch_shapes=[
            pltpu.VMEM((length, wh), BF16),
            pltpu.VMEM((length, wh), BF16),
            pltpu.VMEM((length, wh), F32),
        ]
        + [pltpu.VMEM((length, 128), BF16)] * 4
        + [pltpu.VMEM((length, 128), F32)] * 7
        + [pltpu.VMEM((8, seg_w), F32)],
        cost_estimate=pl.CostEstimate(
            flops=4 * length * width * (wq + wh) + 24 * length * length * wh,
            bytes_accessed=12 * length * width,
            transcendentals=length * length * wh // 64,
        ),
        name="attention",
    )(sc, na, dy, vec, waves_of, seg_rows, cgrad, *weights)


def attn_terms(sc, nat, dyt, o_all, gqs_all, wqs, vec, sums, ob, ubs, rss):
    width, total = nat.shape
    wq = gqs_all.shape[1]
    wh = o_all.shape[1]
    blk = total // 4
    half = width // 2
    o_rows = width // 4
    n_w = len(ubs)

    def kern(sc_ref, nat_r, dyt_r, o_r, g_r, w_r, vec_r, s0, ob_r, *refs):
        ub_r, rs_r = refs[:n_w], refs[n_w : 2 * n_w]
        keep, send, acc_q, acc_o, tbl = refs[2 * n_w :]
        s = sc_ref[0]
        c = jnp.bitwise_and(s, 1)
        y = jnp.right_shift(s, 1)
        i = pl.program_id(0)
        pq = dnn(nat_r[...], g_r[...])
        po = dnn(dyt_r[...], o_r[...])

        @pl.when(i == 0)
        def _():
            acc_q[...] = pq
            acc_o[...] = po

        @pl.when(i > 0)
        def _():
            acc_q[...] += pq
            acc_o[...] += po

        @pl.when(i == pl.num_programs(0) - 1)
        def _():
            mine = pl.multiple_of(y * half, 16)
            other = pl.multiple_of((1 - y) * half, 16)
            keep[:half, :] = acc_q[pl.ds(mine, half), :].astype(BF16)
            send[:half, :] = acc_q[pl.ds(other, half), :].astype(BF16)
            got = acc_o[...].T
            lower = got[:o_rows, :].astype(BF16)
            upper = got[o_rows:, :].astype(BF16)
            fold(keep, half, o_rows, jnp.where(y == 0, lower, upper), wq)
            fold(send, half, o_rows, jnp.where(y == 0, upper, lower), wq)
            line = lambda v: jnp.sum(v, axis=0, keepdims=True)
            w = w_r[...].astype(F32)
            both = s0[...]
            fs = line(col_sums(w * line(both)))
            fg = line(col_sums(w * acc_q[...]))
            ss = sum([line(r[8:16, :]) for r in rs_r])
            sg = sum([line(r[0:8, :]) for r in rs_r])
            tbl[...] = jnp.zeros_like(tbl)
            tbl[0:1, :] = (fg - vec_r[1:2, :] * fs) / vec_r[0:1, :]
            tbl[1:2, :] = fs
            tbl[2:3, :] = (sg - vec_r[3:4, :] * ss) / vec_r[2:3, :]
            tbl[3:4, :] = ss
            tbl[4:5, :] = line(ob_r[...])
            qb8 = jnp.broadcast_to(line(both[:, :wh]), (8, wh))
            tbl[5:6, :] = head_spread(qb8, c, width)[0:1, :]
            tbl[6:7, : wq - wh] = line(both[:, wh:])
            for w_i, ref in enumerate(ub_r):
                u = line(ref[...])
                wd = wq // 2
                tbl[pl.ds(8 + s, 1), w_i * wd : (w_i + 1) * wd] = u[:, :wd]
                tbl[pl.ds(8 + jnp.bitwise_xor(s, 2), 1), w_i * wd : (w_i + 1) * wd] = u[:, wd:]
            at = half + o_rows * 3 // 2
            for out in (keep, send):
                out[at : at + 16, :] = tbl[:, :wq].astype(BF16)
                out[at + 16 : at + 32, : width - wq] = tbl[:, wq:].astype(BF16)
                out[at + 16 : at + 32, width - wq :] = jnp.zeros((16, 2 * wq - width), BF16)
                out[at + 32 :, :] = jnp.zeros((width - at - 32, wq), BF16)

    def fixed(dims):
        return pl.BlockSpec(dims, lambda i: (0, 0))

    col = pl.BlockSpec((width, blk), lambda i: (0, i))
    return pl.pallas_call(
        kern,
        grid=(4,),
        in_specs=[SMEM, col, col, pl.BlockSpec((blk, wh), lambda i: (i, 0)), pl.BlockSpec((blk, wq), lambda i: (i, 0))]
        + [fixed((width, wq)), fixed((16, width)), fixed((8, wq)), fixed((8, width))]
        + [fixed((8, wq))] * n_w
        + [fixed((16, width))] * n_w,
        out_specs=[fixed((width, wq))] * 2,
        out_shape=[shape((width, wq), BF16)] * 2,
        scratch_shapes=[pltpu.VMEM((width, wq), F32), pltpu.VMEM((width, wh), F32), pltpu.VMEM((16, width), F32)],
        cost_estimate=pl.CostEstimate(
            flops=2 * total * width * (wq + wh), bytes_accessed=4 * total * width, transcendentals=0
        ),
        name="attn_terms",
    )(sc, nat, dyt, o_all, gqs_all, wqs, vec, sums, ob, *ubs, *rss)


def outputs(which, hids, gls, ups, downs, o_all, gqs_all, wo, wqs, vec):
    total, wid2 = hids[0].shape
    width = wqs.shape[0]
    n_w = len(hids)
    blk = total // 8
    base = 4 * which

    def kern(*refs):
        h_r, g_r, u_r, d_r = (refs[k * n_w : (k + 1) * n_w] for k in range(4))
        o_r, q_r, wo_r, wq_r, vec_r, out, hp = refs[4 * n_w :]
        br = dnn(o_r[...], wo_r[...])
        ea = dnt(q_r[...], wq_r[...])
        em = None
        for w in range(n_w):
            br = br + dnn(h_r[w][...], d_r[w][...])
            t = dnt(g_r[w][...], u_r[w][...])
            em = t if em is None else em + t
        out[...] = br.astype(BF16)
        hp[...] = (ea * vec_r[0:1, :] + em * vec_r[2:3, :]).astype(BF16)

    def rows(lanes):
        return pl.BlockSpec((blk, lanes), lambda i: (i + base, 0))

    def fixed(dims):
        return pl.BlockSpec(dims, lambda i: (0, 0))

    res = pl.BlockSpec((blk, width), lambda i: (i, 0))
    return pl.pallas_call(
        kern,
        grid=(4,),
        in_specs=[rows(wid2)] * (2 * n_w)
        + [fixed((width, wid2))] * n_w
        + [fixed((wid2, width))] * n_w
        + [rows(o_all.shape[1]), rows(gqs_all.shape[1]), fixed(wo.shape), fixed(wqs.shape), fixed((16, width))],
        out_specs=[res, res],
        out_shape=[shape((total // 2, width), BF16)] * 2,
        cost_estimate=pl.CostEstimate(
            flops=total * width * (2 * n_w * wid2 + 900), bytes_accessed=12 * total * width, transcendentals=0
        ),
        name="outputs",
    )(*hids, *gls, *ups, *downs, o_all, gqs_all, wo, wqs, vec)


def finish(tok, dy, out_own, out_in, h_own, h_in, vec):
    n_tok, width = tok.shape
    blk = n_tok // 4

    def kern(tok_r, dy_r, oo, oi, ho, hi, vec_r, out, tg):
        x = tok_r[...].astype(F32)
        xhat, rstd = normalize(x)
        out[...] = (x + oo[...].astype(F32) + oi[...].astype(F32) + vec_r[4:5, :] + vec_r[5:6, :]).astype(BF16)
        h = ho[...].astype(F32) + hi[...].astype(F32)
        mean = jnp.mean(h, axis=-1, keepdims=True)
        cov = jnp.mean(h * xhat, axis=-1, keepdims=True)
        tg[...] = (dy_r[...].astype(F32) + rstd * (h - mean - xhat * cov)).astype(BF16)

    row = pl.BlockSpec((blk, width), lambda i: (i, 0))
    return pl.pallas_call(
        kern,
        grid=(4,),
        in_specs=[row] * 6 + [pl.BlockSpec((16, width), lambda i: (0, 0))],
        out_specs=[row, row],
        out_shape=[shape((n_tok, width), BF16)] * 2,
        cost_estimate=pl.CostEstimate(
            flops=20 * n_tok * width, bytes_accessed=16 * n_tok * width, transcendentals=0
        ),
        name="finish",
    )(tok, dy, out_own, out_in, h_own, h_in, vec)


def piece_row(sc_ref, n, h):
    b0, b1 = jnp.bitwise_xor(sc_ref[1], n & 1), jnp.bitwise_xor(sc_ref[2], n >> 1)
    return pl.multiple_of(b0 * (h // 2) + b1 * (h // 4), 8)


def mlp_grads(sc, pieces, width, ff):
    prow, wid2 = pieces[0][0].shape[1:]
    wid = wid2 // 2
    chunk = ff // 4
    shard_rows = width // 4
    flat = [p for ps in pieces for p in ps]
    n_p = len(pieces[0])

    def kern(sc_ref, *refs):
        up, down, tmp = refs[-3:]
        s = sc_ref[0]
        for w in range(WAVES):
            for n in range(n_p):
                ref = refs[w * n_p + n]
                at = piece_row(sc_ref, n, shard_rows)
                for p in range(4):
                    for h in range(2):
                        v = ref[p, :, h * wid : (h + 1) * wid].astype(F32)
                        if p < 2:
                            t = jnp.bitwise_xor(s, p + 2 * h)
                            lanes = pl.multiple_of(t * chunk + w * wid, 256)
                            up[pl.ds(at, prow), pl.ds(lanes, wid)] = v
                        else:
                            tmp[pl.ds((2 * h + p - 2) * shard_rows + at, prow), :] = v
            down[w * wid : (w + 1) * wid, :] = tmp[...].T

    return pl.pallas_call(
        kern,
        in_specs=[SMEM] + [VM] * len(flat),
        out_specs=[VM, VM],
        out_shape=[shape((shard_rows, ff), F32), shape((chunk, width), F32)],
        scratch_shapes=[pltpu.VMEM((width, wid), F32)],
        cost_estimate=pl.CostEstimate(flops=0, bytes_accessed=12 * shard_rows * ff, transcendentals=0),
        name="mlp_grads",
    )(sc, *flat)


def attn_grads(sc, pieces, width, shared_w):
    n_p = len(pieces)
    _, prow, wq = pieces[0].shape
    part = width // 4
    wh = wq - shared_w

    def kern(sc_ref, *refs):
        full = refs[-1]
        ins = refs[:n_p]
        gq, gs, go = refs[n_p : n_p + 3]
        lines = refs[n_p + 3 : -1]
        s = sc_ref[0]
        c = jnp.bitwise_and(s, 1)
        for n in range(n_p):
            at = piece_row(sc_ref, n, part // 2)
            for p in range(8):
                full[pl.ds(p * (part // 2) + at, prow), :] = ins[n][p].astype(F32)
        gq[...] = head_spread(full[:part, :wh], c, width) + head_spread(full[part : 2 * part, :wh], 1 - c, width)
        gs[...] = full[:part, wh:]
        go[...] = unfold(full, 2 * part, part, wq)
        at = 2 * part + part * 3 // 2
        tab = jnp.concatenate([full[at : at + 16, :], full[at + 16 : at + 32, : width - wq]], axis=1)
        left = pltpu.roll(tab, (width - s * part) % width, 1)
        for out, i in zip(lines, (0, 1, 2, 3, 4, 5)):
            out[...] = left[i : i + 1, :part]
        few = shared_w // 4
        lines[6][...] = pltpu.roll(tab, (width - s * few) % width, 1)[6:7, :few]
        full[0:16, :] = tab[:, :wq]
        full[16:32, : width - wq] = tab[:, wq:]
        lines[7][:, :wq] = full[pl.ds(8 + s, 1), :]
        lines[7][:, wq:] = full[pl.ds(24 + s, 1), : width - wq]

    return pl.pallas_call(
        kern,
        in_specs=[SMEM] + [VM] * n_p,
        out_specs=[VM] * 11,
        out_shape=[shape((part, width), F32), shape((part, shared_w), F32), shape((part, width), F32)]
        + [shape((1, part), F32)] * 6
        + [shape((1, shared_w // 4), F32), shape((1, width), F32)],
        scratch_shapes=[pltpu.VMEM((width, wq), F32)],
        name="attn_grads",
    )(sc, *pieces)


def to_shard(value, k):
    return lax.ppermute(value, "shard", [(s, s ^ k) for s in range(4)])


def to_replica(value, k, count):
    return lax.ppermute(value, "replica", [(r, r ^ k) for r in range(count)])


def both_add(a, b):
    return (a.astype(F32) + b.astype(F32)).astype(BF16)


def after(value, *others):
    return lax.optimization_barrier((value,) + others)[0]


def send_y(value):
    return to_shard(value, 2)


def reduce_chain(keep, got, count, rank, mix, join):
    def halve(mine, other, k):
        h = mine.shape[1] // 2
        b = (rank // k) & 1

        def cut(which):
            f = lambda v: lax.dynamic_slice_in_dim(v, which * h, h, axis=1)
            return both_add(f(mine), f(other))

        half, away = cut(b), cut(1 - b)
        return half, to_replica(away, k, count)

    half, got = halve(keep, got, 1)
    half, got = halve(half, got, 2)
    half = both_add(half, got)
    k = 4
    while k < count:
        half = both_add(half, to_replica(half, k, count))
        k *= 2
    sent, kept = mix(half)
    half = join(kept, to_shard(sent, 1))
    return [half] + [to_replica(half, k, count) for k in (1, 2, 3)]


def shards(
    tokens, segment_ids, positions, first_gain, first_shift, query_weight, query_bias, shared_weight,
    shared_bias, output_weight, output_bias, second_gain, second_shift, up_weight, up_bias, down_weight,
    down_bias, result_grad, shared_grad, *, replicas,
):
    width = tokens.shape[1]
    ff = up_weight.shape[1]
    part = width // 4
    sw = shared_weight.shape[1]
    s = lax.axis_index("shard")
    r = lax.axis_index("replica")
    c = s & 1
    sc = jnp.stack([s, r & 1, (r >> 1) & 1]).astype(jnp.int32)

    small = pack_small(
        sc,
        [first_gain, first_shift, second_gain, second_shift, output_bias, down_bias, query_bias],
        shared_bias, up_bias,
    )
    near = [small] + [to_shard(small, k) for k in (1, 2, 3)]
    own0, k1, k3, m2 = pack_first(sc, after(up_weight, small), down_weight)
    k1 = to_shard(k1, 1)
    m2 = to_shard(m2, 2)
    k3 = to_shard(k3, 3)
    core_out = pack_core(sc, after(up_weight, own0), query_weight, shared_weight)
    core_got = to_shard(core_out, 1)
    tok_in = to_shard(tokens, 1)
    dy_in = to_shard(result_grad, 1)
    ints_in = to_shard(jnp.concatenate([segment_ids, positions], axis=0), 1)

    prev, ob, vec = norm_pair(0, tokens, result_grad, near, [])
    prev, _, _ = norm_pair(1, tok_in, dy_in, near, prev)
    nm, nmt, na, nat, dy, dyt = prev
    own1, own2, ownq, y1, y2, ya = pack_rest(
        sc, up_weight, down_weight, query_weight, shared_weight, output_weight, after(core_got, vec)
    )

    pos = jnp.concatenate([positions, ints_in[1:]], axis=0)
    inv = 10000.0 ** (-2.0 * jnp.arange(ROT // 2, dtype=F32) / ROT)
    ang = pos.astype(F32)[:, None, :] * inv[None, :, None]
    angles = jnp.concatenate([jnp.cos(ang), jnp.sin(ang)], axis=1)
    segs = jnp.stack([segment_ids, ints_in[:1]])

    rows = part

    def mix_mlp(v):
        mine = jnp.where(c == 0, v[0], v[1])
        theirs = jnp.where(c == 0, v[1], v[0])
        return theirs, (mine, v[2:])

    def join_mlp(kept, got):
        return jnp.concatenate([kept[0][None], got[None], kept[1]], axis=0)

    wh = width // 2

    def mix_attn(v):
        mine = jnp.where(c == 0, v[:2], v[2:4])
        theirs = jnp.where(c == 0, v[2:4], v[:2])
        return jnp.concatenate([theirs, v[7:]], axis=0), (mine, v[4:7], v[7:])

    def join_attn(kept, got):
        mine, outs_rows, table = kept
        front = jnp.concatenate([mine[:, :, :wh], both_add(mine[:, :, wh:], got[:2, :, wh:])], axis=2)
        return jnp.concatenate([front, got[:2], outs_rows, both_add(table, got[2:])], axis=0)

    def wave(w, pieces, down_at, split):
        return mlp_wave(w, sc, nm, nmt, dy, dyt, pieces, down_at, down_weight, vec, split)

    m1 = to_shard(y1, 2)
    hid0, gl0, wu0, wd0, ub0, rs0, keep0, send0 = wave(0, [(own0, 0), (k1, 0), (m2, 0), (k3, 0)], (m2, rows), False)
    ma = to_shard(after(ya, m1), 2)
    hid1, gl1, wu1, wd1, ub1, rs1, keep1, send1 = wave(
        1, [(own1, 0), (core_got, 0), (m1, 0), (m1, rows)], (m1, 2 * rows), False
    )
    m2b = to_shard(after(y2, ma), 2)
    got0 = send_y(after(send0, ma))
    got1 = send_y(after(send1, ma))
    o_all, gqs_all, cache, sums, wqs, wo = attention(
        sc, na, dy, (ownq, core_got, ma, output_weight), vec, angles, segs, shared_grad
    )
    hid2, gl2, wu2, wd2, ub2, rs2, keep2, send2 = wave(
        2, [(own2, 0), (core_got, 2 * rows), (m2b, 0), (m2b, rows)], (m2b, 2 * rows), False
    )
    keepa, senda = attn_terms(
        sc, nat, dyt, o_all, gqs_all, wqs, vec, sums, ob, (ub0, ub1, ub2), (rs0, rs1, rs2)
    )

    def chain(keep, got, planes, mix, join):
        lanes = keep.shape[1]
        return reduce_chain(keep.reshape(planes, -1, lanes), got.reshape(planes, -1, lanes), replicas, r, mix, join)

    p0 = chain(keep0, got0, 4, mix_mlp, join_mlp)
    p1 = chain(keep1, got1, 4, mix_mlp, join_mlp)
    p2 = chain(keep2, send_y(send2), 4, mix_mlp, join_mlp)
    pa = chain(keepa, send_y(senda), 8, mix_attn, join_attn)

    hids, gls, wus, wds = (hid0, hid1, hid2), (gl0, gl1, gl2), (wu0, wu1, wu2), (wd0, wd1, wd2)

    def outs(which):
        return outputs(which, hids, gls, wus, wds, o_all, gqs_all, wo, wqs, vec)

    out_p, h_p = outs(1)
    out_in = to_shard(out_p, 1)
    h_in = to_shard(h_p, 1)
    out_o, h_o = outs(0)
    block_output, tokens_grad = finish(tokens, result_grad, out_o, out_in, h_o, h_in, vec)

    grad_up, grad_down = mlp_grads(sc, [p0, p1, p2], width, ff)
    out = attn_grads(sc, pa, width, sw)
    grad_q, grad_s, grad_o = out[:3]
    fg, fs, sg, ss, ob_g, qb_g, sb_g, ub_g = [v.reshape(-1) for v in out[3:]]
    return (
        block_output, cache, tokens_grad,
        fg, fs, grad_q, qb_g, grad_s, sb_g, grad_o, ob_g,
        sg, ss, grad_up, ub_g, grad_down, ob_g,
    )


def solution(mesh):
    both = P(("replica", "shard"), None)
    one, two = P("shard"), P("shard", None)

    def body(*args):
        return shards(*args, replicas=mesh.shape["replica"])

    return jax.shard_map(
        body,
        mesh=mesh,
        in_specs=(both, both, both, one, one, two, one, two, one, two, one, one, one, two, one, two, one, both, both),
        out_specs=(both, both, both, one, one, two, one, two, one, two, one, one, one, two, one, two, one),
        check_vma=False,
    )
```

```python
import jax
import jax.numpy as jnp
from jax import lax
from jax.experimental import pallas as pl
from jax.experimental.pallas import tpu as pltpu
from jax.sharding import PartitionSpec as P


HEAD_DIM = 64
ROT = 16
FIRST_DOC = 800
EPS = 1e-05
F32 = jnp.float32
BF16 = jnp.bfloat16
WAVES = 3


def dnn(a, b):
    return lax.dot_general(a, b, (((1,), (0,)), ((), ())), preferred_element_type=F32)


def dnt(a, b):
    return lax.dot_general(a, b, (((1,), (1,)), ((), ())), preferred_element_type=F32)


def dtn(a, b):
    return lax.dot_general(a, b, (((0,), (0,)), ((), ())), preferred_element_type=F32)


def sum8(v):
    return jnp.sum(v.reshape(-1, 8, v.shape[1]), axis=0)


def normalize(x):
    centre = x - jnp.mean(x, axis=-1, keepdims=True)
    var = jnp.mean(centre * centre, axis=-1, keepdims=True)
    rstd = lax.rsqrt(var + EPS)
    return centre * rstd, rstd


ANY = pl.BlockSpec(memory_space=pl.ANY)
SMEM = pl.BlockSpec(memory_space=pltpu.SMEM)
VM = pl.BlockSpec(memory_space=pltpu.VMEM)


def shape(dims, kind):
    return jax.ShapeDtypeStruct(dims, kind)


def head_columns(w, c):
    width = w.shape[1]
    part = width // 4
    lane = lax.broadcasted_iota(jnp.int32, (1, width), 1)
    r = pltpu.roll(w, (width - c * part) % width, 1)
    return jnp.where(lane < part, r, pltpu.roll(r, width - part, 1))[:, : 2 * part]


def head_spread(x, c, width):
    part = width // 4
    lane = lax.broadcasted_iota(jnp.int32, (1, width), 1)
    v = jnp.concatenate([x, jnp.zeros_like(x)], axis=1)
    zero = jnp.zeros_like(v)
    u = jnp.where(lane < part, v, zero)
    u = u + pltpu.roll(jnp.where((lane >= part) & (lane < 2 * part), v, zero), part, 1)
    return pltpu.roll(u, c * part, 1)


def up_piece(w_ref, s, k, w, chunk):
    wid = chunk // WAVES
    t = jnp.bitwise_xor(s, k)
    a = pl.multiple_of(t * chunk + w * wid, 256)
    b = pl.multiple_of(jnp.bitwise_xor(t, 2) * chunk + w * wid, 256)
    return jnp.concatenate([w_ref[:, pl.ds(a, wid)], w_ref[:, pl.ds(b, wid)]], axis=1)


def fold(out, at, rows, v, lanes):
    h = rows // 2
    out[at : at + rows, :] = v[:, :lanes]
    out[at + rows : at + rows + h, : lanes // 2] = v[:h, lanes:]
    out[at + rows : at + rows + h, lanes // 2 :] = v[h:, lanes:]


def unfold(ref, at, rows, lanes):
    h = rows // 2
    top = ref[at : at + rows, :]
    low = ref[at + rows : at + rows + h, :]
    return jnp.concatenate(
        [top, jnp.concatenate([low[:, : lanes // 2], low[:, lanes // 2 :]], axis=0)], axis=1
    )


def pack_small(sc, seven, shared_bias, up_bias):
    part = seven[0].shape[0]
    width = up_bias.shape[0]
    few = shared_bias.shape[0]

    def kern(sc_ref, *refs):
        out, tmp = refs[-2:]
        s = sc_ref[0]
        tmp[...] = jnp.zeros_like(tmp)
        for i in range(7):
            tmp[i : i + 1, :part] = refs[i][...].astype(F32).reshape(1, part)
        tmp[:7, :] = pltpu.roll(tmp[0:8, :], s * part, 1)[:7]
        tmp[7:8, :few] = refs[7][...].astype(F32).reshape(1, few)
        tmp[7:8, :] = pltpu.roll(tmp[0:8, :], s * few, 1)[7:8]
        tmp[pl.ds(8 + s, 1), :] = refs[8][...].astype(F32).reshape(1, width)
        out[...] = tmp[...].astype(BF16)

    return pl.pallas_call(
        kern,
        in_specs=[SMEM] + [VM] * 9,
        out_specs=VM,
        out_shape=shape((16, width), BF16),
        scratch_shapes=[pltpu.VMEM((16, width), F32)],
        name="pack_small",
    )(sc, *seven, shared_bias, up_bias)


def pack_first(sc, up_weight, down_weight):
    rows, ff = up_weight.shape
    chunk, width = down_weight.shape
    wid = chunk // WAVES

    def kern(sc_ref, w_ref, d_ref, own, k1, k3, m2):
        s = sc_ref[0]
        own[...] = up_piece(w_ref, s, 0, 0, chunk)
        k1[...] = up_piece(w_ref, s, 1, 0, chunk)
        k3[...] = up_piece(w_ref, s, 3, 0, chunk)
        m2[:rows, :] = up_piece(w_ref, s, 2, 0, chunk)
        fold(m2, rows, wid, d_ref[...], 2 * wid)

    return pl.pallas_call(
        kern,
        grid=(1,),
        in_specs=[SMEM, pl.BlockSpec((rows, ff), lambda i: (0, 0)), pl.BlockSpec((wid, width), lambda i: (0, 0))],
        out_specs=[pl.BlockSpec((rows, 2 * wid), lambda i: (0, 0))] * 3
        + [pl.BlockSpec((rows + wid * 3 // 2, 2 * wid), lambda i: (0, 0))],
        out_shape=[shape((rows, 2 * wid), BF16)] * 3 + [shape((rows + wid * 3 // 2, 2 * wid), BF16)],
        name="pack_first",
    )(sc, up_weight, down_weight)


def pack_core(sc, up_weight, query_weight, shared_weight):
    rows, ff = up_weight.shape
    width = query_weight.shape[1]
    chunk = ff // 4
    wid = chunk // WAVES
    n = 2 * (WAVES - 1)
    half = width // 2

    def kern(sc_ref, w_ref, q_ref, s_ref, out):
        s = sc_ref[0]
        c = jnp.bitwise_and(s, 1)
        for w in range(1, WAVES):
            for i, k in enumerate((1, 3)):
                at = (2 * (w - 1) + i) * rows
                out[at : at + rows, :] = up_piece(w_ref, s, k, w, chunk)
        out[n * rows :, :half] = head_columns(q_ref[...].astype(F32), 1 - c).astype(BF16)
        out[n * rows :, half:] = s_ref[...]

    return pl.pallas_call(
        kern,
        in_specs=[SMEM, VM, VM, VM],
        out_specs=VM,
        out_shape=shape(((n + 1) * rows, 2 * wid), BF16),
        name="pack_core",
    )(sc, up_weight, query_weight, shared_weight)


def pack_rest(sc, up_weight, down_weight, query_weight, shared_weight, output_weight, got):
    rows, _ = up_weight.shape
    chunk, width = down_weight.shape
    wid = chunk // WAVES
    lanes = 2 * wid
    n = 2 * (WAVES - 1)
    half = width // 2

    def kern(sc_ref, w_ref, d_ref, q_ref, s_ref, o_ref, g_ref, own1, own2, ownq, y1, y2, ya):
        s = sc_ref[0]
        c = jnp.bitwise_and(s, 1)
        for w, own, out in ((1, own1, y1), (2, own2, y2)):
            own[...] = up_piece(w_ref, s, 0, w, chunk)
            out[:rows, :] = up_piece(w_ref, s, 2, w, chunk)
            at = (2 * (w - 1) + 1) * rows
            out[rows : 2 * rows, :] = g_ref[at : at + rows, :]
            fold(out, 2 * rows, wid, d_ref[w * wid : (w + 1) * wid, :], lanes)
        mine = head_columns(q_ref[...].astype(F32), c).astype(BF16)
        for out in (ownq, ya):
            out[:rows, :half] = mine
            out[:rows, half:] = s_ref[...]
        ya[rows : 2 * rows, :] = g_ref[n * rows :, :]
        fold(ya, 2 * rows, rows, o_ref[...], lanes)

    msg = 2 * rows + wid * 3 // 2
    msg_a = 2 * rows + rows * 3 // 2
    return pl.pallas_call(
        kern,
        in_specs=[SMEM] + [VM] * 6,
        out_specs=[VM] * 6,
        out_shape=[shape((rows, lanes), BF16)] * 3
        + [shape((msg, lanes), BF16)] * 2
        + [shape((msg_a, lanes), BF16)],
        name="pack_rest",
    )(sc, up_weight, down_weight, query_weight, shared_weight, output_weight, got)


def norm_pair(which, tok, dy, near, prev):
    n_tok, width = tok.shape
    n_near = len(near)
    blk = n_tok // 2
    base = 2 * which

    def kern(tok_ref, dy_ref, *refs):
        nm, na, dyc, ob, vec_ref = refs[n_near + len(prev) :]
        vec_ref[...] = sum([r[...].astype(F32) for r in refs[1:n_near]], refs[0][...].astype(F32))
        xhat, _ = normalize(tok_ref[...].astype(F32))
        a = (xhat * vec_ref[0:1, :] + vec_ref[1:2, :]).astype(BF16)
        m = (xhat * vec_ref[2:3, :] + vec_ref[3:4, :]).astype(BF16)
        g = dy_ref[...]
        na[...] = a
        nm[...] = m
        dyc[...] = g

        @pl.when(pl.program_id(0) == 0)
        def _():
            ob[...] = jnp.zeros_like(ob)

        ob[...] += sum8(g.astype(F32))

    row = pl.BlockSpec((blk, width), lambda i: (i + base, 0))
    src = pl.BlockSpec((blk, width), lambda i: (i, 0))
    whole = pl.BlockSpec((8, width), lambda i: (0, 0))
    small = pl.BlockSpec((16, width), lambda i: (0, 0))
    res = pl.pallas_call(
        kern,
        grid=(2,),
        in_specs=[src, src] + [small] * n_near + [ANY] * len(prev),
        out_specs=[row, row, row, whole, small],
        out_shape=[shape((2 * n_tok, width), BF16)] * 3
        + [shape((8, width), F32), shape((16, width), F32)],
        input_output_aliases={2 + n_near + i: i for i in range(len(prev))},
        cost_estimate=pl.CostEstimate(
            flops=20 * n_tok * width, bytes_accessed=16 * n_tok * width, transcendentals=0
        ),
        name="norm_pair",
    )(tok, dy, *near, *prev)
    return res[:3], res[3], res[4]


def write_table(outs, tbl, lanes):
    width = tbl.shape[1]
    for out in outs:
        at = out.shape[0] - 32
        out[at : at + 16, :] = tbl[:, :lanes].astype(BF16)
        out[at + 16 :, : width - lanes] = tbl[:, lanes:].astype(BF16)
        out[at + 16 :, width - lanes :] = jnp.zeros((16, 2 * lanes - width), BF16)


def put_hidden_bias(tbl, s, w, u):
    wd = u.shape[1] // 2
    tbl[pl.ds(8 + s, 1), w * wd : (w + 1) * wd] = u[:, :wd]
    tbl[pl.ds(8 + jnp.bitwise_xor(s, 2), 1), w * wd : (w + 1) * wd] = u[:, wd:]


def col_sums(v):
    part = v[:, :128]
    for i in range(128, v.shape[1], 128):
        part = part + v[:, i : i + 128]
    return sum8(part.T)


def mlp_wave(wave, sc, nm, dy, pieces, down_at, down_own, vec, table=None):
    n_tok, width = nm.shape
    blk = n_tok // 4
    rows = width // 4
    chunk = down_own.shape[0]
    wid = chunk // WAVES
    wid2 = 2 * wid
    half = width // 2
    srcs = []
    for arr, _ in list(pieces) + [down_at]:
        if not any(arr is t for t in srcs):
            srcs.append(arr)
    where = [next(i for i, t in enumerate(srcs) if t is arr) for arr, _ in list(pieces) + [down_at]]
    n_src = len(srcs)

    def kern(sc_ref, nm_r, dy_r, d0, vec_r, *refs):
        got, refs = refs[:n_src], refs[n_src:]
        if table is not None:
            t_r, refs = refs[0], refs[1:]
        hid_o, gl_o, w_s, wd_s, ub, rs = refs[:6]
        b_s, acc_u, acc_d, tbl = refs[-4:]
        keep, to1, to2, to3 = refs[6:-4]
        i = pl.program_id(0)
        s = sc_ref[0]

        @pl.when(i == 0)
        def _():
            acc_u[...] = jnp.zeros_like(acc_u)
            acc_d[...] = jnp.zeros_like(acc_d)
            ub[...] = jnp.zeros_like(ub)
            for k in range(4):
                at = pl.multiple_of(jnp.bitwise_xor(s, k) * rows, 16)
                r0 = pieces[k][1]
                w_s[pl.ds(at, rows), :] = got[where[k]][r0 : r0 + rows, :]
            wd_s[:wid, :] = d0[...]
            wd_s[wid:, :] = unfold(got[where[4]], down_at[1], wid, wid2)
            for h, t in enumerate((s, jnp.bitwise_xor(s, 2))):
                line = vec_r[pl.ds(8 + t, 1), :]
                b_s[:, h * wid : (h + 1) * wid] = jnp.broadcast_to(line[:, wave * wid : (wave + 1) * wid], (8, wid))

        up = dnn(nm_r[...], w_s[...]) + b_s[0:1, :]
        cdf = 0.5 * (1.0 + lax.erf(up * 0.7071067811865476))
        hid = (up * cdf).astype(BF16)
        slope = cdf + up * (jnp.exp(-0.5 * up * up) * 0.3989422804014327)
        gu = dnt(dy_r[...], wd_s[...]) * slope
        gl = gu.astype(BF16)
        hid_o[...] = hid
        gl_o[...] = gl
        acc_u[...] += dtn(nm_r[...], gl)
        acc_d[...] += dtn(dy_r[...], hid)
        ub[...] += sum8(gu)

        @pl.when(i == pl.num_programs(0) - 1)
        def _():
            for k, out in enumerate((keep, to1, to2, to3)):
                v = acc_u[pl.ds(pl.multiple_of(jnp.bitwise_xor(s, k) * rows, 16), rows), :].astype(BF16)
                h = wid if k >= 2 else 0
                out[:rows, :wid] = v[:, h : h + wid]
                out[:rows, wid:] = v[:, wid - h : wid2 - h]
            down = slice(rows, rows + half)
            keep[down, :wid] = acc_d[:half, :wid].astype(BF16)
            keep[down, wid:] = acc_d[half:, :wid].astype(BF16)
            to2[down, :wid] = acc_d[:half, wid:].astype(BF16)
            to2[down, wid:] = acc_d[half:, wid:].astype(BF16)
            w = w_s[...].astype(F32)
            rs[0:8, :] = col_sums(w * acc_u[...])
            rs[8:16, :] = col_sums(w * jnp.sum(ub[...], axis=0, keepdims=True))
            if table is not None:
                tbl[...] = t_r[...]
                line = lambda v: jnp.sum(v, axis=0, keepdims=True)
                ss = tbl[3:4, :] + line(rs[8:16, :])
                sg = tbl[2:3, :] + line(rs[0:8, :])
                tbl[2:3, :] = (sg - vec_r[3:4, :] * ss) / vec_r[2:3, :]
                tbl[3:4, :] = ss
                put_hidden_bias(tbl, s, wave, line(ub[...]))
                write_table((keep, to1, to2, to3), tbl, wid2)

    row = pl.BlockSpec((blk, width), lambda i: (i, 0))
    mid = pl.BlockSpec((blk, wid2), lambda i: (i, 0))

    def fixed(dims, at=(0, 0)):
        return pl.BlockSpec(dims, lambda i: at)

    more = 0 if table is None else 32
    extra = [] if table is None else [table]
    grads = [(rows + half + more, wid2), (rows + more, wid2)] * 2
    return pl.pallas_call(
        kern,
        grid=(4,),
        in_specs=[SMEM, row, row]
        + [fixed((wid, width), (wave, 0)), fixed((16, width))]
        + [fixed(t.shape) for t in srcs + extra],
        out_specs=[mid, mid, fixed((width, wid2)), fixed((wid2, width)), fixed((8, wid2)), fixed((16, width))]
        + [fixed(g) for g in grads],
        out_shape=[shape((n_tok, wid2), BF16)] * 2
        + [shape((width, wid2), BF16), shape((wid2, width), BF16), shape((8, wid2), F32), shape((16, width), F32)]
        + [shape(g, BF16) for g in grads],
        scratch_shapes=[
            pltpu.VMEM((8, wid2), F32),
            pltpu.VMEM((width, wid2), F32),
            pltpu.VMEM((width, wid2), F32),
            pltpu.VMEM((16, width), F32),
        ],
        cost_estimate=pl.CostEstimate(
            flops=8 * n_tok * width * wid2,
            bytes_accessed=10 * n_tok * width,
            transcendentals=2 * n_tok * wid2,
        ),
        name="mlp_wave",
    )(sc, nm, dy, down_own, vec, *srcs, *extra)


def attention(sc, na, dy, weights, vec, waves_of, seg_rows, cgrad):
    width = na.shape[1]
    length = cgrad.shape[0]
    rows, wq = weights[0].shape
    o_rows = weights[3].shape[0]
    core_rows = weights[1].shape[0]
    wh = wq - 2 * HEAD_DIM
    pairs = wh // 128
    chunk = 256
    n_chunk = length // chunk
    tail = length - FIRST_DOC
    blocks = []
    at = 0
    while at + chunk <= FIRST_DOC - FIRST_DOC % chunk - chunk:
        blocks.append((at, chunk, 0, at + chunk, False))
        at += chunk
    blocks.append((at, FIRST_DOC - at, 0, FIRST_DOC, False))
    blocks.append((FIRST_DOC, tail, FIRST_DOC, tail, True))

    def kern(sc_ref, na_r, dy_r, vec_r, cs_r, sr_r, cg_r, *refs):
        q0, cg_in, mg_in, o0 = refs[:4]
        o_s, gqs_s, cache, sums, wqs, wo = refs[4:10]
        q_s, do_s, dq_s, kz, zk, vz, zv, ek, ok, ev, ov, tc_r, ta_r, tb_r, sg_s = refs[10:]
        s = sc_ref[0]
        c = jnp.bitwise_and(s, 1)
        y = jnp.right_shift(s, 1)
        step = pl.program_id(0)

        @pl.when(step == 0)
        def _():
            for k in range(4):
                at = pl.multiple_of(jnp.bitwise_xor(s, k) * rows, 16)
                piece = (q0, cg_in, mg_in, mg_in)[k]
                r0 = (0, 0, 0, rows)[k]
                wqs[pl.ds(at, rows), :] = piece[r0 : r0 + rows, :]
            wo[pl.ds(pl.multiple_of(y * o_rows, 16), o_rows), :] = o0[...]
            wo[pl.ds(pl.multiple_of((1 - y) * o_rows, 16), o_rows), :] = unfold(mg_in, 2 * rows, o_rows, wq)
            sums[...] = jnp.zeros_like(sums)

        ek[...] = jnp.zeros_like(ek)
        ok[...] = jnp.zeros_like(ok)
        ev[...] = jnp.zeros_like(ev)
        ov[...] = jnp.zeros_like(ov)
        lane = lax.broadcasted_iota(jnp.int32, (1, 128), 1)
        low = lane < HEAD_DIM
        qb_line = jnp.broadcast_to(head_columns(vec_r[0:8, :], c)[6:7, :], (8, wh))
        sb_line = jnp.broadcast_to(vec_r[7:8, : 2 * HEAD_DIM], (8, 2 * HEAD_DIM))
        qb_all = jnp.concatenate([qb_line, sb_line], axis=1)[0:1, :]

        def spread(v, lo, hi):
            i = lax.broadcasted_iota(jnp.int32, (8, 128), 0)
            ln = lax.broadcasted_iota(jnp.int32, (8, 128), 1)
            ln = jnp.bitwise_and(ln, HEAD_DIM - 1)
            hit = (jnp.bitwise_and(ln, ROT // 2 - 1) == i) & (ln >= lo) & (ln < hi)
            return lax.dot_general(v, hit.astype(F32), (((0,), (0,)), ((), ())),
                                   precision=lax.Precision.HIGHEST, preferred_element_type=F32)

        still = jnp.bitwise_and(lax.broadcasted_iota(jnp.int32, (1, 128), 1), HEAD_DIM - 1) >= ROT
        cs = cs_r[0]
        tc_r[...] = spread(cs[0:8, :], 0, ROT) + jnp.where(still, 1.0, 0.0)
        ta_r[...] = spread(-cs[8:16, :], 0, ROT // 2)
        tb_r[...] = spread(cs[8:16, :], ROT // 2, ROT)
        last = jnp.broadcast_to(sr_r[0].astype(F32), (8, length))
        sg_s[...] = pltpu.roll(last, length - FIRST_DOC, 1)[:, : sg_s.shape[1]]
        seg_cols = sg_s[...].T[:tail, 0:1]

        def turn(v, c, a, b, sign):
            return v * c + sign * (pltpu.roll(v, 120, 1) * a + pltpu.roll(v, 8, 1) * b)

        def tabs(at, keys):
            c = tc_r[pl.ds(at, chunk), :]
            a = ta_r[pl.ds(at, chunk), :]
            b = tb_r[pl.ds(at, chunk), :]
            if keys:
                c = jnp.where(low, c, 1.0)
                a = jnp.where(low, a, 0.0)
                b = jnp.where(low, b, 0.0)
            return c, a, b

        @pl.loop(0, n_chunk)
        def _(n):
            at = pl.multiple_of(n * chunk, chunk)
            sl = pl.ds(at, chunk)
            lin = dnn(na_r[sl, :], wqs[...]) + qb_all
            tq = tabs(at, False)
            for p in range(pairs):
                v = turn(lin[:, p * 128 : (p + 1) * 128], *tq, 1.0)
                q_s[sl, p * 128 : (p + 1) * 128] = v.astype(BF16) * BF16(0.125)
            v = turn(lin[:, wh:], *tabs(at, True), 1.0)
            kv = v.astype(BF16)
            cache[sl, :] = kv
            vr = pltpu.roll(v, 64, 1)
            zero = jnp.zeros_like(v)
            kz[sl, :] = jnp.where(low, v, zero).astype(BF16)
            zv[sl, :] = jnp.where(low, zero, v).astype(BF16)
            zk[sl, :] = jnp.where(low, zero, vr).astype(BF16)
            vz[sl, :] = jnp.where(low, vr, zero).astype(BF16)
            do_s[sl, :] = dnt(dy_r[sl, :], wo[...]).astype(BF16)

        @pl.loop(0, pairs)
        def _(p):
            cols = pl.ds(pl.multiple_of(p * 128, 128), 128)
            for r0, rn, k0, kn, segs in blocks:
                q2 = q_s[r0 : r0 + rn, cols]
                do2 = do_s[r0 : r0 + rn, cols]
                dof = do2.astype(F32)
                keys = [ks[k0 : k0 + kn, :] for ks in (kz, zk)]
                vals = [vs[k0 : k0 + kn, :] for vs in (vz, zv)]
                free = 0 if segs else r0 // 128 * 128
                qi = lax.broadcasted_iota(jnp.int32, (rn, kn - free), 0) + r0
                ki = lax.broadcasted_iota(jnp.int32, (rn, kn - free), 1) + k0 + free
                allowed = ki <= qi
                if segs:
                    allowed = allowed & (seg_cols == sg_s[0:1, :tail])
                exps, invs = [], []
                for kk in keys:
                    logit = dnt(q2, kk)
                    edge = jnp.where(allowed, logit[:, free:], -1e30)
                    logit = jnp.concatenate([logit[:, :free], edge], axis=1) if free else edge
                    ex = jnp.exp(logit - jnp.max(logit, axis=-1, keepdims=True))
                    exps.append(ex)
                    invs.append(1.0 / jnp.sum(ex, axis=-1, keepdims=True))
                scale = jnp.where(low, invs[0], invs[1])
                dos = (dof * scale).astype(BF16)
                exb = [ex.astype(BF16) for ex in exps]
                o2 = (dnn(exb[0], vals[0]) + dnn(exb[1], vals[1])) * scale
                o_s[r0 : r0 + rn, cols] = o2.astype(BF16)
                dsb = []
                for e in range(2):
                    dp = dnt(dos, vals[e])
                    mean = jnp.sum(exps[e] * dp, axis=-1, keepdims=True) * invs[e]
                    dsb.append((exps[e] * (dp - mean)).astype(BF16))
                dq_s[r0 : r0 + rn, cols] = dnn(dsb[0], keys[0]) + dnn(dsb[1], keys[1])
                for e, (ak, av) in enumerate(((ek, ev), (ok, ov))):
                    ak[k0 : k0 + kn, :] += dtn(dsb[e], q2)
                    av[k0 : k0 + kn, :] += dtn(exb[e], dos)

        @pl.loop(0, n_chunk)
        def _(n):
            at = pl.multiple_of(n * chunk, chunk)
            sl = pl.ds(at, chunk)
            tq = tabs(at, False)
            for p in range(pairs):
                cc = slice(p * 128, (p + 1) * 128)
                v = turn(dq_s[sl, cc] * 0.125, *tq, -1.0)
                sums[:, cc] += sum8(v)
                gqs_s[sl, cc] = v.astype(BF16)
            gk = ek[sl, :] + pltpu.roll(ok[sl, :], 64, 1)
            gv = pltpu.roll(ev[sl, :], 64, 1) + ov[sl, :]
            v = jnp.where(low, gk, gv)
            v = v + jnp.where(step == 1, cg_r[sl, :].astype(F32), 0.0)
            v = turn(v, *tabs(at, True), -1.0)
            sums[:, wh:] += sum8(v)
            gqs_s[sl, wh:] = v.astype(BF16)

    def fixed(dims, at=(0, 0)):
        return pl.BlockSpec(dims, lambda i: at, pipeline_mode=pl.Buffered(1))

    def seq(lanes):
        return pl.BlockSpec((length, lanes), lambda i: (1 - i, 0))

    seg_w = (tail + 127) // 128 * 128
    total = na.shape[0]
    return pl.pallas_call(
        kern,
        grid=(2,),
        in_specs=[SMEM, seq(width), seq(width), fixed((16, width))]
        + [pl.BlockSpec((1, 16, length), lambda i: (1 - i, 0, 0)), pl.BlockSpec((1, 1, length), lambda i: (1 - i, 0, 0))]
        + [fixed((length, 128))]
        + [fixed((rows, wq)), fixed((rows, wq), (core_rows // rows - 1, 0)), fixed(weights[2].shape), fixed((o_rows, width))],
        out_specs=[seq(wh), seq(wq), fixed((length, 128)), fixed((8, wq)), fixed((width, wq)), fixed((wh, width))],
        out_shape=[
            shape((total, wh), BF16), shape((total, wq), BF16), shape((length, 128), BF16), shape((8, wq), F32),
            shape((width, wq), BF16), shape((wh, width), BF16),
        ],
        scratch_shapes=[
            pltpu.VMEM((length, wh), BF16),
            pltpu.VMEM((length, wh), BF16),
            pltpu.VMEM((length, wh), F32),
        ]
        + [pltpu.VMEM((length, 128), BF16)] * 4
        + [pltpu.VMEM((length, 128), F32)] * 7
        + [pltpu.VMEM((8, seg_w), F32)],
        cost_estimate=pl.CostEstimate(
            flops=4 * length * width * (wq + wh) + 24 * length * length * wh,
            bytes_accessed=12 * length * width,
            transcendentals=length * length * wh // 64,
        ),
        name="attention",
    )(sc, na, dy, vec, waves_of, seg_rows, cgrad, *weights)


def attn_terms(sc, na, dy, o_all, gqs_all, wqs, vec, sums, ob, ubs, rss):
    total, width = na.shape
    wq = gqs_all.shape[1]
    wh = o_all.shape[1]
    blk = total // 4
    o_rows = width // 4
    n_w = len(ubs)
    sizes = [(o_rows * 5 // 2, wq), (o_rows, wq)] * 2

    def kern(sc_ref, na_r, dy_r, o_r, g_r, w_r, vec_r, s0, ob_r, *refs):
        ub_r, rs_r = refs[:n_w], refs[n_w : 2 * n_w]
        keep, to1, to2, to3, tbl, acc_q, acc_o = refs[2 * n_w :]
        s = sc_ref[0]
        c = jnp.bitwise_and(s, 1)
        y = jnp.right_shift(s, 1)
        i = pl.program_id(0)
        pq = dtn(na_r[...], g_r[...])
        po = dtn(dy_r[...], o_r[...])

        @pl.when(i == 0)
        def _():
            acc_q[...] = pq
            acc_o[...] = po

        @pl.when(i > 0)
        def _():
            acc_q[...] += pq
            acc_o[...] += po

        @pl.when(i == pl.num_programs(0) - 1)
        def _():
            for k, out in enumerate((keep, to1, to2, to3)):
                at = pl.multiple_of(jnp.bitwise_xor(s, k) * o_rows, 16)
                out[:o_rows, :] = acc_q[pl.ds(at, o_rows), :].astype(BF16)
            got = acc_o[...].T
            lower = got[:o_rows, :].astype(BF16)
            upper = got[o_rows:, :].astype(BF16)
            fold(keep, o_rows, o_rows, jnp.where(y == 0, lower, upper), wq)
            fold(to2, o_rows, o_rows, jnp.where(y == 0, upper, lower), wq)
            line = lambda v: jnp.sum(v, axis=0, keepdims=True)
            w = w_r[...].astype(F32)
            both = s0[...]
            fs = line(col_sums(w * line(both)))
            fg = line(col_sums(w * acc_q[...]))
            ss = sum([line(r[8:16, :]) for r in rs_r])
            sg = sum([line(r[0:8, :]) for r in rs_r])
            tbl[...] = jnp.zeros_like(tbl)
            tbl[0:1, :] = (fg - vec_r[1:2, :] * fs) / vec_r[0:1, :]
            tbl[1:2, :] = fs
            tbl[2:3, :] = sg
            tbl[3:4, :] = ss
            tbl[4:5, :] = line(ob_r[...])
            qb8 = jnp.broadcast_to(line(both[:, :wh]), (8, wh))
            tbl[5:6, :] = head_spread(qb8, c, width)[0:1, :]
            tbl[6:7, : wq - wh] = line(both[:, wh:])
            for w_i, ref in enumerate(ub_r):
                put_hidden_bias(tbl, s, w_i, line(ref[...]))

    def fixed(dims):
        return pl.BlockSpec(dims, lambda i: (0, 0))

    row = pl.BlockSpec((blk, width), lambda i: (i, 0))
    return pl.pallas_call(
        kern,
        grid=(4,),
        in_specs=[SMEM, row, row, pl.BlockSpec((blk, wh), lambda i: (i, 0)), pl.BlockSpec((blk, wq), lambda i: (i, 0))]
        + [fixed((width, wq)), fixed((16, width)), fixed((8, wq)), fixed((8, width))]
        + [fixed((8, wq))] * n_w
        + [fixed((16, width))] * n_w,
        out_specs=[fixed(g) for g in sizes] + [fixed((16, width))],
        out_shape=[shape(g, BF16) for g in sizes] + [shape((16, width), F32)],
        scratch_shapes=[pltpu.VMEM((width, wq), F32), pltpu.VMEM((width, wh), F32)],
        cost_estimate=pl.CostEstimate(
            flops=2 * total * width * (wq + wh), bytes_accessed=4 * total * width, transcendentals=0
        ),
        name="attn_terms",
    )(sc, na, dy, o_all, gqs_all, wqs, vec, sums, ob, *ubs, *rss)


def outputs(which, hids, gls, ups, downs, o_all, gqs_all, wo, wqs, vec, last=()):
    total, wid2 = hids[0].shape
    width = wqs.shape[0]
    n_w = len(hids)
    blk = total // 8
    base = 4 * which

    def kern(*refs):
        h_r, g_r, u_r, d_r = (refs[k * n_w : (k + 1) * n_w] for k in range(4))
        o_r, q_r, wo_r, wq_r, vec_r = refs[4 * n_w : 4 * n_w + 5]
        out, hp = refs[-2:]
        br = dnn(o_r[...], wo_r[...])
        ea = dnt(q_r[...], wq_r[...])
        em = None
        for w in range(n_w):
            br = br + dnn(h_r[w][...], d_r[w][...])
            t = dnt(g_r[w][...], u_r[w][...])
            em = t if em is None else em + t
        h = ea * vec_r[0:1, :] + em * vec_r[2:3, :]
        if not last:
            out[...] = br.astype(BF16)
            hp[...] = h.astype(BF16)
        else:
            tok_r, dy_r, oi, hi = refs[4 * n_w + 5 : 4 * n_w + 9]
            x = tok_r[...].astype(F32)
            xhat, rstd = normalize(x)
            out[...] = (x + br + oi[...].astype(F32) + vec_r[4:5, :] + vec_r[5:6, :]).astype(BF16)
            h = h + hi[...].astype(F32)
            mean = jnp.mean(h, axis=-1, keepdims=True)
            cov = jnp.mean(h * xhat, axis=-1, keepdims=True)
            hp[...] = (dy_r[...].astype(F32) + rstd * (h - mean - xhat * cov)).astype(BF16)

    def rows(lanes):
        return pl.BlockSpec((blk, lanes), lambda i: (i + base, 0))

    def fixed(dims):
        return pl.BlockSpec(dims, lambda i: (0, 0))

    res = pl.BlockSpec((blk, width), lambda i: (i, 0))
    return pl.pallas_call(
        kern,
        grid=(4,),
        in_specs=[rows(wid2)] * (2 * n_w)
        + [fixed((width, wid2))] * n_w
        + [fixed((wid2, width))] * n_w
        + [rows(o_all.shape[1]), rows(gqs_all.shape[1]), fixed(wo.shape), fixed(wqs.shape), fixed((16, width))]
        + [res] * len(last),
        out_specs=[res, res],
        out_shape=[shape((total // 2, width), BF16)] * 2,
        cost_estimate=pl.CostEstimate(
            flops=total * width * (2 * n_w * wid2 + 900), bytes_accessed=12 * total * width, transcendentals=0
        ),
        name="outputs",
    )(*hids, *gls, *ups, *downs, o_all, gqs_all, wo, wqs, vec, *last)


def first_sum(sc, sets, rows, table, planes):
    lanes = sets[0][0].shape[1]
    n = sets[0][0].shape[0] - rows - table
    total = 2 * rows + n + table
    high = total // planes
    half = high // 2

    def kern(sc_ref, *refs):
        mine, away, tmp = refs[-3:]
        f = lambda ref, at, m: ref[at : at + m, :].astype(F32)
        for i in range(len(sets)):
            k_r, r1, r2, r3 = refs[4 * i : 4 * i + 4]
            tmp[:rows, :] = f(k_r, 0, rows) + f(r2, 0, rows)
            tmp[rows : 2 * rows, :] = f(r1, 0, rows) + f(r3, 0, rows)
            tmp[2 * rows : 2 * rows + n, :] = f(k_r, rows, n) + f(r2, rows, n)
            if table:
                near = f(k_r, rows + n, table) + f(r1, rows, table)
                tmp[2 * rows + n :, :] = near + (f(r2, rows + n, table) + f(r3, rows, table))
            for out, flip in ((mine, 0), (away, 1)):
                b = jnp.bitwise_xor(sc_ref[1], flip)
                for p in range(planes):
                    at = pl.multiple_of(p * high + b * half, 8)
                    out[i * planes + p] = tmp[pl.ds(at, half), :].astype(BF16)

    flat = [v for keep, got in sets for v in (keep, *got)]
    return pl.pallas_call(
        kern,
        in_specs=[SMEM] + [VM] * len(flat),
        out_specs=[VM, VM],
        out_shape=[shape((planes * len(sets), half, lanes), BF16)] * 2,
        scratch_shapes=[pltpu.VMEM((total, lanes), F32)],
        cost_estimate=pl.CostEstimate(flops=2 * total * lanes, bytes_accessed=8 * total * lanes, transcendentals=0),
        name="first_sum",
    )(sc, *flat)


def piece_row(sc_ref, n, h):
    b0, b1 = jnp.bitwise_xor(sc_ref[1], n & 1), jnp.bitwise_xor(sc_ref[2], n >> 1)
    return pl.multiple_of(b0 * (h // 2) + b1 * (h // 4), 8)


def early_grads(sc, pieces, width, ff, count):
    prow, wid2 = pieces[0].shape[1:]
    wid = wid2 // 2
    chunk = ff // 4
    part = width // 4
    n_p = len(pieces)

    def kern(sc_ref, *refs):
        ins = refs[:n_p]
        up, down, tmp = refs[-3:]
        s = sc_ref[0]
        for w in range(count):
            for n in range(n_p):
                at = piece_row(sc_ref, n, part)
                for p in range(4):
                    for h in range(2):
                        v = ins[n][4 * w + p, :, h * wid : (h + 1) * wid].astype(F32)
                        if p < 2:
                            t = jnp.bitwise_xor(s, p + 2 * h)
                            lanes = pl.multiple_of(t * chunk + w * wid, 256)
                            up[pl.ds(at, prow), pl.ds(lanes, wid)] = v
                        else:
                            tmp[pl.ds((2 * h + p - 2) * part + at, prow), :] = v
            down[w * wid : (w + 1) * wid, :] = tmp[...].T

    return pl.pallas_call(
        kern,
        in_specs=[SMEM] + [VM] * n_p,
        out_specs=[VM, VM],
        out_shape=[shape((part, ff), F32), shape((chunk, width), F32)],
        scratch_shapes=[pltpu.VMEM((width, wid), F32)],
        cost_estimate=pl.CostEstimate(flops=0, bytes_accessed=12 * part * ff, transcendentals=0),
        name="early_grads",
    )(sc, *pieces)


def late_grads(sc, pieces, width, ff, shared_w, prev):
    n_p = len(pieces)
    planes, prow, wid2 = pieces[0].shape
    wid = wid2 // 2
    chunk = ff // 4
    part = width // 4
    half = width // 2
    high = prow * n_p
    wave = WAVES - 1

    def kern(sc_ref, *refs):
        ins = refs[:n_p]
        up, down = refs[n_p + len(prev) : n_p + len(prev) + 2]
        lines = refs[n_p + len(prev) + 2 : -1]
        full = refs[-1]
        s = sc_ref[0]
        i = pl.program_id(0)

        @pl.when(i == 0)
        def _():
            for n in range(n_p):
                at = piece_row(sc_ref, n, high)
                for p in range(planes):
                    full[pl.ds(p * high + at, prow), :] = ins[n][p].astype(F32)
            d = 2 * part
            down[...] = jnp.concatenate([full[d : d + half, :wid], full[d : d + half, wid:]], axis=0).T
            at = d + half
            tab = jnp.concatenate([full[at : at + 16, :], full[at + 16 : at + 32, : width - wid2]], axis=1)
            left = pltpu.roll(tab, (width - s * part) % width, 1)
            for out, k in zip(lines, (0, 1, 2, 3, 4, 5, 4)):
                out[...] = left[k : k + 1, :part].reshape(part)
            few = shared_w // 4
            lines[7][...] = pltpu.roll(tab, (width - s * few) % width, 1)[6:7, :few].reshape(few)
            row = jnp.concatenate(
                [full[pl.ds(at + 8 + s, 1), :], full[pl.ds(at + 24 + s, 1), :][:, : width - wid2]], axis=1
            )
            lines[8][...] = row.reshape(width)

        for k in range(4):

            @pl.when(i == k)
            def _(k=k):
                r0, h = (k & 1) * part, (k >> 1) * wid
                up[...] = full[r0 : r0 + part, h : h + wid]

    line_shapes = [(part,)] * 7 + [(shared_w // 4,), (width,)]
    spec = pltpu.PrefetchScalarGridSpec(
        num_scalar_prefetch=1,
        grid=(4,),
        in_specs=[pl.BlockSpec(p.shape, lambda i, sc: (0, 0, 0)) for p in pieces] + [ANY] * len(prev),
        out_specs=[
            pl.BlockSpec((part, wid), lambda i, sc: (0, jnp.bitwise_xor(sc[0], i) * WAVES + wave)),
            pl.BlockSpec((wid, width), lambda i, sc: (wave, 0)),
        ]
        + [pl.BlockSpec(d, lambda i, sc: (0,)) for d in line_shapes],
        scratch_shapes=[pltpu.VMEM((planes * high, wid2), F32)],
    )
    return pl.pallas_call(
        kern,
        grid_spec=spec,
        out_shape=[shape((part, ff), F32), shape((chunk, width), F32)] + [shape(d, F32) for d in line_shapes],
        input_output_aliases={1 + n_p + i: i for i in range(len(prev))},
        cost_estimate=pl.CostEstimate(flops=0, bytes_accessed=4 * part * ff, transcendentals=0),
        name="late_grads",
    )(sc, *pieces, *prev)


def attn_grads(sc, pieces, width, shared_w):
    n_p = len(pieces)
    planes, prow, wq = pieces[0].shape
    part = width // 4
    wh = wq - shared_w
    high = prow * n_p

    def kern(sc_ref, *refs):
        ins = refs[:n_p]
        gq, gs, go, full = refs[n_p:]
        c = jnp.bitwise_and(sc_ref[0], 1)
        for n in range(n_p):
            at = piece_row(sc_ref, n, high)
            for p in range(planes):
                full[pl.ds(p * high + at, prow), :] = ins[n][p].astype(F32)
        gq[...] = head_spread(full[:part, :wh], c, width) + head_spread(full[part : 2 * part, :wh], 1 - c, width)
        gs[...] = full[:part, wh:] + full[part : 2 * part, wh:]
        go[...] = unfold(full, 2 * part, part, wq)

    return pl.pallas_call(
        kern,
        in_specs=[SMEM] + [VM] * n_p,
        out_specs=[VM] * 3,
        out_shape=[shape((part, width), F32), shape((part, shared_w), F32), shape((part, width), F32)],
        scratch_shapes=[pltpu.VMEM((planes * high, wq), F32)],
        cost_estimate=pl.CostEstimate(flops=0, bytes_accessed=12 * part * width, transcendentals=0),
        name="attn_grads",
    )(sc, *pieces)


def to_shard(value, k):
    return lax.ppermute(value, "shard", [(s, s ^ k) for s in range(4)])


def to_replica(value, k, count):
    return lax.ppermute(value, "replica", [(r, r ^ k) for r in range(count)])


def both_add(a, b):
    return (a.astype(F32) + b.astype(F32)).astype(BF16)


def after(value, *others):
    return lax.optimization_barrier((value,) + others)[0]


def send_terms(to1, to2, to3):
    return [to_shard(v, k) for v, k in ((to1, 1), (to2, 2), (to3, 3))]


def reduce_chain(half, away, count, rank):
    got = to_replica(away, 1, count)
    h = half.shape[1] // 2
    b = (rank >> 1) & 1

    def cut(which):
        f = lambda v: lax.dynamic_slice_in_dim(v, which * h, h, axis=1)
        return both_add(f(half), f(got))

    quarter, away = cut(b), cut(1 - b)
    quarter = both_add(quarter, to_replica(away, 2, count))
    k = 4
    while k < count:
        quarter = both_add(quarter, to_replica(quarter, k, count))
        k *= 2
    return [quarter] + [to_replica(quarter, k, count) for k in (1, 2, 3)]


def shards(
    tokens, segment_ids, positions, first_gain, first_shift, query_weight, query_bias, shared_weight,
    shared_bias, output_weight, output_bias, second_gain, second_shift, up_weight, up_bias, down_weight,
    down_bias, result_grad, shared_grad, *, replicas,
):
    width = tokens.shape[1]
    ff = up_weight.shape[1]
    part = width // 4
    sw = shared_weight.shape[1]
    s = lax.axis_index("shard")
    r = lax.axis_index("replica")
    sc = jnp.stack([s, r & 1, (r >> 1) & 1]).astype(jnp.int32)

    small = pack_small(
        sc,
        [first_gain, first_shift, second_gain, second_shift, output_bias, down_bias, query_bias],
        shared_bias, up_bias,
    )
    near = [small] + [to_shard(small, k) for k in (1, 2, 3)]
    own0, k1, k3, m2 = pack_first(sc, after(up_weight, small), down_weight)
    k1 = to_shard(k1, 1)
    m2 = to_shard(m2, 2)
    k3 = to_shard(k3, 3)
    core_out = pack_core(sc, after(up_weight, own0), query_weight, shared_weight)
    core_got = to_shard(core_out, 1)
    tok_in = to_shard(tokens, 1)
    dy_in = to_shard(result_grad, 1)
    ints_in = to_shard(jnp.concatenate([segment_ids, positions], axis=0), 1)

    prev, ob, vec = norm_pair(0, tokens, result_grad, near, [])
    prev, _, _ = norm_pair(1, tok_in, dy_in, near, prev)
    nm, na, dy = prev
    own1, own2, ownq, y1, y2, ya = pack_rest(
        sc, up_weight, down_weight, query_weight, shared_weight, output_weight, after(core_got, vec)
    )

    pos = jnp.concatenate([positions, ints_in[1:]], axis=0)
    inv = 10000.0 ** (-2.0 * jnp.arange(ROT // 2, dtype=F32) / ROT)
    ang = pos.astype(F32)[:, None, :] * inv[None, :, None]
    angles = jnp.concatenate([jnp.cos(ang), jnp.sin(ang)], axis=1)
    segs = jnp.stack([segment_ids, ints_in[:1]])

    rows = part

    def wave(w, pieces, down_at, table=None):
        return mlp_wave(w, sc, nm, dy, pieces, down_at, down_weight, vec, table)

    m1 = to_shard(y1, 2)
    hid0, gl0, wu0, wd0, ub0, rs0, keep0, *send0 = wave(0, [(own0, 0), (k1, 0), (m2, 0), (k3, 0)], (m2, rows))
    ma = to_shard(after(ya, m1), 2)
    hid1, gl1, wu1, wd1, ub1, rs1, keep1, *send1 = wave(
        1, [(own1, 0), (core_got, 0), (m1, 0), (m1, rows)], (m1, 2 * rows)
    )
    m2b = to_shard(after(y2, ma), 2)
    got0 = send_terms(*[after(v, ma) for v in send0])
    got1 = send_terms(*[after(v, ma) for v in send1])
    o_all, gqs_all, cache, sums, wqs, wo = attention(
        sc, na, dy, (ownq, core_got, ma, output_weight), vec, angles, segs, shared_grad
    )
    keepa, ta1, ta2, ta3, table = attn_terms(
        sc, na, dy, o_all, gqs_all, wqs, vec, sums, ob, (ub0, ub1), (rs0, rs1)
    )
    hid2, gl2, wu2, wd2, _, _, keep2, *send2 = wave(
        2, [(own2, 0), (core_got, 2 * rows), (m2b, 0), (m2b, rows)], (m2b, 2 * rows), table
    )

    def chain(sets, table_rows, planes):
        return reduce_chain(*first_sum(sc, sets, part, table_rows, planes), replicas, r)

    p01 = chain([(keep0, got0), (keep1, got1)], 0, 4)
    pa = chain([(keepa, send_terms(ta1, ta2, ta3))], 0, 21)
    p2 = chain([(keep2, send_terms(*send2))], 32, 25)

    hids, gls, wus, wds = (hid0, hid1, hid2), (gl0, gl1, gl2), (wu0, wu1, wu2), (wd0, wd1, wd2)

    def outs(which, last=()):
        return outputs(which, hids, gls, wus, wds, o_all, gqs_all, wo, wqs, vec, last)

    out_p, h_p = outs(1)
    out_in = to_shard(out_p, 1)
    h_in = to_shard(h_p, 1)
    block_output, tokens_grad = outs(0, (tokens, result_grad, out_in, h_in))

    grads = early_grads(sc, p01, width, ff, WAVES - 1)
    grad_q, grad_s, grad_o = attn_grads(sc, pa, width, sw)
    out = late_grads(sc, p2, width, ff, sw, grads)
    grad_up, grad_down, fg, fs, sg, ss, ob_g, qb_g, db_g, sb_g, ub_g = out
    return (
        block_output, cache, tokens_grad,
        fg, fs, grad_q, qb_g, grad_s, sb_g, grad_o, ob_g,
        sg, ss, grad_up, ub_g, grad_down, db_g,
    )


def solution(mesh):
    both = P(("replica", "shard"), None)
    one, two = P("shard"), P("shard", None)

    def body(*args):
        return shards(*args, replicas=mesh.shape["replica"])

    return jax.shard_map(
        body,
        mesh=mesh,
        in_specs=(both, both, both, one, one, two, one, two, one, two, one, one, one, two, one, two, one, both, both),
        out_specs=(both, both, both, one, one, two, one, two, one, two, one, one, one, two, one, two, one),
        check_vma=False,
    )
```

```python
import jax
import jax.numpy as jnp
from jax import lax
from jax.experimental import pallas as pl
from jax.experimental.pallas import tpu as pltpu
from jax.sharding import PartitionSpec as P


HEAD_DIM = 64
ROT = 16
FIRST_DOC = 800
EPS = 1e-05
F32 = jnp.float32
BF16 = jnp.bfloat16
WAVES = 3


def dnn(a, b):
    return lax.dot_general(a, b, (((1,), (0,)), ((), ())), preferred_element_type=F32)


def dnt(a, b):
    return lax.dot_general(a, b, (((1,), (1,)), ((), ())), preferred_element_type=F32)


def dtn(a, b):
    return lax.dot_general(a, b, (((0,), (0,)), ((), ())), preferred_element_type=F32)


def sum8(v):
    return jnp.sum(v.reshape(-1, 8, v.shape[1]), axis=0)


def normalize(x):
    centre = x - jnp.mean(x, axis=-1, keepdims=True)
    var = jnp.mean(centre * centre, axis=-1, keepdims=True)
    rstd = lax.rsqrt(var + EPS)
    return centre * rstd, rstd


ANY = pl.BlockSpec(memory_space=pl.ANY)
SMEM = pl.BlockSpec(memory_space=pltpu.SMEM)
VM = pl.BlockSpec(memory_space=pltpu.VMEM)


def shape(dims, kind):
    return jax.ShapeDtypeStruct(dims, kind)


def head_columns(w, c):
    width = w.shape[1]
    part = width // 4
    lane = lax.broadcasted_iota(jnp.int32, (1, width), 1)
    r = pltpu.roll(w, (width - c * part) % width, 1)
    return jnp.where(lane < part, r, pltpu.roll(r, width - part, 1))[:, : 2 * part]


def head_spread(x, c, width):
    part = width // 4
    lane = lax.broadcasted_iota(jnp.int32, (1, width), 1)
    v = jnp.concatenate([x, jnp.zeros_like(x)], axis=1)
    zero = jnp.zeros_like(v)
    u = jnp.where(lane < part, v, zero)
    u = u + pltpu.roll(jnp.where((lane >= part) & (lane < 2 * part), v, zero), part, 1)
    return pltpu.roll(u, c * part, 1)


def up_piece(w_ref, s, k, w, chunk):
    wid = chunk // WAVES
    t = jnp.bitwise_xor(s, k)
    a = pl.multiple_of(t * chunk + w * wid, 256)
    b = pl.multiple_of(jnp.bitwise_xor(t, 2) * chunk + w * wid, 256)
    return jnp.concatenate([w_ref[:, pl.ds(a, wid)], w_ref[:, pl.ds(b, wid)]], axis=1)


def fold(out, at, rows, v, lanes):
    h = rows // 2
    out[at : at + rows, :] = v[:, :lanes]
    out[at + rows : at + rows + h, : lanes // 2] = v[:h, lanes:]
    out[at + rows : at + rows + h, lanes // 2 :] = v[h:, lanes:]


def unfold(ref, at, rows, lanes):
    h = rows // 2
    top = ref[at : at + rows, :]
    low = ref[at + rows : at + rows + h, :]
    return jnp.concatenate(
        [top, jnp.concatenate([low[:, : lanes // 2], low[:, lanes // 2 :]], axis=0)], axis=1
    )


def pack_small(sc, seven, shared_bias, up_bias):
    part = seven[0].shape[0]
    width = up_bias.shape[0]
    few = shared_bias.shape[0]

    def kern(sc_ref, *refs):
        out, tmp = refs[-2:]
        s = sc_ref[0]
        tmp[...] = jnp.zeros_like(tmp)
        for i in range(7):
            tmp[i : i + 1, :part] = refs[i][...].astype(F32).reshape(1, part)
        tmp[:7, :] = pltpu.roll(tmp[0:8, :], s * part, 1)[:7]
        tmp[7:8, :few] = refs[7][...].astype(F32).reshape(1, few)
        tmp[7:8, :] = pltpu.roll(tmp[0:8, :], s * few, 1)[7:8]
        tmp[pl.ds(8 + s, 1), :] = refs[8][...].astype(F32).reshape(1, width)
        out[...] = tmp[...].astype(BF16)

    return pl.pallas_call(
        kern,
        in_specs=[SMEM] + [VM] * 9,
        out_specs=VM,
        out_shape=shape((16, width), BF16),
        scratch_shapes=[pltpu.VMEM((16, width), F32)],
        name="pack_small",
    )(sc, *seven, shared_bias, up_bias)


def pack_first(sc, up_weight, down_weight):
    rows, ff = up_weight.shape
    chunk, width = down_weight.shape
    wid = chunk // WAVES

    def kern(sc_ref, w_ref, d_ref, own, k1, k3, m2):
        s = sc_ref[0]
        own[...] = up_piece(w_ref, s, 0, 0, chunk)
        k1[...] = up_piece(w_ref, s, 1, 0, chunk)
        k3[...] = up_piece(w_ref, s, 3, 0, chunk)
        m2[:rows, :] = up_piece(w_ref, s, 2, 0, chunk)
        fold(m2, rows, wid, d_ref[...], 2 * wid)

    return pl.pallas_call(
        kern,
        grid=(1,),
        in_specs=[SMEM, pl.BlockSpec((rows, ff), lambda i: (0, 0)), pl.BlockSpec((wid, width), lambda i: (0, 0))],
        out_specs=[pl.BlockSpec((rows, 2 * wid), lambda i: (0, 0))] * 3
        + [pl.BlockSpec((rows + wid * 3 // 2, 2 * wid), lambda i: (0, 0))],
        out_shape=[shape((rows, 2 * wid), BF16)] * 3 + [shape((rows + wid * 3 // 2, 2 * wid), BF16)],
        name="pack_first",
    )(sc, up_weight, down_weight)


def pack_core(sc, up_weight, query_weight, shared_weight):
    rows, ff = up_weight.shape
    width = query_weight.shape[1]
    chunk = ff // 4
    wid = chunk // WAVES
    n = 2 * (WAVES - 1)
    half = width // 2

    def kern(sc_ref, w_ref, q_ref, s_ref, out):
        s = sc_ref[0]
        c = jnp.bitwise_and(s, 1)
        for w in range(1, WAVES):
            for i, k in enumerate((1, 3)):
                at = (2 * (w - 1) + i) * rows
                out[at : at + rows, :] = up_piece(w_ref, s, k, w, chunk)
        out[n * rows :, :half] = head_columns(q_ref[...].astype(F32), 1 - c).astype(BF16)
        out[n * rows :, half:] = s_ref[...]

    return pl.pallas_call(
        kern,
        in_specs=[SMEM, VM, VM, VM],
        out_specs=VM,
        out_shape=shape(((n + 1) * rows, 2 * wid), BF16),
        name="pack_core",
    )(sc, up_weight, query_weight, shared_weight)


def pack_rest(sc, up_weight, down_weight, query_weight, shared_weight, output_weight, got):
    rows, _ = up_weight.shape
    chunk, width = down_weight.shape
    wid = chunk // WAVES
    lanes = 2 * wid
    n = 2 * (WAVES - 1)
    half = width // 2

    def kern(sc_ref, w_ref, d_ref, q_ref, s_ref, o_ref, g_ref, own1, own2, ownq, y1, y2, ya):
        s = sc_ref[0]
        c = jnp.bitwise_and(s, 1)
        for w, own, out in ((1, own1, y1), (2, own2, y2)):
            own[...] = up_piece(w_ref, s, 0, w, chunk)
            out[:rows, :] = up_piece(w_ref, s, 2, w, chunk)
            at = (2 * (w - 1) + 1) * rows
            out[rows : 2 * rows, :] = g_ref[at : at + rows, :]
            fold(out, 2 * rows, wid, d_ref[w * wid : (w + 1) * wid, :], lanes)
        mine = head_columns(q_ref[...].astype(F32), c).astype(BF16)
        for out in (ownq, ya):
            out[:rows, :half] = mine
            out[:rows, half:] = s_ref[...]
        ya[rows : 2 * rows, :] = g_ref[n * rows :, :]
        fold(ya, 2 * rows, rows, o_ref[...], lanes)

    msg = 2 * rows + wid * 3 // 2
    msg_a = 2 * rows + rows * 3 // 2
    return pl.pallas_call(
        kern,
        in_specs=[SMEM] + [VM] * 6,
        out_specs=[VM] * 6,
        out_shape=[shape((rows, lanes), BF16)] * 3
        + [shape((msg, lanes), BF16)] * 2
        + [shape((msg_a, lanes), BF16)],
        name="pack_rest",
    )(sc, up_weight, down_weight, query_weight, shared_weight, output_weight, got)


def norm_pair(which, tok, dy, near, prev):
    n_tok, width = tok.shape
    n_near = len(near)
    blk = n_tok // 2
    base = 2 * which

    def kern(tok_ref, dy_ref, *refs):
        nm, na, dyc, ob, vec_ref = refs[n_near + len(prev) :]
        vec_ref[...] = sum([r[...].astype(F32) for r in refs[1:n_near]], refs[0][...].astype(F32))
        xhat, _ = normalize(tok_ref[...].astype(F32))
        a = (xhat * vec_ref[0:1, :] + vec_ref[1:2, :]).astype(BF16)
        m = (xhat * vec_ref[2:3, :] + vec_ref[3:4, :]).astype(BF16)
        g = dy_ref[...]
        na[...] = a
        nm[...] = m
        dyc[...] = g

        @pl.when(pl.program_id(0) == 0)
        def _():
            ob[...] = jnp.zeros_like(ob)

        ob[...] += sum8(g.astype(F32))

    row = pl.BlockSpec((blk, width), lambda i: (i + base, 0))
    src = pl.BlockSpec((blk, width), lambda i: (i, 0))
    whole = pl.BlockSpec((8, width), lambda i: (0, 0))
    small = pl.BlockSpec((16, width), lambda i: (0, 0))
    res = pl.pallas_call(
        kern,
        grid=(2,),
        in_specs=[src, src] + [small] * n_near + [ANY] * len(prev),
        out_specs=[row, row, row, whole, small],
        out_shape=[shape((2 * n_tok, width), BF16)] * 3
        + [shape((8, width), F32), shape((16, width), F32)],
        input_output_aliases={2 + n_near + i: i for i in range(len(prev))},
        cost_estimate=pl.CostEstimate(
            flops=20 * n_tok * width, bytes_accessed=16 * n_tok * width, transcendentals=0
        ),
        name="norm_pair",
    )(tok, dy, *near, *prev)
    return res[:3], res[3], res[4]


MOVES = [(k, j) for k in range(4) for j in range(2)]


def message_rows(k, sizes):
    first, more, table = sizes
    return (first + (more if k in (0, 2) else 0) + table) // 2


def put_half(out, at, src, rows, high, b):
    half = high // 2
    for p in range(rows // high):
        v = src(pl.multiple_of(p * high + b * half, 8), half)
        out[at + p * half : at + (p + 1) * half, :] = v.astype(BF16)


def fold_table(dst, tbl, lanes):
    width = tbl.shape[1]
    dst[:16, :] = tbl[:, :lanes]
    dst[16:, : width - lanes] = tbl[:, lanes:]
    dst[16:, width - lanes :] = jnp.zeros((16, 2 * lanes - width), F32)


def put_hidden_bias(tbl, s, w, u):
    wd = u.shape[1] // 2
    tbl[pl.ds(8 + s, 1), w * wd : (w + 1) * wd] = u[:, :wd]
    tbl[pl.ds(8 + jnp.bitwise_xor(s, 2), 1), w * wd : (w + 1) * wd] = u[:, wd:]


def col_sums(v):
    part = v[:, :128]
    for i in range(128, v.shape[1], 128):
        part = part + v[:, i : i + 128]
    return sum8(part.T)


def mlp_wave(wave, sc, nm, dy, pieces, down_at, down_own, vec, high, slot=None, prev=(), table=None):
    n_tok, width = nm.shape
    blk = n_tok // 4
    rows = width // 4
    chunk = down_own.shape[0]
    wid = chunk // WAVES
    wid2 = 2 * wid
    half = width // 2
    srcs = []
    for arr, _ in list(pieces) + [down_at]:
        if not any(arr is t for t in srcs):
            srcs.append(arr)
    where = [next(i for i, t in enumerate(srcs) if t is arr) for arr, _ in list(pieces) + [down_at]]
    n_src = len(srcs)

    def kern(sc_ref, nm_r, dy_r, d0, vec_r, *refs):
        got, refs = refs[:n_src], refs[n_src:]
        if table is not None:
            t_r, refs = refs[0], refs[1:]
        refs = refs[len(prev) :]
        hid_o, gl_o, w_s, wd_s, ub, rs = refs[:6]
        b_s, acc_u, acc_d, tbl, t_f = refs[-5:]
        outs = refs[6:-5]
        i = pl.program_id(0)
        s = sc_ref[0]

        @pl.when(i == 0)
        def _():
            acc_u[...] = jnp.zeros_like(acc_u)
            acc_d[...] = jnp.zeros_like(acc_d)
            ub[...] = jnp.zeros_like(ub)
            for k in range(4):
                at = pl.multiple_of(jnp.bitwise_xor(s, k) * rows, 16)
                r0 = pieces[k][1]
                w_s[pl.ds(at, rows), :] = got[where[k]][r0 : r0 + rows, :]
            wd_s[:wid, :] = d0[...]
            wd_s[wid:, :] = unfold(got[where[4]], down_at[1], wid, wid2)
            for h, t in enumerate((s, jnp.bitwise_xor(s, 2))):
                line = vec_r[pl.ds(8 + t, 1), :]
                b_s[:, h * wid : (h + 1) * wid] = jnp.broadcast_to(line[:, wave * wid : (wave + 1) * wid], (8, wid))

        up = dnn(nm_r[...], w_s[...]) + b_s[0:1, :]
        cdf = 0.5 * (1.0 + lax.erf(up * 0.7071067811865476))
        hid = (up * cdf).astype(BF16)
        slope = cdf + up * (jnp.exp(-0.5 * up * up) * 0.3989422804014327)
        gu = dnt(dy_r[...], wd_s[...]) * slope
        gl = gu.astype(BF16)
        hid_o[...] = hid
        gl_o[...] = gl
        acc_u[...] += dtn(nm_r[...], gl)
        acc_d[...] += dtn(dy_r[...], hid)
        ub[...] += sum8(gu)

        @pl.when(i == pl.num_programs(0) - 1)
        def _():
            w = w_s[...].astype(F32)
            rs[0:8, :] = col_sums(w * acc_u[...])
            rs[8:16, :] = col_sums(w * jnp.sum(ub[...], axis=0, keepdims=True))
            if table is not None:
                tbl[...] = t_r[...]
                line = lambda v: jnp.sum(v, axis=0, keepdims=True)
                ss = tbl[3:4, :] + line(rs[8:16, :])
                sg = tbl[2:3, :] + line(rs[0:8, :])
                tbl[2:3, :] = (sg - vec_r[3:4, :] * ss) / vec_r[2:3, :]
                tbl[3:4, :] = ss
                put_hidden_bias(tbl, s, wave, line(ub[...]))
                fold_table(t_f, tbl, wid2)
            for (k, j), out in zip(MOVES, outs):
                b = jnp.bitwise_xor(sc_ref[1], j)
                r0 = jnp.bitwise_xor(s, k) * rows
                h = wid if k >= 2 else 0

                def up_rows(at, n, r0=r0, h=h):
                    v = acc_u[pl.ds(pl.multiple_of(r0 + at, 8), n), :]
                    return jnp.concatenate([v[:, h : h + wid], v[:, wid - h : wid2 - h]], axis=1)

                def down_rows(at, n, h=h):
                    low = acc_d[pl.ds(pl.multiple_of(at, 8), n), :]
                    top = acc_d[pl.ds(pl.multiple_of(half + at, 8), n), :]
                    return jnp.concatenate([low[:, h : h + wid], top[:, h : h + wid]], axis=1)

                put_half(out, 0, up_rows, rows, high, b)
                end = rows // 2
                if k in (0, 2):
                    put_half(out, end, down_rows, half, high, b)
                    end += half // 2
                if table is not None:
                    put_half(out, end, lambda at, n: t_f[pl.ds(at, n), :], 32, 32, b)

    row = pl.BlockSpec((blk, width), lambda i: (i, 0))
    mid = pl.BlockSpec((blk, wid2), lambda i: (i, 0))

    def fixed(dims, at=(0, 0)):
        return pl.BlockSpec(dims, lambda i: at)

    extra = [] if table is None else [table]
    sizes = (rows, half, 0 if table is None else 32)
    n_out = [message_rows(k, sizes) for k, _ in MOVES]
    at = 0 if slot is None else slot
    times = 1 if slot is None else 2
    return pl.pallas_call(
        kern,
        grid=(4,),
        in_specs=[SMEM, row, row]
        + [fixed((wid, width), (wave, 0)), fixed((16, width))]
        + [fixed(t.shape) for t in srcs + extra]
        + [ANY] * len(prev),
        out_specs=[mid, mid, fixed((width, wid2)), fixed((wid2, width)), fixed((8, wid2)), fixed((16, width))]
        + [fixed((n, wid2), (at, 0)) for n in n_out],
        out_shape=[shape((n_tok, wid2), BF16)] * 2
        + [shape((width, wid2), BF16), shape((wid2, width), BF16), shape((8, wid2), F32), shape((16, width), F32)]
        + [shape((times * n, wid2), BF16) for n in n_out],
        scratch_shapes=[
            pltpu.VMEM((8, wid2), F32),
            pltpu.VMEM((width, wid2), F32),
            pltpu.VMEM((width, wid2), F32),
            pltpu.VMEM((16, width), F32),
            pltpu.VMEM((32, wid2), F32),
        ],
        input_output_aliases={5 + n_src + len(extra) + i: 6 + i for i in range(len(prev))},
        cost_estimate=pl.CostEstimate(
            flops=8 * n_tok * width * wid2,
            bytes_accessed=10 * n_tok * width,
            transcendentals=2 * n_tok * wid2,
        ),
        name="mlp_wave",
    )(sc, nm, dy, down_own, vec, *srcs, *extra, *prev)


def attention(sc, na, dy, weights, vec, waves_of, seg_rows, cgrad):
    width = na.shape[1]
    length = cgrad.shape[0]
    rows, wq = weights[0].shape
    o_rows = weights[3].shape[0]
    core_rows = weights[1].shape[0]
    wh = wq - 2 * HEAD_DIM
    pairs = wh // 128
    chunk = 256
    n_chunk = length // chunk
    tail = length - FIRST_DOC
    blocks = []
    at = 0
    while at + chunk <= FIRST_DOC - FIRST_DOC % chunk - chunk:
        blocks.append((at, chunk, 0, at + chunk, False))
        at += chunk
    blocks.append((at, FIRST_DOC - at, 0, FIRST_DOC, False))
    k_last = FIRST_DOC // 128 * 128
    blocks.append((FIRST_DOC, tail, k_last, length - k_last, True))

    def kern(sc_ref, na_r, dy_r, vec_r, cs_r, sr_r, cg_r, *refs):
        q0, cg_in, mg_in, o0 = refs[:4]
        o_s, gqs_s, cache, sums, wqs, wo = refs[4:10]
        q_s, do_s, dq_s, kz, zk, vz, zv, ek, ok, ev, ov, tc_r, ta_r, tb_r, sg_s = refs[10:]
        s = sc_ref[0]
        c = jnp.bitwise_and(s, 1)
        y = jnp.right_shift(s, 1)
        step = pl.program_id(0)

        @pl.when(step == 0)
        def _():
            for k in range(4):
                at = pl.multiple_of(jnp.bitwise_xor(s, k) * rows, 16)
                piece = (q0, cg_in, mg_in, mg_in)[k]
                r0 = (0, 0, 0, rows)[k]
                wqs[pl.ds(at, rows), :] = piece[r0 : r0 + rows, :]
            wo[pl.ds(pl.multiple_of(y * o_rows, 16), o_rows), :] = o0[...]
            wo[pl.ds(pl.multiple_of((1 - y) * o_rows, 16), o_rows), :] = unfold(mg_in, 2 * rows, o_rows, wq)
            sums[...] = jnp.zeros_like(sums)

        ek[...] = jnp.zeros_like(ek)
        ok[...] = jnp.zeros_like(ok)
        ev[...] = jnp.zeros_like(ev)
        ov[...] = jnp.zeros_like(ov)
        lane = lax.broadcasted_iota(jnp.int32, (1, 128), 1)
        low = lane < HEAD_DIM
        qb_line = jnp.broadcast_to(head_columns(vec_r[0:8, :], c)[6:7, :], (8, wh))
        sb_line = jnp.broadcast_to(vec_r[7:8, : 2 * HEAD_DIM], (8, 2 * HEAD_DIM))
        qb_all = jnp.concatenate([qb_line, sb_line], axis=1)[0:1, :]

        def spread(v, lo, hi):
            i = lax.broadcasted_iota(jnp.int32, (8, 128), 0)
            ln = lax.broadcasted_iota(jnp.int32, (8, 128), 1)
            ln = jnp.bitwise_and(ln, HEAD_DIM - 1)
            hit = (jnp.bitwise_and(ln, ROT // 2 - 1) == i) & (ln >= lo) & (ln < hi)
            return lax.dot_general(v, hit.astype(F32), (((0,), (0,)), ((), ())),
                                   precision=lax.Precision.HIGHEST, preferred_element_type=F32)

        still = jnp.bitwise_and(lax.broadcasted_iota(jnp.int32, (1, 128), 1), HEAD_DIM - 1) >= ROT
        cs = cs_r[0]
        tc_r[...] = spread(cs[0:8, :], 0, ROT) + jnp.where(still, 1.0, 0.0)
        ta_r[...] = spread(-cs[8:16, :], 0, ROT // 2)
        tb_r[...] = spread(cs[8:16, :], ROT // 2, ROT)
        sg_s[...] = jnp.broadcast_to(sr_r[0].astype(F32), (8, length))[:, k_last:]
        seg_cols = sg_s[...].T[FIRST_DOC - k_last :, 0:1]

        def turn(v, c, a, b, sign):
            return v * c + sign * (pltpu.roll(v, 120, 1) * a + pltpu.roll(v, 8, 1) * b)

        def tabs(at, keys):
            c = tc_r[pl.ds(at, chunk), :]
            a = ta_r[pl.ds(at, chunk), :]
            b = tb_r[pl.ds(at, chunk), :]
            if keys:
                c = jnp.where(low, c, 1.0)
                a = jnp.where(low, a, 0.0)
                b = jnp.where(low, b, 0.0)
            return c, a, b

        @pl.loop(0, n_chunk)
        def _(n):
            at = pl.multiple_of(n * chunk, chunk)
            sl = pl.ds(at, chunk)
            lin = dnn(na_r[sl, :], wqs[...]) + qb_all
            tq = tabs(at, False)
            for p in range(pairs):
                v = turn(lin[:, p * 128 : (p + 1) * 128], *tq, 1.0)
                q_s[sl, p * 128 : (p + 1) * 128] = v.astype(BF16) * BF16(0.125)
            v = turn(lin[:, wh:], *tabs(at, True), 1.0)
            kv = v.astype(BF16)
            cache[sl, :] = kv
            vr = pltpu.roll(v, 64, 1)
            zero = jnp.zeros_like(v)
            kz[sl, :] = jnp.where(low, v, zero).astype(BF16)
            zv[sl, :] = jnp.where(low, zero, v).astype(BF16)
            zk[sl, :] = jnp.where(low, zero, vr).astype(BF16)
            vz[sl, :] = jnp.where(low, vr, zero).astype(BF16)
            do_s[sl, :] = dnt(dy_r[sl, :], wo[...]).astype(BF16)

        @pl.loop(0, pairs)
        def _(p):
            cols = pl.ds(pl.multiple_of(p * 128, 128), 128)
            for r0, rn, k0, kn, segs in blocks:
                q2 = q_s[r0 : r0 + rn, cols]
                do2 = do_s[r0 : r0 + rn, cols]
                dof = do2.astype(F32)
                keys = [ks[k0 : k0 + kn, :] for ks in (kz, zk)]
                vals = [vs[k0 : k0 + kn, :] for vs in (vz, zv)]
                free = 0 if segs else r0 // 128 * 128
                qi = lax.broadcasted_iota(jnp.int32, (rn, kn - free), 0) + r0
                ki = lax.broadcasted_iota(jnp.int32, (rn, kn - free), 1) + k0 + free
                allowed = ki <= qi
                if segs:
                    allowed = allowed & (seg_cols == sg_s[0:1, :])
                exps, invs = [], []
                for kk in keys:
                    logit = dnt(q2, kk)
                    edge = jnp.where(allowed, logit[:, free:], -1e30)
                    logit = jnp.concatenate([logit[:, :free], edge], axis=1) if free else edge
                    ex = jnp.exp(logit - jnp.max(logit, axis=-1, keepdims=True))
                    exps.append(ex)
                    invs.append(1.0 / jnp.sum(ex, axis=-1, keepdims=True))
                scale = jnp.where(low, invs[0], invs[1])
                dos = (dof * scale).astype(BF16)
                exb = [ex.astype(BF16) for ex in exps]
                o2 = (dnn(exb[0], vals[0]) + dnn(exb[1], vals[1])) * scale
                o_s[r0 : r0 + rn, cols] = o2.astype(BF16)
                prod = o2 * dof
                m0 = jnp.sum(jnp.where(low, prod, 0.0), axis=-1, keepdims=True)
                m1 = jnp.sum(jnp.where(low, 0.0, prod), axis=-1, keepdims=True)
                dsb = []
                for e, mm in enumerate((m0, m1)):
                    dp = dnt(dos, vals[e])
                    dsb.append((exps[e] * (dp - mm * invs[e])).astype(BF16))
                dq_s[r0 : r0 + rn, cols] = dnn(dsb[0], keys[0]) + dnn(dsb[1], keys[1])
                for e, (ak, av) in enumerate(((ek, ev), (ok, ov))):
                    ak[:, k0 : k0 + kn] += dtn(q2, dsb[e])
                    av[:, k0 : k0 + kn] += dtn(dos, exb[e])

        @pl.loop(0, n_chunk)
        def _(n):
            at = pl.multiple_of(n * chunk, chunk)
            sl = pl.ds(at, chunk)
            tq = tabs(at, False)
            for p in range(pairs):
                cc = slice(p * 128, (p + 1) * 128)
                v = turn(dq_s[sl, cc] * 0.125, *tq, -1.0)
                sums[:, cc] += sum8(v)
                gqs_s[sl, cc] = v.astype(BF16)
            v = jnp.concatenate([ek[:64, sl] + ok[64:, sl], ev[:64, sl] + ov[64:, sl]], axis=0).T
            v = v + jnp.where(step == 1, cg_r[sl, :].astype(F32), 0.0)
            v = turn(v, *tabs(at, True), -1.0)
            sums[:, wh:] += sum8(v)
            gqs_s[sl, wh:] = v.astype(BF16)

    def fixed(dims, at=(0, 0)):
        return pl.BlockSpec(dims, lambda i: at, pipeline_mode=pl.Buffered(1))

    def seq(lanes):
        return pl.BlockSpec((length, lanes), lambda i: (1 - i, 0))

    seg_w = length - k_last
    total = na.shape[0]
    return pl.pallas_call(
        kern,
        grid=(2,),
        in_specs=[SMEM, seq(width), seq(width), fixed((16, width))]
        + [pl.BlockSpec((1, 16, length), lambda i: (1 - i, 0, 0)), pl.BlockSpec((1, 1, length), lambda i: (1 - i, 0, 0))]
        + [fixed((length, 128))]
        + [fixed((rows, wq)), fixed((rows, wq), (core_rows // rows - 1, 0)), fixed(weights[2].shape), fixed((o_rows, width))],
        out_specs=[seq(wh), seq(wq), fixed((length, 128)), fixed((8, wq)), fixed((width, wq)), fixed((wh, width))],
        out_shape=[
            shape((total, wh), BF16), shape((total, wq), BF16), shape((length, 128), BF16), shape((8, wq), F32),
            shape((width, wq), BF16), shape((wh, width), BF16),
        ],
        scratch_shapes=[
            pltpu.VMEM((length, wh), BF16),
            pltpu.VMEM((length, wh), BF16),
            pltpu.VMEM((length, wh), F32),
        ]
        + [pltpu.VMEM((length, 128), BF16)] * 4
        + [pltpu.VMEM((128, length), F32)] * 4
        + [pltpu.VMEM((length, 128), F32)] * 3
        + [pltpu.VMEM((8, seg_w), F32)],
        cost_estimate=pl.CostEstimate(
            flops=4 * length * width * (wq + wh) + 24 * length * length * wh,
            bytes_accessed=12 * length * width,
            transcendentals=length * length * wh // 64,
        ),
        name="attention",
    )(sc, na, dy, vec, waves_of, seg_rows, cgrad, *weights)


def attn_terms(sc, na, dy, o_all, gqs_all, wqs, vec, sums, ob, ubs, rss):
    total, width = na.shape
    wq = gqs_all.shape[1]
    wh = o_all.shape[1]
    blk = total // 4
    o_rows = width // 4
    n_w = len(ubs)
    sizes = [(message_rows(k, (o_rows, o_rows * 3 // 2, 0)), wq) for k, _ in MOVES]

    def kern(sc_ref, na_r, dy_r, o_r, g_r, w_r, vec_r, s0, ob_r, *refs):
        ub_r, rs_r = refs[:n_w], refs[n_w : 2 * n_w]
        outs, (tbl, acc_q, acc_o, o_f) = refs[2 * n_w : -4], refs[-4:]
        s = sc_ref[0]
        c = jnp.bitwise_and(s, 1)
        y = jnp.right_shift(s, 1)
        i = pl.program_id(0)
        pq = dtn(na_r[...], g_r[...])
        po = dtn(dy_r[...], o_r[...])

        @pl.when(i == 0)
        def _():
            acc_q[...] = pq
            acc_o[...] = po

        @pl.when(i > 0)
        def _():
            acc_q[...] += pq
            acc_o[...] += po

        @pl.when(i == pl.num_programs(0) - 1)
        def _():
            got = acc_o[...].T
            lower, upper = got[:o_rows, :], got[o_rows:, :]
            for i, v in enumerate((jnp.where(y == 0, lower, upper), jnp.where(y == 0, upper, lower))):
                fold(o_f.at[i], 0, o_rows, v, wq)
            for (k, j), out in zip(MOVES, outs):
                b = jnp.bitwise_xor(sc_ref[1], j)
                r0 = jnp.bitwise_xor(s, k) * o_rows
                put_half(out, 0, lambda at, n, r0=r0: acc_q[pl.ds(pl.multiple_of(r0 + at, 8), n), :], o_rows, 32, b)
                if k in (0, 2):
                    put_half(out, o_rows // 2, lambda at, n, k=k: o_f[k // 2, pl.ds(at, n), :], o_rows * 3 // 2, 32, b)
            line = lambda v: jnp.sum(v, axis=0, keepdims=True)
            w = w_r[...].astype(F32)
            both = s0[...]
            fs = line(col_sums(w * line(both)))
            fg = line(col_sums(w * acc_q[...]))
            ss = sum([line(r[8:16, :]) for r in rs_r])
            sg = sum([line(r[0:8, :]) for r in rs_r])
            tbl[...] = jnp.zeros_like(tbl)
            tbl[0:1, :] = (fg - vec_r[1:2, :] * fs) / vec_r[0:1, :]
            tbl[1:2, :] = fs
            tbl[2:3, :] = sg
            tbl[3:4, :] = ss
            tbl[4:5, :] = line(ob_r[...])
            qb8 = jnp.broadcast_to(line(both[:, :wh]), (8, wh))
            tbl[5:6, :] = head_spread(qb8, c, width)[0:1, :]
            tbl[6:7, : wq - wh] = line(both[:, wh:])
            for w_i, ref in enumerate(ub_r):
                put_hidden_bias(tbl, s, w_i, line(ref[...]))

    def fixed(dims):
        return pl.BlockSpec(dims, lambda i: (0, 0))

    row = pl.BlockSpec((blk, width), lambda i: (i, 0))
    return pl.pallas_call(
        kern,
        grid=(4,),
        in_specs=[SMEM, row, row, pl.BlockSpec((blk, wh), lambda i: (i, 0)), pl.BlockSpec((blk, wq), lambda i: (i, 0))]
        + [fixed((width, wq)), fixed((16, width)), fixed((8, wq)), fixed((8, width))]
        + [fixed((8, wq))] * n_w
        + [fixed((16, width))] * n_w,
        out_specs=[fixed(g) for g in sizes] + [fixed((16, width))],
        out_shape=[shape(g, BF16) for g in sizes] + [shape((16, width), F32)],
        scratch_shapes=[
            pltpu.VMEM((width, wq), F32),
            pltpu.VMEM((width, wh), F32),
            pltpu.VMEM((2, o_rows * 3 // 2, wq), F32),
        ],
        cost_estimate=pl.CostEstimate(
            flops=2 * total * width * (wq + wh), bytes_accessed=4 * total * width, transcendentals=0
        ),
        name="attn_terms",
    )(sc, na, dy, o_all, gqs_all, wqs, vec, sums, ob, *ubs, *rss)


def outputs(which, hids, gls, ups, downs, o_all, gqs_all, wo, wqs, vec, last=()):
    total, wid2 = hids[0].shape
    width = wqs.shape[0]
    n_w = len(hids)
    blk = total // 8
    base = 4 * which

    def kern(*refs):
        h_r, g_r, u_r, d_r = (refs[k * n_w : (k + 1) * n_w] for k in range(4))
        o_r, q_r, wo_r, wq_r, vec_r = refs[4 * n_w : 4 * n_w + 5]
        out, hp = refs[-2:]
        br = dnn(o_r[...], wo_r[...])
        ea = dnt(q_r[...], wq_r[...])
        em = None
        for w in range(n_w):
            br = br + dnn(h_r[w][...], d_r[w][...])
            t = dnt(g_r[w][...], u_r[w][...])
            em = t if em is None else em + t
        h = ea * vec_r[0:1, :] + em * vec_r[2:3, :]
        if not last:
            out[...] = br.astype(BF16)
            hp[...] = h.astype(BF16)
        else:
            tok_r, dy_r, oi, hi = refs[4 * n_w + 5 : 4 * n_w + 9]
            x = tok_r[...].astype(F32)
            xhat, rstd = normalize(x)
            out[...] = (x + br + oi[...].astype(F32) + vec_r[4:5, :] + vec_r[5:6, :]).astype(BF16)
            h = h + hi[...].astype(F32)
            mean = jnp.mean(h, axis=-1, keepdims=True)
            cov = jnp.mean(h * xhat, axis=-1, keepdims=True)
            hp[...] = (dy_r[...].astype(F32) + rstd * (h - mean - xhat * cov)).astype(BF16)

    def rows(lanes):
        return pl.BlockSpec((blk, lanes), lambda i: (i + base, 0))

    def fixed(dims):
        return pl.BlockSpec(dims, lambda i: (0, 0))

    res = pl.BlockSpec((blk, width), lambda i: (i, 0))
    return pl.pallas_call(
        kern,
        grid=(4,),
        in_specs=[rows(wid2)] * (2 * n_w)
        + [fixed((width, wid2))] * n_w
        + [fixed((wid2, width))] * n_w
        + [rows(o_all.shape[1]), rows(gqs_all.shape[1]), fixed(wo.shape), fixed(wqs.shape), fixed((16, width))]
        + [res] * len(last),
        out_specs=[res, res],
        out_shape=[shape((total // 2, width), BF16)] * 2,
        cost_estimate=pl.CostEstimate(
            flops=total * width * (2 * n_w * wid2 + 900), bytes_accessed=12 * total * width, transcendentals=0
        ),
        name="outputs",
    )(*hids, *gls, *ups, *downs, o_all, gqs_all, wo, wqs, vec, *last)


def first_sum(sc, msgs, sizes, high, sets):
    first, more, table = [v // 2 for v in sizes]
    lanes = msgs[0].shape[1]
    total = 2 * first + more + table
    half = high // 2
    quarter = high // 4
    planes = total // half

    def kern(sc_ref, *refs):
        ins = dict(zip(MOVES, refs[:8]))
        mine, away, tmp = refs[8:]
        for i in range(sets):

            def add(at, n, keys):
                parts = []
                for m in keys:
                    base = i * (ins[m].shape[0] // sets) + at(m[0])
                    parts.append(ins[m][base : base + n, :].astype(F32))
                while len(parts) > 1:
                    parts = [a + b for a, b in zip(parts[::2], parts[1::2])]
                return parts[0]

            even = [m for m in MOVES if m[0] in (0, 2)]
            odd = [m for m in MOVES if m[0] in (1, 3)]
            tmp[:first, :] = add(lambda k: 0, first, even)
            tmp[first : 2 * first, :] = add(lambda k: 0, first, odd)
            tmp[2 * first : 2 * first + more, :] = add(lambda k: first, more, even)
            if table:
                tmp[2 * first + more :, :] = add(lambda k: first + (more if k in (0, 2) else 0), table, MOVES)
            for out, flip in ((mine, 0), (away, 1)):
                b = jnp.bitwise_xor(sc_ref[2], flip)
                for p in range(planes):
                    at = pl.multiple_of(p * half + b * quarter, 8)
                    out[i * planes + p] = tmp[pl.ds(at, quarter), :].astype(BF16)

    return pl.pallas_call(
        kern,
        in_specs=[SMEM] + [VM] * 8,
        out_specs=[VM, VM],
        out_shape=[shape((planes * sets, quarter, lanes), BF16)] * 2,
        scratch_shapes=[pltpu.VMEM((total, lanes), F32)],
        cost_estimate=pl.CostEstimate(
            flops=8 * sets * total * lanes, bytes_accessed=10 * sets * total * lanes, transcendentals=0
        ),
        name="first_sum",
    )(sc, *msgs)


def piece_row(sc_ref, n, h):
    b0, b1 = jnp.bitwise_xor(sc_ref[1], n & 1), jnp.bitwise_xor(sc_ref[2], n >> 1)
    return pl.multiple_of(b0 * (h // 2) + b1 * (h // 4), 8)


def early_grads(sc, pieces, width, ff, count):
    prow, wid2 = pieces[0].shape[1:]
    wid = wid2 // 2
    chunk = ff // 4
    part = width // 4
    n_p = len(pieces)

    def kern(sc_ref, *refs):
        ins = refs[:n_p]
        up, down, tmp = refs[-3:]
        s = sc_ref[0]
        for w in range(count):
            for n in range(n_p):
                at = piece_row(sc_ref, n, part)
                for p in range(4):
                    for h in range(2):
                        v = ins[n][4 * w + p, :, h * wid : (h + 1) * wid].astype(F32)
                        if p < 2:
                            t = jnp.bitwise_xor(s, p + 2 * h)
                            lanes = pl.multiple_of(t * chunk + w * wid, 256)
                            up[pl.ds(at, prow), pl.ds(lanes, wid)] = v
                        else:
                            tmp[pl.ds((2 * h + p - 2) * part + at, prow), :] = v
            down[w * wid : (w + 1) * wid, :] = tmp[...].T

    return pl.pallas_call(
        kern,
        in_specs=[SMEM] + [VM] * n_p,
        out_specs=[VM, VM],
        out_shape=[shape((part, ff), F32), shape((chunk, width), F32)],
        scratch_shapes=[pltpu.VMEM((width, wid), F32)],
        cost_estimate=pl.CostEstimate(flops=0, bytes_accessed=12 * part * ff, transcendentals=0),
        name="early_grads",
    )(sc, *pieces)


def late_grads(sc, pieces, width, ff, shared_w, prev):
    n_p = len(pieces)
    planes, prow, wid2 = pieces[0].shape
    wid = wid2 // 2
    chunk = ff // 4
    part = width // 4
    half = width // 2
    high = prow * n_p
    wave = WAVES - 1

    def kern(sc_ref, *refs):
        ins = refs[:n_p]
        up, down = refs[n_p + len(prev) : n_p + len(prev) + 2]
        lines = refs[n_p + len(prev) + 2 : -1]
        full = refs[-1]
        s = sc_ref[0]
        i = pl.program_id(0)

        @pl.when(i == 0)
        def _():
            for n in range(n_p):
                at = piece_row(sc_ref, n, high)
                for p in range(planes):
                    full[pl.ds(p * high + at, prow), :] = ins[n][p].astype(F32)
            d = 2 * part
            down[...] = jnp.concatenate([full[d : d + half, :wid], full[d : d + half, wid:]], axis=0).T
            at = d + half
            tab = jnp.concatenate([full[at : at + 16, :], full[at + 16 : at + 32, : width - wid2]], axis=1)
            left = pltpu.roll(tab, (width - s * part) % width, 1)
            for out, k in zip(lines, (0, 1, 2, 3, 4, 5, 4)):
                out[...] = left[k : k + 1, :part].reshape(part)
            few = shared_w // 4
            lines[7][...] = pltpu.roll(tab, (width - s * few) % width, 1)[6:7, :few].reshape(few)
            row = jnp.concatenate(
                [full[pl.ds(at + 8 + s, 1), :], full[pl.ds(at + 24 + s, 1), :][:, : width - wid2]], axis=1
            )
            lines[8][...] = row.reshape(width)

        for k in range(4):

            @pl.when(i == k)
            def _(k=k):
                r0, h = (k & 1) * part, (k >> 1) * wid
                up[...] = full[r0 : r0 + part, h : h + wid]

    line_shapes = [(part,)] * 7 + [(shared_w // 4,), (width,)]
    spec = pltpu.PrefetchScalarGridSpec(
        num_scalar_prefetch=1,
        grid=(4,),
        in_specs=[pl.BlockSpec(p.shape, lambda i, sc: (0, 0, 0)) for p in pieces] + [ANY] * len(prev),
        out_specs=[
            pl.BlockSpec((part, wid), lambda i, sc: (0, jnp.bitwise_xor(sc[0], i) * WAVES + wave)),
            pl.BlockSpec((wid, width), lambda i, sc: (wave, 0)),
        ]
        + [pl.BlockSpec(d, lambda i, sc: (0,)) for d in line_shapes],
        scratch_shapes=[pltpu.VMEM((planes * high, wid2), F32)],
    )
    return pl.pallas_call(
        kern,
        grid_spec=spec,
        out_shape=[shape((part, ff), F32), shape((chunk, width), F32)] + [shape(d, F32) for d in line_shapes],
        input_output_aliases={1 + n_p + i: i for i in range(len(prev))},
        cost_estimate=pl.CostEstimate(flops=0, bytes_accessed=4 * part * ff, transcendentals=0),
        name="late_grads",
    )(sc, *pieces, *prev)


def attn_grads(sc, pieces, width, shared_w):
    n_p = len(pieces)
    planes, prow, wq = pieces[0].shape
    part = width // 4
    wh = wq - shared_w
    high = prow * n_p

    def kern(sc_ref, *refs):
        ins = refs[:n_p]
        gq, gs, go, full = refs[n_p:]
        c = jnp.bitwise_and(sc_ref[0], 1)
        for n in range(n_p):
            at = piece_row(sc_ref, n, high)
            for p in range(planes):
                full[pl.ds(p * high + at, prow), :] = ins[n][p].astype(F32)
        gq[...] = head_spread(full[:part, :wh], c, width) + head_spread(full[part : 2 * part, :wh], 1 - c, width)
        gs[...] = full[:part, wh:] + full[part : 2 * part, wh:]
        go[...] = unfold(full, 2 * part, part, wq)

    return pl.pallas_call(
        kern,
        in_specs=[SMEM] + [VM] * n_p,
        out_specs=[VM] * 3,
        out_shape=[shape((part, width), F32), shape((part, shared_w), F32), shape((part, width), F32)],
        scratch_shapes=[pltpu.VMEM((planes * high, wq), F32)],
        cost_estimate=pl.CostEstimate(flops=0, bytes_accessed=12 * part * width, transcendentals=0),
        name="attn_grads",
    )(sc, *pieces)


def to_shard(value, k):
    return lax.ppermute(value, "shard", [(s, s ^ k) for s in range(4)])


def to_replica(value, k, count):
    return lax.ppermute(value, "replica", [(r, r ^ k) for r in range(count)])


def both_add(a, b):
    return (a.astype(F32) + b.astype(F32)).astype(BF16)


def after(value, *others):
    return lax.optimization_barrier((value,) + others)[0]


def to_group(value, k, j, count):
    pairs = [(r * 4 + s, (r ^ j) * 4 + (s ^ k)) for r in range(count) for s in range(4)]
    return lax.ppermute(value, ("replica", "shard"), pairs)


def send_terms(msgs, count):
    return [v if (k, j) == (0, 0) else to_group(v, k, j, count) for (k, j), v in zip(MOVES, msgs)]


def reduce_chain(quarter, away, count):
    quarter = both_add(quarter, to_replica(away, 2, count))
    k = 4
    while k < count:
        quarter = both_add(quarter, to_replica(quarter, k, count))
        k *= 2
    return [quarter] + [to_replica(quarter, k, count) for k in (1, 2, 3)]


def shards(
    tokens, segment_ids, positions, first_gain, first_shift, query_weight, query_bias, shared_weight,
    shared_bias, output_weight, output_bias, second_gain, second_shift, up_weight, up_bias, down_weight,
    down_bias, result_grad, shared_grad, *, replicas,
):
    width = tokens.shape[1]
    ff = up_weight.shape[1]
    part = width // 4
    sw = shared_weight.shape[1]
    s = lax.axis_index("shard")
    r = lax.axis_index("replica")
    sc = jnp.stack([s, r & 1, (r >> 1) & 1]).astype(jnp.int32)

    small = pack_small(
        sc,
        [first_gain, first_shift, second_gain, second_shift, output_bias, down_bias, query_bias],
        shared_bias, up_bias,
    )
    near = [small] + [to_shard(small, k) for k in (1, 2, 3)]
    own0, k1, k3, m2 = pack_first(after(sc, small), up_weight, down_weight)
    k1 = to_shard(k1, 1)
    m2 = to_shard(m2, 2)
    k3 = to_shard(k3, 3)
    core_out = pack_core(after(sc, own0), up_weight, query_weight, shared_weight)
    core_got = to_shard(core_out, 1)
    tok_in = to_shard(tokens, 1)
    dy_in = to_shard(result_grad, 1)
    ints_in = to_shard(jnp.concatenate([segment_ids, positions], axis=0), 1)

    prev, ob, vec = norm_pair(0, tokens, result_grad, near, [])
    prev, _, _ = norm_pair(1, tok_in, dy_in, near, prev)
    nm, na, dy = prev
    own1, own2, ownq, y1, y2, ya = pack_rest(
        sc, up_weight, down_weight, query_weight, shared_weight, output_weight, after(core_got, vec)
    )

    pos = jnp.concatenate([positions, ints_in[1:]], axis=0)
    inv = 10000.0 ** (-2.0 * jnp.arange(ROT // 2, dtype=F32) / ROT)
    ang = pos.astype(F32)[:, None, :] * inv[None, :, None]
    angles = jnp.concatenate([jnp.cos(ang), jnp.sin(ang)], axis=1)
    segs = jnp.stack([segment_ids, ints_in[:1]])

    rows = part

    def wave(w, pieces, down_at, high, slot=None, prev=(), table=None):
        return mlp_wave(w, sc, nm, dy, pieces, down_at, down_weight, vec, high, slot, prev, table)

    m1 = to_shard(y1, 2)
    hid0, gl0, wu0, wd0, ub0, rs0, *msg0 = wave(0, [(own0, 0), (k1, 0), (m2, 0), (k3, 0)], (m2, rows), part, 0)
    ma = to_shard(after(ya, m1), 2)
    hid1, gl1, wu1, wd1, ub1, rs1, *msg01 = wave(
        1, [(own1, 0), (core_got, 0), (m1, 0), (m1, rows)], (m1, 2 * rows), part, 1, msg0
    )
    m2b = to_shard(after(y2, ma), 2)
    got01 = send_terms([after(v, ma) for v in msg01], replicas)
    o_all, gqs_all, cache, sums, wqs, wo = attention(
        sc, na, dy, (ownq, core_got, ma, output_weight), vec, angles, segs, shared_grad
    )
    *msga, table = attn_terms(
        sc, na, dy, o_all, gqs_all, wqs, vec, sums, ob, (ub0, ub1), (rs0, rs1)
    )
    hid2, gl2, wu2, wd2, _, _, *msg2 = wave(
        2, [(own2, 0), (core_got, 2 * rows), (m2b, 0), (m2b, rows)], (m2b, 2 * rows), 32, table=table
    )

    def chain(got, sizes, high, sets):
        return reduce_chain(*first_sum(sc, got, sizes, high, sets), replicas)

    p01 = chain(got01, (part, width // 2, 0), part, 2)
    pa = chain(send_terms(msga, replicas), (part, part * 3 // 2, 0), 32, 1)
    p2 = chain(send_terms(msg2, replicas), (part, width // 2, 32), 32, 1)

    hids, gls, wus, wds = (hid0, hid1, hid2), (gl0, gl1, gl2), (wu0, wu1, wu2), (wd0, wd1, wd2)

    def outs(which, last=()):
        return outputs(which, hids, gls, wus, wds, o_all, gqs_all, wo, wqs, vec, last)

    out_p, h_p = outs(1)
    out_in = to_shard(out_p, 1)
    h_in = to_shard(h_p, 1)
    block_output, tokens_grad = outs(0, (tokens, result_grad, out_in, h_in))

    grads = early_grads(sc, p01, width, ff, WAVES - 1)
    grad_q, grad_s, grad_o = attn_grads(sc, pa, width, sw)
    out = late_grads(sc, p2, width, ff, sw, grads)
    grad_up, grad_down, fg, fs, sg, ss, ob_g, qb_g, db_g, sb_g, ub_g = out
    return (
        block_output, cache, tokens_grad,
        fg, fs, grad_q, qb_g, grad_s, sb_g, grad_o, ob_g,
        sg, ss, grad_up, ub_g, grad_down, db_g,
    )


def solution(mesh):
    both = P(("replica", "shard"), None)
    one, two = P("shard"), P("shard", None)

    def body(*args):
        return shards(*args, replicas=mesh.shape["replica"])

    return jax.shard_map(
        body,
        mesh=mesh,
        in_specs=(both, both, both, one, one, two, one, two, one, two, one, one, one, two, one, two, one, both, both),
        out_specs=(both, both, both, one, one, two, one, two, one, two, one, one, one, two, one, two, one),
        check_vma=False,
    )
```

```python
import jax
import jax.numpy as jnp
from jax import lax
from jax.experimental import pallas as pl
from jax.experimental.pallas import tpu as pltpu
from jax.sharding import PartitionSpec as P


HEAD_DIM = 64
ROT = 16
FIRST_DOC = 800
EPS = 1e-05
F32 = jnp.float32
BF16 = jnp.bfloat16
WAVES = 3


def dnn(a, b):
    return lax.dot_general(a, b, (((1,), (0,)), ((), ())), preferred_element_type=F32)


def dnt(a, b):
    return lax.dot_general(a, b, (((1,), (1,)), ((), ())), preferred_element_type=F32)


def dtn(a, b):
    return lax.dot_general(a, b, (((0,), (0,)), ((), ())), preferred_element_type=F32)


def sum8(v):
    return jnp.sum(v.reshape(-1, 8, v.shape[1]), axis=0)


def normalize(x):
    centre = x - jnp.mean(x, axis=-1, keepdims=True)
    var = jnp.mean(centre * centre, axis=-1, keepdims=True)
    rstd = lax.rsqrt(var + EPS)
    return centre * rstd, rstd


ANY = pl.BlockSpec(memory_space=pl.ANY)
SMEM = pl.BlockSpec(memory_space=pltpu.SMEM)
VM = pl.BlockSpec(memory_space=pltpu.VMEM)


def shape(dims, kind):
    return jax.ShapeDtypeStruct(dims, kind)


def head_columns(w, c):
    width = w.shape[1]
    part = width // 4
    lane = lax.broadcasted_iota(jnp.int32, (1, width), 1)
    r = pltpu.roll(w, (width - c * part) % width, 1)
    return jnp.where(lane < part, r, pltpu.roll(r, width - part, 1))[:, : 2 * part]


def head_spread(x, c, width):
    part = width // 4
    lane = lax.broadcasted_iota(jnp.int32, (1, width), 1)
    v = jnp.concatenate([x, jnp.zeros_like(x)], axis=1)
    zero = jnp.zeros_like(v)
    u = jnp.where(lane < part, v, zero)
    u = u + pltpu.roll(jnp.where((lane >= part) & (lane < 2 * part), v, zero), part, 1)
    return pltpu.roll(u, c * part, 1)


def up_piece(w_ref, s, k, w, chunk):
    wid = chunk // WAVES
    t = jnp.bitwise_xor(s, k)
    a = pl.multiple_of(t * chunk + w * wid, 256)
    b = pl.multiple_of(jnp.bitwise_xor(t, 2) * chunk + w * wid, 256)
    return jnp.concatenate([w_ref[:, pl.ds(a, wid)], w_ref[:, pl.ds(b, wid)]], axis=1)


def fold(out, at, rows, v, lanes):
    h = rows // 2
    out[at : at + rows, :] = v[:, :lanes]
    out[at + rows : at + rows + h, : lanes // 2] = v[:h, lanes:]
    out[at + rows : at + rows + h, lanes // 2 :] = v[h:, lanes:]


def unfold(ref, at, rows, lanes):
    h = rows // 2
    top = ref[at : at + rows, :]
    low = ref[at + rows : at + rows + h, :]
    return jnp.concatenate(
        [top, jnp.concatenate([low[:, : lanes // 2], low[:, lanes // 2 :]], axis=0)], axis=1
    )


def pack_small(sc, seven, shared_bias, up_bias):
    part = seven[0].shape[0]
    width = up_bias.shape[0]
    few = shared_bias.shape[0]

    def kern(sc_ref, *refs):
        out, tmp = refs[-2:]
        s = sc_ref[0]
        tmp[...] = jnp.zeros_like(tmp)
        for i in range(7):
            tmp[i : i + 1, :part] = refs[i][...].astype(F32).reshape(1, part)
        tmp[:7, :] = pltpu.roll(tmp[0:8, :], s * part, 1)[:7]
        tmp[7:8, :few] = refs[7][...].astype(F32).reshape(1, few)
        tmp[7:8, :] = pltpu.roll(tmp[0:8, :], s * few, 1)[7:8]
        tmp[pl.ds(8 + s, 1), :] = refs[8][...].astype(F32).reshape(1, width)
        out[...] = tmp[...].astype(BF16)

    return pl.pallas_call(
        kern,
        in_specs=[SMEM] + [VM] * 9,
        out_specs=VM,
        out_shape=shape((16, width), BF16),
        scratch_shapes=[pltpu.VMEM((16, width), F32)],
        name="pack_small",
    )(sc, *seven, shared_bias, up_bias)


def pack_first(sc, up_weight, down_weight):
    rows, ff = up_weight.shape
    chunk, width = down_weight.shape
    wid = chunk // WAVES

    def kern(sc_ref, w_ref, d_ref, own, k1, k3, m2):
        s = sc_ref[0]
        own[...] = up_piece(w_ref, s, 0, 0, chunk)
        k1[...] = up_piece(w_ref, s, 1, 0, chunk)
        k3[...] = up_piece(w_ref, s, 3, 0, chunk)
        m2[:rows, :] = up_piece(w_ref, s, 2, 0, chunk)
        fold(m2, rows, wid, d_ref[...], 2 * wid)

    return pl.pallas_call(
        kern,
        grid=(1,),
        in_specs=[SMEM, pl.BlockSpec((rows, ff), lambda i: (0, 0)), pl.BlockSpec((wid, width), lambda i: (0, 0))],
        out_specs=[pl.BlockSpec((rows, 2 * wid), lambda i: (0, 0))] * 3
        + [pl.BlockSpec((rows + wid * 3 // 2, 2 * wid), lambda i: (0, 0))],
        out_shape=[shape((rows, 2 * wid), BF16)] * 3 + [shape((rows + wid * 3 // 2, 2 * wid), BF16)],
        name="pack_first",
    )(sc, up_weight, down_weight)


def pack_core(sc, up_weight, query_weight, shared_weight):
    rows, ff = up_weight.shape
    width = query_weight.shape[1]
    chunk = ff // 4
    wid = chunk // WAVES
    n = 2 * (WAVES - 1)
    half = width // 2

    def kern(sc_ref, w_ref, q_ref, s_ref, out):
        s = sc_ref[0]
        c = jnp.bitwise_and(s, 1)
        for w in range(1, WAVES):
            for i, k in enumerate((1, 3)):
                at = (2 * (w - 1) + i) * rows
                out[at : at + rows, :] = up_piece(w_ref, s, k, w, chunk)
        out[n * rows :, :half] = head_columns(q_ref[...].astype(F32), 1 - c).astype(BF16)
        out[n * rows :, half:] = s_ref[...]

    return pl.pallas_call(
        kern,
        in_specs=[SMEM, VM, VM, VM],
        out_specs=VM,
        out_shape=shape(((n + 1) * rows, 2 * wid), BF16),
        name="pack_core",
        compiler_params=pltpu.CompilerParams(vmem_limit_bytes=12 << 20),
    )(sc, up_weight, query_weight, shared_weight)


def pack_rest(sc, up_weight, down_weight, query_weight, shared_weight, output_weight, got):
    rows, _ = up_weight.shape
    chunk, width = down_weight.shape
    wid = chunk // WAVES
    lanes = 2 * wid
    n = 2 * (WAVES - 1)
    half = width // 2

    def kern(sc_ref, w_ref, d_ref, q_ref, s_ref, o_ref, g_ref, own1, own2, ownq, y1, y2, ya):
        s = sc_ref[0]
        c = jnp.bitwise_and(s, 1)
        for w, own, out in ((1, own1, y1), (2, own2, y2)):
            own[...] = up_piece(w_ref, s, 0, w, chunk)
            out[:rows, :] = up_piece(w_ref, s, 2, w, chunk)
            at = (2 * (w - 1) + 1) * rows
            out[rows : 2 * rows, :] = g_ref[at : at + rows, :]
            fold(out, 2 * rows, wid, d_ref[w * wid : (w + 1) * wid, :], lanes)
        mine = head_columns(q_ref[...].astype(F32), c).astype(BF16)
        for out in (ownq, ya):
            out[:rows, :half] = mine
            out[:rows, half:] = s_ref[...]
        ya[rows : 2 * rows, :] = g_ref[n * rows :, :]
        fold(ya, 2 * rows, rows, o_ref[...], lanes)

    msg = 2 * rows + wid * 3 // 2
    msg_a = 2 * rows + rows * 3 // 2
    return pl.pallas_call(
        kern,
        in_specs=[SMEM] + [VM] * 6,
        out_specs=[VM] * 6,
        out_shape=[shape((rows, lanes), BF16)] * 3
        + [shape((msg, lanes), BF16)] * 2
        + [shape((msg_a, lanes), BF16)],
        name="pack_rest",
        compiler_params=pltpu.CompilerParams(vmem_limit_bytes=20 << 20),
    )(sc, up_weight, down_weight, query_weight, shared_weight, output_weight, got)


def norm_pair(which, tok, dy, near, prev):
    n_tok, width = tok.shape
    n_near = len(near)
    blk = n_tok // 2
    base = 2 * which

    def kern(tok_ref, dy_ref, *refs):
        nm, na, dyc, ob, vec_ref = refs[n_near + len(prev) :]
        vec_ref[...] = sum([r[...].astype(F32) for r in refs[1:n_near]], refs[0][...].astype(F32))
        xhat, _ = normalize(tok_ref[...].astype(F32))
        a = (xhat * vec_ref[0:1, :] + vec_ref[1:2, :]).astype(BF16)
        m = (xhat * vec_ref[2:3, :] + vec_ref[3:4, :]).astype(BF16)
        g = dy_ref[...]
        na[...] = a
        nm[...] = m
        dyc[...] = g

        @pl.when(pl.program_id(0) == 0)
        def _():
            ob[...] = jnp.zeros_like(ob)

        ob[...] += sum8(g.astype(F32))

    row = pl.BlockSpec((blk, width), lambda i: (i + base, 0))
    src = pl.BlockSpec((blk, width), lambda i: (i, 0))
    whole = pl.BlockSpec((8, width), lambda i: (0, 0))
    small = pl.BlockSpec((16, width), lambda i: (0, 0))
    res = pl.pallas_call(
        kern,
        grid=(2,),
        in_specs=[src, src] + [small] * n_near + [ANY] * len(prev),
        out_specs=[row, row, row, whole, small],
        out_shape=[shape((2 * n_tok, width), BF16)] * 3
        + [shape((8, width), F32), shape((16, width), F32)],
        input_output_aliases={2 + n_near + i: i for i in range(len(prev))},
        cost_estimate=pl.CostEstimate(
            flops=20 * n_tok * width, bytes_accessed=16 * n_tok * width, transcendentals=0
        ),
        name="norm_pair",
        compiler_params=pltpu.CompilerParams(vmem_limit_bytes=16 << 20),
    )(tok, dy, *near, *prev)
    return res[:3], res[3], res[4]


MOVES = [(k, j) for k in range(4) for j in range(2)]


def message_rows(k, sizes):
    first, more, table = sizes
    return (first + (more if k in (0, 2) else 0) + table) // 2


def put_half(out, at, src, rows, high, b):
    half = high // 2
    for p in range(rows // high):
        v = src(pl.multiple_of(p * high + b * half, 8), half)
        out[at + p * half : at + (p + 1) * half, :] = v.astype(BF16)


def fold_table(dst, tbl, lanes):
    width = tbl.shape[1]
    dst[:16, :] = tbl[:, :lanes]
    dst[16:, : width - lanes] = tbl[:, lanes:]
    dst[16:, width - lanes :] = jnp.zeros((16, 2 * lanes - width), F32)


def put_hidden_bias(tbl, s, w, u):
    wd = u.shape[1] // 2
    tbl[pl.ds(8 + s, 1), w * wd : (w + 1) * wd] = u[:, :wd]
    tbl[pl.ds(8 + jnp.bitwise_xor(s, 2), 1), w * wd : (w + 1) * wd] = u[:, wd:]


def col_sums(v):
    part = v[:, :128]
    for i in range(128, v.shape[1], 128):
        part = part + v[:, i : i + 128]
    return sum8(part.T)


def mlp_wave(wave, sc, nm, dy, pieces, down_at, down_own, vec, high, slot=None, prev=(), table=None):
    n_tok, width = nm.shape
    blk = n_tok // 4
    rows = width // 4
    chunk = down_own.shape[0]
    wid = chunk // WAVES
    wid2 = 2 * wid
    half = width // 2
    srcs = []
    for arr, _ in list(pieces) + [down_at]:
        if not any(arr is t for t in srcs):
            srcs.append(arr)
    where = [next(i for i, t in enumerate(srcs) if t is arr) for arr, _ in list(pieces) + [down_at]]
    n_src = len(srcs)

    def kern(sc_ref, nm_r, dy_r, d0, vec_r, *refs):
        got, refs = refs[:n_src], refs[n_src:]
        if table is not None:
            t_r, refs = refs[0], refs[1:]
        refs = refs[len(prev) :]
        hid_o, gl_o, w_s, wd_s, ub, rs = refs[:6]
        b_s, acc_u, acc_d, tbl, t_f = refs[-5:]
        outs = refs[6:-5]
        i = pl.program_id(0)
        s = sc_ref[0]

        @pl.when(i == 0)
        def _():
            acc_u[...] = jnp.zeros_like(acc_u)
            acc_d[...] = jnp.zeros_like(acc_d)
            ub[...] = jnp.zeros_like(ub)
            for k in range(4):
                at = pl.multiple_of(jnp.bitwise_xor(s, k) * rows, 16)
                r0 = pieces[k][1]
                w_s[pl.ds(at, rows), :] = got[where[k]][r0 : r0 + rows, :]
            wd_s[:wid, :] = d0[...]
            wd_s[wid:, :] = unfold(got[where[4]], down_at[1], wid, wid2)
            for h, t in enumerate((s, jnp.bitwise_xor(s, 2))):
                line = vec_r[pl.ds(8 + t, 1), :]
                b_s[:, h * wid : (h + 1) * wid] = jnp.broadcast_to(line[:, wave * wid : (wave + 1) * wid], (8, wid))

        up = dnn(nm_r[...], w_s[...]) + b_s[0:1, :]
        cdf = 0.5 * (1.0 + lax.erf(up * 0.7071067811865476))
        hid = (up * cdf).astype(BF16)
        slope = cdf + up * (jnp.exp(-0.5 * up * up) * 0.3989422804014327)
        gu = dnt(dy_r[...], wd_s[...]) * slope
        gl = gu.astype(BF16)
        hid_o[...] = hid
        gl_o[...] = gl
        acc_u[...] += dtn(nm_r[...], gl)
        acc_d[...] += dtn(dy_r[...], hid)
        ub[...] += sum8(gu)

        @pl.when(i == pl.num_programs(0) - 1)
        def _():
            w = w_s[...].astype(F32)
            rs[0:8, :] = col_sums(w * acc_u[...])
            rs[8:16, :] = col_sums(w * jnp.sum(ub[...], axis=0, keepdims=True))
            if table is not None:
                tbl[...] = t_r[...]
                line = lambda v: jnp.sum(v, axis=0, keepdims=True)
                ss = tbl[3:4, :] + line(rs[8:16, :])
                sg = tbl[2:3, :] + line(rs[0:8, :])
                tbl[2:3, :] = (sg - vec_r[3:4, :] * ss) / vec_r[2:3, :]
                tbl[3:4, :] = ss
                put_hidden_bias(tbl, s, wave, line(ub[...]))
                fold_table(t_f, tbl, wid2)
            for (k, j), out in zip(MOVES, outs):
                b = jnp.bitwise_xor(sc_ref[1], j)
                r0 = jnp.bitwise_xor(s, k) * rows
                h = wid if k >= 2 else 0

                def up_rows(at, n, r0=r0, h=h):
                    v = acc_u[pl.ds(pl.multiple_of(r0 + at, 8), n), :]
                    return jnp.concatenate([v[:, h : h + wid], v[:, wid - h : wid2 - h]], axis=1)

                def down_rows(at, n, h=h):
                    low = acc_d[pl.ds(pl.multiple_of(at, 8), n), :]
                    top = acc_d[pl.ds(pl.multiple_of(half + at, 8), n), :]
                    return jnp.concatenate([low[:, h : h + wid], top[:, h : h + wid]], axis=1)

                put_half(out, 0, up_rows, rows, high, b)
                end = rows // 2
                if k in (0, 2):
                    put_half(out, end, down_rows, half, high, b)
                    end += half // 2
                if table is not None:
                    put_half(out, end, lambda at, n: t_f[pl.ds(at, n), :], 32, 32, b)

    row = pl.BlockSpec((blk, width), lambda i: (i, 0))
    mid = pl.BlockSpec((blk, wid2), lambda i: (i, 0))

    def fixed(dims, at=(0, 0)):
        return pl.BlockSpec(dims, lambda i: at)

    extra = [] if table is None else [table]
    sizes = (rows, half, 0 if table is None else 32)
    n_out = [message_rows(k, sizes) for k, _ in MOVES]
    at = 0 if slot is None else slot
    times = 1 if slot is None else 2
    return pl.pallas_call(
        kern,
        grid=(4,),
        in_specs=[SMEM, row, row]
        + [fixed((wid, width), (wave, 0)), fixed((16, width))]
        + [fixed(t.shape) for t in srcs + extra]
        + [ANY] * len(prev),
        out_specs=[mid, mid, fixed((width, wid2)), fixed((wid2, width)), fixed((8, wid2)), fixed((16, width))]
        + [fixed((n, wid2), (at, 0)) for n in n_out],
        out_shape=[shape((n_tok, wid2), BF16)] * 2
        + [shape((width, wid2), BF16), shape((wid2, width), BF16), shape((8, wid2), F32), shape((16, width), F32)]
        + [shape((times * n, wid2), BF16) for n in n_out],
        scratch_shapes=[
            pltpu.VMEM((8, wid2), F32),
            pltpu.VMEM((width, wid2), F32),
            pltpu.VMEM((width, wid2), F32),
            pltpu.VMEM((16, width), F32),
            pltpu.VMEM((32, wid2), F32),
        ],
        input_output_aliases={5 + n_src + len(extra) + i: 6 + i for i in range(len(prev))},
        cost_estimate=pl.CostEstimate(
            flops=8 * n_tok * width * wid2,
            bytes_accessed=10 * n_tok * width,
            transcendentals=2 * n_tok * wid2,
        ),
        name="mlp_wave",
        compiler_params=pltpu.CompilerParams(vmem_limit_bytes=36 << 20),
    )(sc, nm, dy, down_own, vec, *srcs, *extra, *prev)


def attention(sc, na, dy, weights, vec, waves_of, seg_rows, cgrad):
    width = na.shape[1]
    length = cgrad.shape[0]
    rows, wq = weights[0].shape
    o_rows = weights[3].shape[0]
    core_rows = weights[1].shape[0]
    wh = wq - 2 * HEAD_DIM
    pairs = wh // 128
    chunk = 256
    n_chunk = length // chunk
    tail = length - FIRST_DOC
    blocks = []
    at = 0
    while at + chunk <= FIRST_DOC - FIRST_DOC % chunk - chunk:
        blocks.append((at, chunk, 0, at + chunk, False))
        at += chunk
    blocks.append((at, FIRST_DOC - at, 0, FIRST_DOC, False))
    k_last = FIRST_DOC // 128 * 128
    blocks.append((FIRST_DOC, tail, k_last, length - k_last, True))

    def kern(sc_ref, na_r, dy_r, vec_r, cs_r, sr_r, cg_r, *refs):
        q0, cg_in, mg_in, o0 = refs[:4]
        o_s, gqs_s, cache, sums, wqs, wo = refs[4:10]
        q_s, do_s, dq_s, kz, zk, vz, zv, ek, ok, ev, ov, tc_r, ta_r, tb_r, sg_s = refs[10:]
        s = sc_ref[0]
        c = jnp.bitwise_and(s, 1)
        y = jnp.right_shift(s, 1)
        step = pl.program_id(0)

        @pl.when(step == 0)
        def _():
            for k in range(4):
                at = pl.multiple_of(jnp.bitwise_xor(s, k) * rows, 16)
                piece = (q0, cg_in, mg_in, mg_in)[k]
                r0 = (0, 0, 0, rows)[k]
                wqs[pl.ds(at, rows), :] = piece[r0 : r0 + rows, :]
            wo[pl.ds(pl.multiple_of(y * o_rows, 16), o_rows), :] = o0[...]
            wo[pl.ds(pl.multiple_of((1 - y) * o_rows, 16), o_rows), :] = unfold(mg_in, 2 * rows, o_rows, wq)
            sums[...] = jnp.zeros_like(sums)

        ek[...] = jnp.zeros_like(ek)
        ok[...] = jnp.zeros_like(ok)
        ev[...] = jnp.zeros_like(ev)
        ov[...] = jnp.zeros_like(ov)
        lane = lax.broadcasted_iota(jnp.int32, (1, 128), 1)
        low = lane < HEAD_DIM
        qb_line = jnp.broadcast_to(head_columns(vec_r[0:8, :], c)[6:7, :], (8, wh))
        sb_line = jnp.broadcast_to(vec_r[7:8, : 2 * HEAD_DIM], (8, 2 * HEAD_DIM))
        qb_all = jnp.concatenate([qb_line, sb_line], axis=1)[0:1, :]

        def spread(v, lo, hi):
            i = lax.broadcasted_iota(jnp.int32, (8, 128), 0)
            ln = lax.broadcasted_iota(jnp.int32, (8, 128), 1)
            ln = jnp.bitwise_and(ln, HEAD_DIM - 1)
            hit = (jnp.bitwise_and(ln, ROT // 2 - 1) == i) & (ln >= lo) & (ln < hi)
            return lax.dot_general(v, hit.astype(F32), (((0,), (0,)), ((), ())),
                                   precision=lax.Precision.HIGHEST, preferred_element_type=F32)

        still = jnp.bitwise_and(lax.broadcasted_iota(jnp.int32, (1, 128), 1), HEAD_DIM - 1) >= ROT
        cs = cs_r[0]
        tc_r[...] = spread(cs[0:8, :], 0, ROT) + jnp.where(still, 1.0, 0.0)
        ta_r[...] = spread(-cs[8:16, :], 0, ROT // 2)
        tb_r[...] = spread(cs[8:16, :], ROT // 2, ROT)
        sg_s[...] = jnp.broadcast_to(sr_r[0].astype(F32), (8, length))[:, k_last:]
        seg_cols = sg_s[...].T[FIRST_DOC - k_last :, 0:1]

        def turn(v, c, a, b, sign):
            return v * c + sign * (pltpu.roll(v, 120, 1) * a + pltpu.roll(v, 8, 1) * b)

        def tabs(at, keys):
            c = tc_r[pl.ds(at, chunk), :]
            a = ta_r[pl.ds(at, chunk), :]
            b = tb_r[pl.ds(at, chunk), :]
            if keys:
                c = jnp.where(low, c, 1.0)
                a = jnp.where(low, a, 0.0)
                b = jnp.where(low, b, 0.0)
            return c, a, b

        @pl.loop(0, n_chunk)
        def _(n):
            at = pl.multiple_of(n * chunk, chunk)
            sl = pl.ds(at, chunk)
            lin = dnn(na_r[sl, :], wqs[...]) + qb_all
            tq = tabs(at, False)
            for p in range(pairs):
                v = turn(lin[:, p * 128 : (p + 1) * 128], *tq, 1.0)
                q_s[sl, p * 128 : (p + 1) * 128] = v.astype(BF16) * BF16(0.125)
            v = turn(lin[:, wh:], *tabs(at, True), 1.0)
            kv = v.astype(BF16)
            cache[sl, :] = kv
            vr = pltpu.roll(v, 64, 1)
            zero = jnp.zeros_like(v)
            kz[sl, :] = jnp.where(low, v, zero).astype(BF16)
            zv[sl, :] = jnp.where(low, zero, v).astype(BF16)
            zk[sl, :] = jnp.where(low, zero, vr).astype(BF16)
            vz[sl, :] = jnp.where(low, vr, zero).astype(BF16)
            do_s[sl, :] = dnt(dy_r[sl, :], wo[...]).astype(BF16)

        @pl.loop(0, pairs)
        def _(p):
            cols = pl.ds(pl.multiple_of(p * 128, 128), 128)
            for r0, rn, k0, kn, segs in blocks:
                q2 = q_s[r0 : r0 + rn, cols]
                do2 = do_s[r0 : r0 + rn, cols]
                dof = do2.astype(F32)
                keys = [ks[k0 : k0 + kn, :] for ks in (kz, zk)]
                vals = [vs[k0 : k0 + kn, :] for vs in (vz, zv)]
                free = 0 if segs else r0 // 128 * 128
                qi = lax.broadcasted_iota(jnp.int32, (rn, kn - free), 0) + r0
                ki = lax.broadcasted_iota(jnp.int32, (rn, kn - free), 1) + k0 + free
                allowed = ki <= qi
                if segs:
                    allowed = allowed & (seg_cols == sg_s[0:1, :])
                exps, invs = [], []
                for kk in keys:
                    logit = dnt(q2, kk)
                    edge = jnp.where(allowed, logit[:, free:], -1e30)
                    logit = jnp.concatenate([logit[:, :free], edge], axis=1) if free else edge
                    ex = jnp.exp(logit - jnp.max(logit, axis=-1, keepdims=True))
                    exps.append(ex)
                    invs.append(1.0 / jnp.sum(ex, axis=-1, keepdims=True))
                scale = jnp.where(low, invs[0], invs[1])
                dos = (dof * scale).astype(BF16)
                exb = [ex.astype(BF16) for ex in exps]
                o2 = (dnn(exb[0], vals[0]) + dnn(exb[1], vals[1])) * scale
                o_s[r0 : r0 + rn, cols] = o2.astype(BF16)
                prod = o2 * dof
                m0 = jnp.sum(jnp.where(low, prod, 0.0), axis=-1, keepdims=True)
                m1 = jnp.sum(jnp.where(low, 0.0, prod), axis=-1, keepdims=True)
                dsb = []
                for e, mm in enumerate((m0, m1)):
                    dp = dnt(dos, vals[e])
                    dsb.append((exps[e] * (dp - mm * invs[e])).astype(BF16))
                dq_s[r0 : r0 + rn, cols] = dnn(dsb[0], keys[0]) + dnn(dsb[1], keys[1])
                for e, (ak, av) in enumerate(((ek, ev), (ok, ov))):
                    ak[:, k0 : k0 + kn] += dtn(q2, dsb[e])
                    av[:, k0 : k0 + kn] += dtn(dos, exb[e])

        @pl.loop(0, n_chunk)
        def _(n):
            at = pl.multiple_of(n * chunk, chunk)
            sl = pl.ds(at, chunk)
            tq = tabs(at, False)
            for p in range(pairs):
                cc = slice(p * 128, (p + 1) * 128)
                v = turn(dq_s[sl, cc] * 0.125, *tq, -1.0)
                sums[:, cc] += sum8(v)
                gqs_s[sl, cc] = v.astype(BF16)
            v = jnp.concatenate([ek[:64, sl] + ok[64:, sl], ev[:64, sl] + ov[64:, sl]], axis=0).T
            v = v + jnp.where(step == 1, cg_r[sl, :].astype(F32), 0.0)
            v = turn(v, *tabs(at, True), -1.0)
            sums[:, wh:] += sum8(v)
            gqs_s[sl, wh:] = v.astype(BF16)

    def fixed(dims, at=(0, 0)):
        return pl.BlockSpec(dims, lambda i: at, pipeline_mode=pl.Buffered(1))

    def seq(lanes):
        return pl.BlockSpec((length, lanes), lambda i: (1 - i, 0))

    seg_w = length - k_last
    total = na.shape[0]
    return pl.pallas_call(
        kern,
        grid=(2,),
        in_specs=[SMEM, seq(width), seq(width), fixed((16, width))]
        + [pl.BlockSpec((1, 16, length), lambda i: (1 - i, 0, 0)), pl.BlockSpec((1, 1, length), lambda i: (1 - i, 0, 0))]
        + [fixed((length, 128))]
        + [fixed((rows, wq)), fixed((rows, wq), (core_rows // rows - 1, 0)), fixed(weights[2].shape), fixed((o_rows, width))],
        out_specs=[seq(wh), seq(wq), fixed((length, 128)), fixed((8, wq)), fixed((width, wq)), fixed((wh, width))],
        out_shape=[
            shape((total, wh), BF16), shape((total, wq), BF16), shape((length, 128), BF16), shape((8, wq), F32),
            shape((width, wq), BF16), shape((wh, width), BF16),
        ],
        scratch_shapes=[
            pltpu.VMEM((length, wh), BF16),
            pltpu.VMEM((length, wh), BF16),
            pltpu.VMEM((length, wh), F32),
        ]
        + [pltpu.VMEM((length, 128), BF16)] * 4
        + [pltpu.VMEM((128, length), F32)] * 4
        + [pltpu.VMEM((length, 128), F32)] * 3
        + [pltpu.VMEM((8, seg_w), F32)],
        cost_estimate=pl.CostEstimate(
            flops=4 * length * width * (wq + wh) + 24 * length * length * wh,
            bytes_accessed=12 * length * width,
            transcendentals=length * length * wh // 64,
        ),
        name="attention",
        compiler_params=pltpu.CompilerParams(vmem_limit_bytes=40 << 20),
    )(sc, na, dy, vec, waves_of, seg_rows, cgrad, *weights)


def attn_terms(sc, na, dy, o_all, gqs_all, wqs, vec, sums, ob, ubs, rss):
    total, width = na.shape
    wq = gqs_all.shape[1]
    wh = o_all.shape[1]
    blk = total // 4
    o_rows = width // 4
    n_w = len(ubs)
    sizes = [(message_rows(k, (o_rows, o_rows * 3 // 2, 0)), wq) for k, _ in MOVES]

    def kern(sc_ref, na_r, dy_r, o_r, g_r, w_r, vec_r, s0, ob_r, *refs):
        ub_r, rs_r = refs[:n_w], refs[n_w : 2 * n_w]
        outs, (tbl, acc_q, acc_o, o_f) = refs[2 * n_w : -4], refs[-4:]
        s = sc_ref[0]
        c = jnp.bitwise_and(s, 1)
        y = jnp.right_shift(s, 1)
        i = pl.program_id(0)
        pq = dtn(na_r[...], g_r[...])
        po = dtn(dy_r[...], o_r[...])

        @pl.when(i == 0)
        def _():
            acc_q[...] = pq
            acc_o[...] = po

        @pl.when(i > 0)
        def _():
            acc_q[...] += pq
            acc_o[...] += po

        @pl.when(i == pl.num_programs(0) - 1)
        def _():
            got = acc_o[...].T
            lower, upper = got[:o_rows, :], got[o_rows:, :]
            for i, v in enumerate((jnp.where(y == 0, lower, upper), jnp.where(y == 0, upper, lower))):
                fold(o_f.at[i], 0, o_rows, v, wq)
            for (k, j), out in zip(MOVES, outs):
                b = jnp.bitwise_xor(sc_ref[1], j)
                r0 = jnp.bitwise_xor(s, k) * o_rows
                put_half(out, 0, lambda at, n, r0=r0: acc_q[pl.ds(pl.multiple_of(r0 + at, 8), n), :], o_rows, 32, b)
                if k in (0, 2):
                    put_half(out, o_rows // 2, lambda at, n, k=k: o_f[k // 2, pl.ds(at, n), :], o_rows * 3 // 2, 32, b)
            line = lambda v: jnp.sum(v, axis=0, keepdims=True)
            w = w_r[...].astype(F32)
            both = s0[...]
            fs = line(col_sums(w * line(both)))
            fg = line(col_sums(w * acc_q[...]))
            ss = sum([line(r[8:16, :]) for r in rs_r])
            sg = sum([line(r[0:8, :]) for r in rs_r])
            tbl[...] = jnp.zeros_like(tbl)
            tbl[0:1, :] = (fg - vec_r[1:2, :] * fs) / vec_r[0:1, :]
            tbl[1:2, :] = fs
            tbl[2:3, :] = sg
            tbl[3:4, :] = ss
            tbl[4:5, :] = line(ob_r[...])
            qb8 = jnp.broadcast_to(line(both[:, :wh]), (8, wh))
            tbl[5:6, :] = head_spread(qb8, c, width)[0:1, :]
            tbl[6:7, : wq - wh] = line(both[:, wh:])
            for w_i, ref in enumerate(ub_r):
                put_hidden_bias(tbl, s, w_i, line(ref[...]))

    def fixed(dims):
        return pl.BlockSpec(dims, lambda i: (0, 0))

    row = pl.BlockSpec((blk, width), lambda i: (i, 0))
    return pl.pallas_call(
        kern,
        grid=(4,),
        in_specs=[SMEM, row, row, pl.BlockSpec((blk, wh), lambda i: (i, 0)), pl.BlockSpec((blk, wq), lambda i: (i, 0))]
        + [fixed((width, wq)), fixed((16, width)), fixed((8, wq)), fixed((8, width))]
        + [fixed((8, wq))] * n_w
        + [fixed((16, width))] * n_w,
        out_specs=[fixed(g) for g in sizes] + [fixed((16, width))],
        out_shape=[shape(g, BF16) for g in sizes] + [shape((16, width), F32)],
        scratch_shapes=[
            pltpu.VMEM((width, wq), F32),
            pltpu.VMEM((width, wh), F32),
            pltpu.VMEM((2, o_rows * 3 // 2, wq), F32),
        ],
        cost_estimate=pl.CostEstimate(
            flops=2 * total * width * (wq + wh), bytes_accessed=4 * total * width, transcendentals=0
        ),
        name="attn_terms",
        compiler_params=pltpu.CompilerParams(vmem_limit_bytes=28 << 20),
    )(sc, na, dy, o_all, gqs_all, wqs, vec, sums, ob, *ubs, *rss)


def outputs(which, hids, gls, ups, downs, o_all, gqs_all, wo, wqs, vec, last=()):
    total, wid2 = hids[0].shape
    width = wqs.shape[0]
    n_w = len(hids)
    blk = total // 8
    base = 4 * which

    def kern(*refs):
        h_r, g_r, u_r, d_r = (refs[k * n_w : (k + 1) * n_w] for k in range(4))
        o_r, q_r, wo_r, wq_r, vec_r = refs[4 * n_w : 4 * n_w + 5]
        out, hp = refs[-2:]
        br = dnn(o_r[...], wo_r[...])
        ea = dnt(q_r[...], wq_r[...])
        em = None
        for w in range(n_w):
            br = br + dnn(h_r[w][...], d_r[w][...])
            t = dnt(g_r[w][...], u_r[w][...])
            em = t if em is None else em + t
        h = ea * vec_r[0:1, :] + em * vec_r[2:3, :]
        if not last:
            out[...] = br.astype(BF16)
            hp[...] = h.astype(BF16)
        else:
            tok_r, dy_r, oi, hi = refs[4 * n_w + 5 : 4 * n_w + 9]
            x = tok_r[...].astype(F32)
            xhat, rstd = normalize(x)
            out[...] = (x + br + oi[...].astype(F32) + vec_r[4:5, :] + vec_r[5:6, :]).astype(BF16)
            h = h + hi[...].astype(F32)
            mean = jnp.mean(h, axis=-1, keepdims=True)
            cov = jnp.mean(h * xhat, axis=-1, keepdims=True)
            hp[...] = (dy_r[...].astype(F32) + rstd * (h - mean - xhat * cov)).astype(BF16)

    def rows(lanes):
        return pl.BlockSpec((blk, lanes), lambda i: (i + base, 0))

    def fixed(dims):
        return pl.BlockSpec(dims, lambda i: (0, 0))

    res = pl.BlockSpec((blk, width), lambda i: (i, 0))
    return pl.pallas_call(
        kern,
        grid=(4,),
        in_specs=[rows(wid2)] * (2 * n_w)
        + [fixed((width, wid2))] * n_w
        + [fixed((wid2, width))] * n_w
        + [rows(o_all.shape[1]), rows(gqs_all.shape[1]), fixed(wo.shape), fixed(wqs.shape), fixed((16, width))]
        + [res] * len(last),
        out_specs=[res, res],
        out_shape=[shape((total // 2, width), BF16)] * 2,
        cost_estimate=pl.CostEstimate(
            flops=total * width * (2 * n_w * wid2 + 900), bytes_accessed=12 * total * width, transcendentals=0
        ),
        name="outputs",
    )(*hids, *gls, *ups, *downs, o_all, gqs_all, wo, wqs, vec, *last)


def first_sum(sc, msgs, sizes, high, sets):
    first, more, table = [v // 2 for v in sizes]
    lanes = msgs[0].shape[1]
    total = 2 * first + more + table
    half = high // 2
    quarter = high // 4
    planes = total // half

    def kern(sc_ref, *refs):
        ins = dict(zip(MOVES, refs[:8]))
        mine, away, tmp = refs[8:]
        for i in range(sets):

            def add(at, n, keys):
                parts = []
                for m in keys:
                    base = i * (ins[m].shape[0] // sets) + at(m[0])
                    parts.append(ins[m][base : base + n, :].astype(F32))
                while len(parts) > 1:
                    parts = [a + b for a, b in zip(parts[::2], parts[1::2])]
                return parts[0]

            even = [m for m in MOVES if m[0] in (0, 2)]
            odd = [m for m in MOVES if m[0] in (1, 3)]
            tmp[:first, :] = add(lambda k: 0, first, even)
            tmp[first : 2 * first, :] = add(lambda k: 0, first, odd)
            tmp[2 * first : 2 * first + more, :] = add(lambda k: first, more, even)
            if table:
                tmp[2 * first + more :, :] = add(lambda k: first + (more if k in (0, 2) else 0), table, MOVES)
            for out, flip in ((mine, 0), (away, 1)):
                b = jnp.bitwise_xor(sc_ref[2], flip)
                for p in range(planes):
                    at = pl.multiple_of(p * half + b * quarter, 8)
                    out[i * planes + p] = tmp[pl.ds(at, quarter), :].astype(BF16)

    return pl.pallas_call(
        kern,
        in_specs=[SMEM] + [VM] * 8,
        out_specs=[VM, VM],
        out_shape=[shape((planes * sets, quarter, lanes), BF16)] * 2,
        scratch_shapes=[pltpu.VMEM((total, lanes), F32)],
        cost_estimate=pl.CostEstimate(
            flops=8 * sets * total * lanes, bytes_accessed=10 * sets * total * lanes, transcendentals=0
        ),
        name="first_sum",
        compiler_params=pltpu.CompilerParams(vmem_limit_bytes=14 << 20),
    )(sc, *msgs)


def piece_row(sc_ref, n, h):
    b0, b1 = jnp.bitwise_xor(sc_ref[1], n & 1), jnp.bitwise_xor(sc_ref[2], n >> 1)
    return pl.multiple_of(b0 * (h // 2) + b1 * (h // 4), 8)


def early_grads(sc, pieces, width, ff, count):
    prow, wid2 = pieces[0].shape[1:]
    wid = wid2 // 2
    chunk = ff // 4
    part = width // 4
    n_p = len(pieces)

    def kern(sc_ref, *refs):
        ins = refs[:n_p]
        up, down, tmp = refs[-3:]
        s = sc_ref[0]
        for w in range(count):
            for n in range(n_p):
                at = piece_row(sc_ref, n, part)
                for p in range(4):
                    for h in range(2):
                        v = ins[n][4 * w + p, :, h * wid : (h + 1) * wid].astype(F32)
                        if p < 2:
                            t = jnp.bitwise_xor(s, p + 2 * h)
                            lanes = pl.multiple_of(t * chunk + w * wid, 256)
                            up[pl.ds(at, prow), pl.ds(lanes, wid)] = v
                        else:
                            tmp[pl.ds((2 * h + p - 2) * part + at, prow), :] = v
            down[w * wid : (w + 1) * wid, :] = tmp[...].T

    return pl.pallas_call(
        kern,
        in_specs=[SMEM] + [VM] * n_p,
        out_specs=[VM, VM],
        out_shape=[shape((part, ff), F32), shape((chunk, width), F32)],
        scratch_shapes=[pltpu.VMEM((width, wid), F32)],
        cost_estimate=pl.CostEstimate(flops=0, bytes_accessed=12 * part * ff, transcendentals=0),
        name="early_grads",
        compiler_params=pltpu.CompilerParams(vmem_limit_bytes=18 << 20),
    )(sc, *pieces)


def late_grads(sc, pieces, width, ff, shared_w, prev):
    n_p = len(pieces)
    planes, prow, wid2 = pieces[0].shape
    wid = wid2 // 2
    chunk = ff // 4
    part = width // 4
    half = width // 2
    high = prow * n_p
    wave = WAVES - 1

    def kern(sc_ref, *refs):
        ins = refs[:n_p]
        up, down = refs[n_p + len(prev) : n_p + len(prev) + 2]
        lines = refs[n_p + len(prev) + 2 : -1]
        full = refs[-1]
        s = sc_ref[0]
        i = pl.program_id(0)

        @pl.when(i == 0)
        def _():
            for n in range(n_p):
                at = piece_row(sc_ref, n, high)
                for p in range(planes):
                    full[pl.ds(p * high + at, prow), :] = ins[n][p].astype(F32)
            d = 2 * part
            down[...] = jnp.concatenate([full[d : d + half, :wid], full[d : d + half, wid:]], axis=0).T
            at = d + half
            tab = jnp.concatenate([full[at : at + 16, :], full[at + 16 : at + 32, : width - wid2]], axis=1)
            left = pltpu.roll(tab, (width - s * part) % width, 1)
            for out, k in zip(lines, (0, 1, 2, 3, 4, 5, 4)):
                out[...] = left[k : k + 1, :part].reshape(part)
            few = shared_w // 4
            lines[7][...] = pltpu.roll(tab, (width - s * few) % width, 1)[6:7, :few].reshape(few)
            row = jnp.concatenate(
                [full[pl.ds(at + 8 + s, 1), :], full[pl.ds(at + 24 + s, 1), :][:, : width - wid2]], axis=1
            )
            lines[8][...] = row.reshape(width)

        for k in range(4):

            @pl.when(i == k)
            def _(k=k):
                r0, h = (k & 1) * part, (k >> 1) * wid
                up[...] = full[r0 : r0 + part, h : h + wid]

    line_shapes = [(part,)] * 7 + [(shared_w // 4,), (width,)]
    spec = pltpu.PrefetchScalarGridSpec(
        num_scalar_prefetch=1,
        grid=(4,),
        in_specs=[pl.BlockSpec(p.shape, lambda i, sc: (0, 0, 0)) for p in pieces] + [ANY] * len(prev),
        out_specs=[
            pl.BlockSpec((part, wid), lambda i, sc: (0, jnp.bitwise_xor(sc[0], i) * WAVES + wave)),
            pl.BlockSpec((wid, width), lambda i, sc: (wave, 0)),
        ]
        + [pl.BlockSpec(d, lambda i, sc: (0,)) for d in line_shapes],
        scratch_shapes=[pltpu.VMEM((planes * high, wid2), F32)],
    )
    return pl.pallas_call(
        kern,
        grid_spec=spec,
        out_shape=[shape((part, ff), F32), shape((chunk, width), F32)] + [shape(d, F32) for d in line_shapes],
        input_output_aliases={1 + n_p + i: i for i in range(len(prev))},
        cost_estimate=pl.CostEstimate(flops=0, bytes_accessed=4 * part * ff, transcendentals=0),
        name="late_grads",
        compiler_params=pltpu.CompilerParams(vmem_limit_bytes=10 << 20),
    )(sc, *pieces, *prev)


def attn_grads(sc, pieces, width, shared_w):
    n_p = len(pieces)
    planes, prow, wq = pieces[0].shape
    part = width // 4
    wh = wq - shared_w
    high = prow * n_p

    def kern(sc_ref, *refs):
        ins = refs[:n_p]
        gq, gs, go, full = refs[n_p:]
        c = jnp.bitwise_and(sc_ref[0], 1)
        for n in range(n_p):
            at = piece_row(sc_ref, n, high)
            for p in range(planes):
                full[pl.ds(p * high + at, prow), :] = ins[n][p].astype(F32)
        gq[...] = head_spread(full[:part, :wh], c, width) + head_spread(full[part : 2 * part, :wh], 1 - c, width)
        gs[...] = full[:part, wh:] + full[part : 2 * part, wh:]
        go[...] = unfold(full, 2 * part, part, wq)

    return pl.pallas_call(
        kern,
        in_specs=[SMEM] + [VM] * n_p,
        out_specs=[VM] * 3,
        out_shape=[shape((part, width), F32), shape((part, shared_w), F32), shape((part, width), F32)],
        scratch_shapes=[pltpu.VMEM((planes * high, wq), F32)],
        cost_estimate=pl.CostEstimate(flops=0, bytes_accessed=12 * part * width, transcendentals=0),
        name="attn_grads",
        compiler_params=pltpu.CompilerParams(vmem_limit_bytes=10 << 20),
    )(sc, *pieces)


def to_shard(value, k):
    return lax.ppermute(value, "shard", [(s, s ^ k) for s in range(4)])


def to_replica(value, k, count):
    return lax.ppermute(value, "replica", [(r, r ^ k) for r in range(count)])


def both_add(a, b):
    return (a.astype(F32) + b.astype(F32)).astype(BF16)


def after(value, *others):
    return lax.optimization_barrier((value,) + others)[0]


def to_group(value, k, j, count):
    pairs = [(r * 4 + s, (r ^ j) * 4 + (s ^ k)) for r in range(count) for s in range(4)]
    return lax.ppermute(value, ("replica", "shard"), pairs)


def send_terms(msgs, count):
    return [v if (k, j) == (0, 0) else to_group(v, k, j, count) for (k, j), v in zip(MOVES, msgs)]


def reduce_chain(quarter, away, count):
    quarter = both_add(quarter, to_replica(away, 2, count))
    k = 4
    while k < count:
        quarter = both_add(quarter, to_replica(quarter, k, count))
        k *= 2
    return [quarter] + [to_replica(quarter, k, count) for k in (1, 2, 3)]


def shards(
    tokens, segment_ids, positions, first_gain, first_shift, query_weight, query_bias, shared_weight,
    shared_bias, output_weight, output_bias, second_gain, second_shift, up_weight, up_bias, down_weight,
    down_bias, result_grad, shared_grad, *, replicas,
):
    width = tokens.shape[1]
    ff = up_weight.shape[1]
    part = width // 4
    sw = shared_weight.shape[1]
    s = lax.axis_index("shard")
    r = lax.axis_index("replica")
    sc = jnp.stack([s, r & 1, (r >> 1) & 1]).astype(jnp.int32)

    small = pack_small(
        sc,
        [first_gain, first_shift, second_gain, second_shift, output_bias, down_bias, query_bias],
        shared_bias, up_bias,
    )
    near = [small] + [to_shard(small, k) for k in (1, 2, 3)]
    own0, k1, k3, m2 = pack_first(after(sc, small), up_weight, down_weight)
    k1 = to_shard(k1, 1)
    m2 = to_shard(m2, 2)
    k3 = to_shard(k3, 3)
    core_out = pack_core(after(sc, own0), up_weight, query_weight, shared_weight)
    core_got = to_shard(core_out, 1)
    tok_in = to_shard(tokens, 1)
    dy_in = to_shard(result_grad, 1)
    ints_in = to_shard(jnp.concatenate([segment_ids, positions], axis=0), 1)

    prev, ob, vec = norm_pair(0, tokens, result_grad, near, [])
    prev, _, _ = norm_pair(1, tok_in, dy_in, near, prev)
    nm, na, dy = prev
    own1, own2, ownq, y1, y2, ya = pack_rest(
        sc, up_weight, down_weight, query_weight, shared_weight, output_weight, after(core_got, vec)
    )

    pos = jnp.concatenate([positions, ints_in[1:]], axis=0)
    inv = 10000.0 ** (-2.0 * jnp.arange(ROT // 2, dtype=F32) / ROT)
    ang = pos.astype(F32)[:, None, :] * inv[None, :, None]
    angles = jnp.concatenate([jnp.cos(ang), jnp.sin(ang)], axis=1)
    segs = jnp.stack([segment_ids, ints_in[:1]])

    rows = part

    def wave(w, pieces, down_at, high, slot=None, prev=(), table=None):
        return mlp_wave(w, sc, nm, dy, pieces, down_at, down_weight, vec, high, slot, prev, table)

    m1 = to_shard(y1, 2)
    hid0, gl0, wu0, wd0, ub0, rs0, *msg0 = wave(0, [(own0, 0), (k1, 0), (m2, 0), (k3, 0)], (m2, rows), part, 0)
    ma = to_shard(after(ya, m1), 2)
    hid1, gl1, wu1, wd1, ub1, rs1, *msg01 = wave(
        1, [(own1, 0), (core_got, 0), (m1, 0), (m1, rows)], (m1, 2 * rows), part, 1, msg0
    )
    m2b = to_shard(after(y2, ma), 2)
    got01 = send_terms([after(v, ma) for v in msg01], replicas)
    o_all, gqs_all, cache, sums, wqs, wo = attention(
        sc, na, dy, (ownq, core_got, ma, output_weight), vec, angles, segs, shared_grad
    )
    *msga, table = attn_terms(
        sc, na, dy, o_all, gqs_all, wqs, vec, sums, ob, (ub0, ub1), (rs0, rs1)
    )
    hid2, gl2, wu2, wd2, _, _, *msg2 = wave(
        2, [(own2, 0), (core_got, 2 * rows), (m2b, 0), (m2b, rows)], (m2b, 2 * rows), 32, table=table
    )

    def chain(got, sizes, high, sets):
        return reduce_chain(*first_sum(sc, got, sizes, high, sets), replicas)

    p01 = chain(got01, (part, width // 2, 0), part, 2)
    pa = chain(send_terms(msga, replicas), (part, part * 3 // 2, 0), 32, 1)
    p2 = chain(send_terms(msg2, replicas), (part, width // 2, 32), 32, 1)

    hids, gls, wus, wds = (hid0, hid1, hid2), (gl0, gl1, gl2), (wu0, wu1, wu2), (wd0, wd1, wd2)

    def outs(which, last=()):
        return outputs(which, hids, gls, wus, wds, o_all, gqs_all, wo, wqs, vec, last)

    out_p, h_p = outs(1)
    out_in = to_shard(out_p, 1)
    h_in = to_shard(h_p, 1)
    block_output, tokens_grad = outs(0, (tokens, result_grad, out_in, h_in))

    grads = early_grads(sc, p01, width, ff, WAVES - 1)
    grad_q, grad_s, grad_o = attn_grads(sc, pa, width, sw)
    out = late_grads(sc, p2, width, ff, sw, grads)
    grad_up, grad_down, fg, fs, sg, ss, ob_g, qb_g, db_g, sb_g, ub_g = out
    return (
        block_output, cache, tokens_grad,
        fg, fs, grad_q, qb_g, grad_s, sb_g, grad_o, ob_g,
        sg, ss, grad_up, ub_g, grad_down, db_g,
    )


def solution(mesh):
    both = P(("replica", "shard"), None)
    one, two = P("shard"), P("shard", None)

    def body(*args):
        return shards(*args, replicas=mesh.shape["replica"])

    return jax.shard_map(
        body,
        mesh=mesh,
        in_specs=(both, both, both, one, one, two, one, two, one, two, one, one, one, two, one, two, one, both, both),
        out_specs=(both, both, both, one, one, two, one, two, one, two, one, one, one, two, one, two, one),
        check_vma=False,
    )
```
